32 devices in a mesh: row: 8 (over y, x, core), col: 4 (over z).
Axes of the slice: x: 2, y: 2, z: 4, core: 2. Of those that a mesh axis runs over, the one named last changes fastest.
Arguments:
- a_blocks: bfloat16 [1024, 16, 128, 128], P(('row', 'col')), may hold values from -0.0625 to 0.0625
- omega: bfloat16 [16384, 256], P('col'), may hold values from -6 to 6
- route_dest: int32 [1024, 1], P(('row', 'col')), may hold values from 0 to 7; in each aligned block of 32 rows (0 to 31, 32 to 63, ...) at most 4 rows name the same one
- row_target: int32 [1024], P(('row', 'col')), may hold values from 0 to 31
- col_target: int32 [1024, 16], P(('row', 'col')), may hold values from 0 to 31
Outputs:
- basis: float32 [32768, 256], P(('row', 'col'))
- factor: float32 [256, 256], replicated
The draws below stay inside these ranges and needn't reach their ends.
Inputs may be any that keep to these rules, and one draw needn't show every extreme that they name: `route_dest`: among the 32 rows of one device no value appears more than 4 times, and in some device's rows one value appears exactly 4 times.
All inputs are finite; a program needn't handle non-finite values.
Results may differ from the reference program's by a relative error of at most 0.003.
Values may be sent and summed in bfloat16 or wider, within the bound.
A program may use at most 192 MiB of HBM per device.

```python
import math
import jax
import jax.numpy as jnp
import numpy as np
from jax import lax

BS = 128
SKETCH = 256
RB_DEV = 8
NT = 32
GRP = 16
CB_DEV = 32
CAP = 4
TARGETS = 1024
OMEGA_ROWS = 16384
N_ROW = 8
N_COL = 4


def place_ends(result, own_key, least, top_value):
    extent = result.shape
    index_at = [jax.random.randint(jax.random.fold_in(own_key, axis), (), 0, extent[axis]) for axis in range(len(extent))]
    result = result.at[tuple(index_at)].set(least)
    longest = extent.index(max(extent))
    index_at[longest] = (index_at[longest] + 1) % extent[longest]
    return result.at[tuple(index_at)].set(top_value)


def block_levels(key, extent, cuts, smallest, high):
    level = 1.0
    for dim, blocks in cuts:
        heights = jax.random.uniform(jax.random.fold_in(jax.random.fold_in(key, 6), dim), (blocks,), jnp.float32, smallest / len(cuts), high / len(cuts))
        level = level * jnp.repeat(jnp.exp(heights), extent[dim] // blocks).reshape((-1,) + (1,) * (len(extent) - 1 - dim))
    return level


def assign_block(stream_key, own, number, rows, count, top, limit, skew):
    ranking = jax.random.permutation(stream_key, count)
    crowded, usual = load_shares(count, rows * top, limit, skew, True), load_shares(count, rows * top, limit, skew, False)
    places = jnp.arange(count)

    def named(sizes, rotation):
        used = int((sizes > 0).sum())
        fixed = max(1, used // 4)
        passed = fixed + (places - fixed + rotation * (used - fixed)) % max(1, count - fixed)
        return jnp.zeros((count,), jnp.int32).at[ranking[jnp.where(places < fixed, places, passed)]].set(jnp.asarray(sizes, jnp.int32))

    sizes = jnp.where(number % 4 == 0, named(crowded, number // 4), named(usual, number - number // 4 - 1))
    mixed = jax.random.permutation(jax.random.fold_in(own, 3), count)
    donor, receiver = mixed[0:count // 2 * 2:2], mixed[1:count // 2 * 2:2]
    margin = jnp.minimum(sizes[donor] - 1, limit - sizes[receiver]) // 2
    margin = jnp.where((donor == ranking[0]) | (receiver == ranking[0]) | (sizes[receiver] == 0), 0, jnp.maximum(margin, 0))
    passed = jax.random.randint(jax.random.fold_in(own, 4), (count // 2,), 0, 1 << 20) % (margin + 1)
    sizes = sizes.at[donor].add(-passed).at[receiver].add(passed)
    items = jnp.searchsorted(jnp.cumsum(sizes), jnp.arange(rows * top), side="right").astype(jnp.int32)
    grid = items.reshape(top, rows).T
    grid = grid[jax.random.permutation(jax.random.fold_in(own, 1), rows)]
    rotation = jax.random.randint(jax.random.fold_in(own, 2), (rows, 1), 0, top)
    return jnp.take_along_axis(grid, (jnp.arange(top)[None, :] + rotation) % top, axis=1)


def load_shares(number_of, total, most, slope, full):
    loads = [(1 << 20) // math.isqrt(rank ** slope) + 1 for rank in range(1, number_of + 1)]
    largest = most if full else min(most, max(-(-total // number_of), total * loads[0] // sum(loads)))
    least = 1 if total - largest >= number_of - 1 else 0
    given, surplus = [largest] + [least] * (number_of - 1), total - largest - least * (number_of - 1)
    while surplus > 0:
        movable = [i for i in range(1, number_of) if given[i] < largest] or [i for i in range(1, number_of) if given[i] < most]
        mass, remaining = sum([loads[i] for i in movable]), surplus
        for i in movable:
            extra = min(most - given[i], max(1, remaining * loads[i] // mass), surplus)
            given[i] = given[i] + extra
            surplus = surplus - extra
    return np.array(given)


def bell_draw(own_key, extent, width, limit, pieces=(), held_as=jnp.bfloat16):
    gain = block_levels(own_key, extent, pieces, -0.22, 0.18) if pieces else 1.0
    result = jax.random.normal(own_key, extent, jnp.float32) * width * gain
    return jnp.minimum(jnp.maximum(result, -limit), limit).astype(held_as)


def setup_inputs(seed: int = 0) -> dict:
    seeds = jax.random.split(jax.random.key(seed), 6)
    a_blocks = bell_draw(seeds[0], (TARGETS, GRP, BS, BS), (BS * GRP * NT // RB_DEV) ** -0.5, 0.0625, ((0, 32),))
    omega = bell_draw(seeds[1], (OMEGA_ROWS, SKETCH), 1.0, 6.0, ((0, 4),))
    route_dest_keys = jax.random.split(jax.random.fold_in(seeds[2], 1), TARGETS // NT)
    route_dest_turns = jax.random.permutation(jax.random.fold_in(seeds[2], 3), TARGETS // NT)
    route_dest = jax.vmap(lambda own, number: assign_block(jax.random.fold_in(seeds[2], 2), own, number, NT, N_ROW, 1, CAP, 1))(route_dest_keys, route_dest_turns).reshape((TARGETS, 1))
    row_target = place_ends(jax.random.randint(seeds[3], (TARGETS,), 0, RB_DEV * N_COL), jax.random.fold_in(seeds[3], 1), 0, (RB_DEV * N_COL) - 1).astype(jnp.int32)
    col_target = place_ends(jax.random.randint(seeds[4], (TARGETS, GRP), 0, CB_DEV), jax.random.fold_in(seeds[4], 1), 0, CB_DEV - 1).astype(jnp.int32)
    return dict(a_blocks=a_blocks, omega=omega, route_dest=route_dest, row_target=row_target, col_target=col_target)


def reference(a_blocks, omega, route_dest, row_target, col_target):
    devices = N_ROW * N_COL
    group_blocks = RB_DEV * N_COL
    slabs = omega.reshape(N_COL, CB_DEV, BS, SKETCH)
    blocks = a_blocks.reshape(devices, NT, GRP, BS, BS)
    targets = (route_dest[:, 0] * group_blocks + row_target).astype(jnp.int32).reshape(devices, NT)
    columns = col_target.astype(jnp.int32).reshape(devices, NT, GRP)

    def add_device(carry, inputs):
        dev_blocks, dev_targets, dev_columns, device = inputs
        slab = lax.dynamic_index_in_dim(slabs, device % N_COL, 0, keepdims=False)
        picked = slab[dev_columns].astype(jnp.float32)
        partial_value = jnp.einsum('tgij,tgjk->tik', dev_blocks.astype(jnp.float32), picked, precision=lax.Precision.HIGHEST)
        rounded = lax.optimization_barrier(partial_value.astype(jnp.bfloat16))
        return (carry.at[dev_targets].add(rounded.astype(jnp.float32)), None)
    start = jnp.zeros((RB_DEV * devices, BS, SKETCH), jnp.float32)
    device_ids = jnp.arange(devices, dtype=jnp.int32)
    summed, _ = lax.scan(add_device, start, (blocks, targets, columns, device_ids))
    sketch = summed.reshape(RB_DEV * devices * BS, SKETCH)
    q_factor, r_factor = jnp.linalg.qr(sketch)
    signs = jnp.sign(jnp.diagonal(r_factor))
    q_factor = q_factor * signs[None, :]
    r_factor = r_factor * signs[:, None]
    total = float(RB_DEV * devices * BS)
    basis = (q_factor * jnp.sqrt(total)).astype(jnp.float32)
    factor = (r_factor / jnp.sqrt(total)).astype(jnp.float32)
    return (basis, factor)
```

```python
import functools

import jax
import jax.numpy as jnp
from jax import lax
from jax.experimental import pallas as pl
from jax.experimental.pallas import tpu as pltpu
from jax.sharding import PartitionSpec as P

RB_DEV = 8
CAP = 4
PANEL = 64
LOADS = 4
NOWHERE = 1 << 20
CHUNKS = 4
WIDE = 4
MESH = pl.DeviceIdType.MESH
VMEM = pl.BlockSpec(memory_space=pltpu.VMEM)
SMEM = pl.BlockSpec(memory_space=pltpu.SMEM)
HIGH = lax.Precision.HIGHEST


def dot_nn(a, b):
    return lax.dot_general(a, b, (((1,), (0,)), ((), ())), precision=HIGH, preferred_element_type=jnp.float32)


def dot_nt(a, b):
    return lax.dot_general(a, b, (((1,), (1,)), ((), ())), precision=HIGH, preferred_element_type=jnp.float32)


def dot_tn(a, b):
    return lax.dot_general(a, b, (((0,), (0,)), ((), ())), precision=HIGH, preferred_element_type=jnp.float32)


def partial_kernel(dest_ref, target_ref, col_ref, a_hbm, omega_hbm, out_ref, row_ref, a_buf, omega_buf, slot_of, count, a_sem, omega_sem):
    targets, groups, order, _ = a_buf.shape
    chunks, slots, rq, _ = out_ref.shape
    loads = targets // LOADS

    def fetch(i):
        part = pl.ds(i * LOADS, LOADS)
        return pltpu.make_async_copy(a_hbm.at[part], a_buf.at[part], a_sem.at[i])

    load_omega = pltpu.make_async_copy(omega_hbm, omega_buf, omega_sem.at[0])
    load_omega.start()
    for i in range(loads):
        fetch(i).start()
    owners = slots // CAP
    row_ref[...] = jnp.full(row_ref.shape, NOWHERE, jnp.int32)
    if slots > targets:
        out_ref[...] = jnp.zeros(out_ref.shape, out_ref.dtype)
    for d in range(owners):
        count[d] = 0

    @pl.loop(0, targets)
    def _(t):
        d = dest_ref[t]
        rank = count[d]
        count[d] = rank + 1
        slot_of[t] = d * CAP + rank
        row_ref[d, pl.ds(rank, 1), :] = jnp.full((1, row_ref.shape[2]), target_ref[t], jnp.int32)

    load_omega.wait()

    @pl.loop(0, loads)
    def _(i):
        fetch(i).wait()
        for local in range(LOADS):
            t = i * LOADS + local
            total = None
            for g in range(0, groups, 2):
                left = jnp.concatenate([a_buf[t, g], a_buf[t, g + 1]], axis=1)
                c0 = pl.multiple_of(col_ref[t * groups + g] * order, order)
                c1 = pl.multiple_of(col_ref[t * groups + g + 1] * order, order)
                right = jnp.concatenate([omega_buf[pl.ds(c0, order), :], omega_buf[pl.ds(c1, order), :]], axis=0)
                term = jnp.dot(left, right, preferred_element_type=jnp.float32)
                total = term if total is None else total + term
            total = total.astype(jnp.bfloat16)
            for q in range(chunks):
                out_ref[q, slot_of[t]] = total[q * rq:(q + 1) * rq]


def partials(destination, row_target, col_flat, a_blocks, omega, slots):
    targets, _, order, _ = a_blocks.shape
    width = omega.shape[1]
    dma = pltpu.SemaphoreType.DMA
    any_space = pl.BlockSpec(memory_space=pl.ANY)
    return pl.pallas_call(
        partial_kernel,
        out_shape=(
            jax.ShapeDtypeStruct((CHUNKS, slots, order // CHUNKS, width), jnp.bfloat16),
            jax.ShapeDtypeStruct((slots // CAP, 8, 128), jnp.int32),
        ),
        in_specs=[SMEM, SMEM, SMEM, any_space, any_space],
        out_specs=(VMEM, VMEM),
        scratch_shapes=[
            pltpu.VMEM(a_blocks.shape, a_blocks.dtype),
            pltpu.VMEM(omega.shape, omega.dtype),
            pltpu.SMEM((targets,), jnp.int32),
            pltpu.SMEM((slots // CAP,), jnp.int32),
            dma((targets // LOADS,)), dma((1,)),
        ],
        compiler_params=pltpu.CompilerParams(vmem_limit_bytes=40 << 20),
    )(destination, row_target, col_flat, a_blocks, omega)


def greet(nr, nc, r, c):
    barrier = pltpu.get_barrier_semaphore()
    for k in range(1, nr):
        pl.semaphore_signal(barrier, inc=1, device_id=(lax.rem(r + k, nr), c), device_id_type=MESH)
    for k in range(1, nc):
        pl.semaphore_signal(barrier, inc=1, device_id=(r, lax.rem(c + k, nc)), device_id_type=MESH)
    pl.semaphore_wait(barrier, nr - 1 + nc - 1)


def reduce_packed(nr, nc, r, c, gram, landed, cols, full, sems):
    a_s, a_r, b_s, b_r, c_s, c_r = sems
    chunk = gram.shape[0] // nr
    mine = pl.ds(pl.multiple_of(r * chunk, chunk), chunk)
    copies = []
    for k in range(1, nr):
        d = lax.rem(r + k, nr)
        cp = pltpu.make_async_remote_copy(
            gram.at[pl.ds(pl.multiple_of(d * chunk, chunk), chunk), :], landed.at[k], a_s.at[k], a_r.at[k],
            device_id=(d, c), device_id_type=MESH)
        cp.start()
        copies.append(cp)
    total = gram[mine, :]
    for k in range(1, nr):
        copies[k - 1].wait_recv()
        total = total + landed[k]
    cols[c] = total
    across = []
    for k in range(1, nc):
        cp = pltpu.make_async_remote_copy(
            cols.at[c], cols.at[c], b_s.at[k], b_r.at[k], device_id=(r, lax.rem(c + k, nc)), device_id_type=MESH)
        cp.start()
        across.append(cp)
    for cp in across:
        cp.wait_recv()
    total = cols[0]
    for k in range(1, nc):
        total = total + cols[k]
    full[mine, :] = total
    back = []
    for k in range(1, nr):
        cp = pltpu.make_async_remote_copy(
            full.at[mine, :], full.at[mine, :], c_s.at[k], c_r.at[k], device_id=(lax.rem(r + k, nr), c), device_id_type=MESH)
        cp.start()
        back.append(cp)
    for cp in back:
        cp.wait_recv()
    for cp in copies + across + back:
        cp.wait_send()


def packed_scratch(nr, nc, width):
    dma = pltpu.SemaphoreType.DMA
    half = width // 2
    chunk = 3 * half // nr
    return [
        pltpu.VMEM((3 * half, half), jnp.float32),
        pltpu.VMEM((nr, chunk, half), jnp.float32),
        pltpu.VMEM((nc, chunk, half), jnp.float32),
        pltpu.VMEM((3 * half, half), jnp.float32),
        dma((nr,)), dma((nr,)), dma((nc,)), dma((nc,)), dma((nr,)), dma((nr,)),
    ]


def sum_gram(nr, nc, r, c, gram, out_ref, packed, landed, cols, full, sems):
    half = gram.shape[0] // 2
    packed[:half, :] = gram[:half, :half]
    packed[half:2 * half, :] = gram[:half, half:]
    packed[2 * half:, :] = gram[half:, half:]
    reduce_packed(nr, nc, r, c, packed, landed, cols, full, sems)
    out_ref[:half, :half] = full[:half, :]
    side = full[half:2 * half, :]
    out_ref[:half, half:] = side
    out_ref[half:, :half] = side.T
    out_ref[half:, half:] = full[2 * half:, :]


def arrange(rows, slots):
    count = rows.shape[0]
    i = lax.broadcasted_iota(jnp.int32, rows.shape, 0)
    j = lax.broadcasted_iota(jnp.int32, rows.shape, 1)
    across = jnp.sum(jnp.where(i == j, rows, 0), axis=0, keepdims=True)
    ahead = jnp.logical_or(across < rows, jnp.logical_and(across == rows, j < i))
    ahead = jnp.logical_and(ahead, j < count)
    rank = jnp.sum(ahead.astype(jnp.int32), axis=1, keepdims=True)
    slot = (i // 8) * CAP + lax.rem(i, 8)
    order = jnp.sum(jnp.where(rank == j, slot, 0), axis=0, keepdims=True)
    here = jnp.sum(jnp.where(rank == j, rows, 0), axis=0, keepdims=True)
    before = jnp.sum(jnp.where(rank == j - 1, rows, 0), axis=0, keepdims=True)
    keep = jnp.logical_and(here == before, j[:1] > 0).astype(jnp.int32)
    last = jnp.max(jnp.where(rows == j, rank, -1), axis=0, keepdims=True)
    valid = (last >= 0).astype(jnp.int32)
    order = jnp.minimum(order, slots - 1)
    last = jnp.clip(last, 0, slots - 1)
    return jnp.concatenate([order, keep, last, valid], axis=0)


def sketch_kernel(nr, nc, send_ref, row_ref, sketch_ref, out_ref, *refs):
    chunks, _, _, rq, width = send_ref.shape
    gots, refs = refs[:chunks], refs[chunks:]
    (rows_in, meta, table, prefix, term, to_right, to_left, total, gram, row_s, row_r, own_s,
     send_s, send_r, right_s, right_r, left_s, left_r), refs = refs[:18], refs[18:]
    slots = nr * CAP
    blocks = nc * RB_DEV
    r = lax.axis_index("row")
    c = lax.axis_index("col")

    def route(k):
        d = lax.rem(r + k, nr)
        return pltpu.make_async_remote_copy(
            row_ref.at[d], rows_in.at[r], row_s.at[k], row_r.at[k], device_id=(d, c), device_id_type=MESH)

    def swap(q, k):
        d = lax.rem(r + k, nr)
        return pltpu.make_async_remote_copy(
            send_ref.at[q, d], gots[q].at[pl.ds(r * CAP, CAP)], send_s.at[q, k], send_r.at[q, k],
            device_id=(d, c), device_id_type=MESH)

    def keep_own(q):
        return pltpu.make_async_copy(send_ref.at[q, r], gots[q].at[pl.ds(r * CAP, CAP)], own_s.at[q])

    def hop_right(q, d):
        return pltpu.make_async_remote_copy(
            to_right.at[q, d], to_right.at[q, d], right_s.at[q, d], right_r.at[q, d],
            device_id=(r, lax.rem(c + 1, nc)), device_id_type=MESH)

    def hop_left(q, d):
        return pltpu.make_async_remote_copy(
            to_left.at[q, d], to_left.at[q, d], left_s.at[q, d], left_r.at[q, d],
            device_id=(r, lax.rem(c + nc - 1, nc)), device_id_type=MESH)

    for q in range(chunks):
        keep_own(q).start()
    own_rows = pltpu.make_async_copy(row_ref.at[r], rows_in.at[r], own_s.at[chunks])
    own_rows.start()
    greet(nr, nc, r, c)
    for k in range(1, nr):
        route(k).start()
    for k in range(1, nr):
        swap(0, k).start()
    gram[...] = jnp.zeros_like(gram)
    own_rows.wait()
    for k in range(1, nr):
        route(k).wait_recv()
    meta[...] = jnp.zeros_like(meta)
    meta[:4, :] = arrange(rows_in[...].reshape(nr * 8, 128), slots)
    to_table = pltpu.make_async_copy(meta, table, own_s.at[chunks + 1])
    to_table.start()
    to_table.wait()

    def collect(q):
        keep_own(q).wait()
        for k in range(1, nr):
            swap(q, k).wait_recv()
        if q + 1 < chunks:
            for k in range(1, nr):
                swap(q + 1, k).start()
        got = gots[q]

        def add(k, acc):
            acc = acc * table[1, k].astype(jnp.float32) + got[table[0, k]].astype(jnp.float32)
            prefix[k] = acc
            return acc

        lax.fori_loop(0, slots, add, jnp.zeros((rq, width), jnp.float32), unroll=4)

        @pl.loop(0, blocks, unroll=4)
        def _(b):
            term[q % 2, b] = prefix[table[2, b]] * table[3, b].astype(jnp.float32)

        @pl.when(c == 0)
        def _():
            for d in range(nc - 1, 0, -1):
                to_right[q, d] = term[q % 2, d * RB_DEV:(d + 1) * RB_DEV].astype(jnp.bfloat16)
                hop_right(q, d).start()

        @pl.when(c == nc - 1)
        def _():
            for d in range(nc - 1):
                to_left[q, d] = term[q % 2, d * RB_DEV:(d + 1) * RB_DEV].astype(jnp.bfloat16)
                hop_left(q, d).start()

    def pass_on(q):
        for k in range(nc - 1, 0, -1):
            @pl.when(jnp.logical_and(c > 0, c + k < nc))
            def _():
                d = c + k
                hop_right(q, d).wait_recv()
                mine = term[q % 2, pl.ds(d * RB_DEV, RB_DEV)]
                to_right[q, d] = (to_right[q, d].astype(jnp.float32) + mine).astype(jnp.bfloat16)
                hop_right(q, d).start()

            @pl.when(jnp.logical_and(c < nc - 1, c - k >= 0))
            def _():
                d = c - k
                hop_left(q, d).wait_recv()
                mine = term[q % 2, pl.ds(d * RB_DEV, RB_DEV)]
                to_left[q, d] = (to_left[q, d].astype(jnp.float32) + mine).astype(jnp.bfloat16)
                hop_left(q, d).start()

        total[...] = term[q % 2, pl.ds(c * RB_DEV, RB_DEV)]

        @pl.when(c > 0)
        def _():
            hop_right(q, c).wait_recv()
            total[...] += to_right[q, c].astype(jnp.float32)

        @pl.when(c < nc - 1)
        def _():
            hop_left(q, c).wait_recv()
            total[...] += to_left[q, c].astype(jnp.float32)

        for b in range(RB_DEV):
            start = b * chunks * rq + q * rq
            sketch_ref[start:start + rq, :] = total[b]
        rows = total[...].reshape(RB_DEV * rq, width)
        gram[...] += dot_tn(rows, rows)

    for q in range(chunks):
        collect(q)
        if q > 0:
            pass_on(q - 1)
    pass_on(chunks - 1)
    sum_gram(nr, nc, r, c, gram, out_ref, *refs[:4], refs[4:])
    for k in range(1, nr):
        route(k).wait_send()
    for q in range(chunks):
        for k in range(1, nr):
            swap(q, k).wait_send()
        for k in range(1, nc):
            @pl.when(c + k < nc)
            def _():
                hop_right(q, c + k).wait_send()

            @pl.when(c - k >= 0)
            def _():
                hop_left(q, c - k).wait_send()


def make_sketch(send, rows, nr, nc):
    chunks, _, _, rq, width = send.shape
    dma = pltpu.SemaphoreType.DMA
    slots, blocks = nr * CAP, nc * RB_DEV
    hops = pltpu.VMEM((chunks, nc, RB_DEV, rq, width), jnp.bfloat16)
    return pl.pallas_call(
        functools.partial(sketch_kernel, nr, nc),
        out_shape=(
            jax.ShapeDtypeStruct((RB_DEV * chunks * rq, width), jnp.float32),
            jax.ShapeDtypeStruct((width, width), jnp.float32),
        ),
        in_specs=[VMEM, VMEM],
        out_specs=(VMEM, VMEM),
        scratch_shapes=[pltpu.VMEM((slots, rq, width), jnp.bfloat16)] * chunks + [
            pltpu.VMEM((nr, 8, 128), jnp.int32),
            pltpu.VMEM((8, 128), jnp.int32),
            pltpu.SMEM((8, 128), jnp.int32),
            pltpu.VMEM((slots, rq, width), jnp.float32),
            pltpu.VMEM((2, blocks, rq, width), jnp.float32),
            hops, hops,
            pltpu.VMEM((RB_DEV, rq, width), jnp.float32),
            pltpu.VMEM((width, width), jnp.float32),
            dma((nr,)), dma((nr,)), dma((chunks + 2,)),
            dma((chunks, nr)), dma((chunks, nr)),
            dma((chunks, nc)), dma((chunks, nc)), dma((chunks, nc)), dma((chunks, nc)),
        ] + packed_scratch(nr, nc, width),
        compiler_params=pltpu.CompilerParams(collective_id=1, has_side_effects=True, vmem_limit_bytes=32 << 20),
    )(send, rows)


def gram_sum_kernel(nr, nc, gram, out_ref, packed, landed, cols, full, *sems):
    r = lax.axis_index("row")
    c = lax.axis_index("col")
    greet(nr, nc, r, c)
    sum_gram(nr, nc, r, c, gram, out_ref, packed, landed, cols, full, sems)


def gram_sum(gram, nr, nc):
    return pl.pallas_call(
        functools.partial(gram_sum_kernel, nr, nc),
        out_shape=jax.ShapeDtypeStruct(gram.shape, jnp.float32),
        in_specs=[VMEM],
        out_specs=VMEM,
        scratch_shapes=packed_scratch(nr, nc, gram.shape[0]),
        compiler_params=pltpu.CompilerParams(collective_id=3, has_side_effects=True, vmem_limit_bytes=8 << 20),
    )(gram)


def eliminate(x):
    rows = x.shape[0]
    shape = (8, x.shape[1])
    groups = [x[i:i + 8, :] for i in range(0, rows, 8)]
    sub = lax.broadcasted_iota(jnp.int32, shape, 0)
    for j in range(0, rows, WIDE):
        g, o = divmod(j, 8)
        cols = [[jnp.broadcast_to(groups[i][:, j + l:j + l + 1], shape) for l in range(WIDE)]
                for i in range(g, rows // 8)]
        piv = [[jnp.broadcast_to(cols[0][l][o + k:o + k + 1, :], shape) for l in range(WIDE)] for k in range(WIDE)]
        tops = [jnp.broadcast_to(groups[g][o + k:o + k + 1, :], shape) for k in range(WIDE)]
        recip = []
        for k in range(WIDE):
            recip.append(1.0 / piv[k][k])
            for m in range(k + 1, WIDE):
                q = piv[m][k] * recip[k]
                for l in range(k + 1, WIDE):
                    piv[m][l] = piv[m][l] - q * piv[k][l]
                tops[m] = tops[m] - q * tops[k]
        for i in range(g, rows // 8):
            here = cols[i - g]
            value = groups[i]
            for k in range(WIDE):
                f = here[k] * recip[k]
                for l in range(k + 1, WIDE):
                    here[l] = here[l] - f * piv[k][l]
                value = value - f * tops[k]
            if i == g:
                value = jnp.where(sub >= o + WIDE, value, groups[i])
                for k in range(1, WIDE):
                    value = jnp.where(sub == o + k, tops[k], value)
            groups[i] = value
    return jnp.concatenate(groups, axis=0)


def factor_gram(gram, work, upper, inverse):
    order = gram.shape[0]
    row = lax.broadcasted_iota(jnp.int32, (order, order), 0)
    col = lax.broadcasted_iota(jnp.int32, (order, order), 1)
    work[:, :order] = gram[...]
    work[:, order:] = (row == col).astype(jnp.float32)
    lane = lax.broadcasted_iota(jnp.int32, (PANEL, 2 * PANEL), 1)
    prow = lax.broadcasted_iota(jnp.int32, (PANEL, 2 * PANEL), 0)

    @pl.loop(0, order // PANEL)
    def _(p):
        base = pl.multiple_of(p * PANEL, PANEL)
        tile = work[pl.ds(base, PANEL), pl.ds(pl.multiple_of((p // 2) * 2 * PANEL, 2 * PANEL), 2 * PANEL)]
        tile = jnp.where(p % 2 == 1, pltpu.roll(tile, PANEL, 1), tile)
        x = jnp.where(lane < PANEL, tile, (lane - PANEL == prow).astype(jnp.float32))
        x = eliminate(x)
        diag = jnp.sum(jnp.where(lane == prow, x, 0.0), axis=1, keepdims=True)
        left = pltpu.roll(x, PANEL, 1)[:, :PANEL]
        panel = dot_nn(left, work[pl.ds(base, PANEL), :])
        root = 1.0 / jnp.sqrt(diag)
        pcol = lax.broadcasted_iota(jnp.int32, (PANEL, order), 1)
        pr = lax.broadcasted_iota(jnp.int32, (PANEL, order), 0) + base
        upper[pl.ds(base, PANEL), :] = jnp.where(pcol >= pr, panel[:, :order] * root, 0.0)
        inverse[pl.ds(base, PANEL), :] = jnp.where(pcol <= pr, panel[:, order:] * root, 0.0)

        @pl.when(p < order // PANEL - 1)
        def _():
            half = panel * root
            update = dot_tn(half[:, :order], half)
            below = lax.broadcasted_iota(jnp.int32, (order, 1), 0) >= base + PANEL
            work[...] = jnp.where(below, work[...] - update, work[...])


def first_kernel(gram, sketch, upper, once, second, work, inverse):
    factor_gram(gram, work, upper, inverse)
    second[...] = jnp.zeros_like(second)
    step = 256

    @pl.loop(0, sketch.shape[0] // step)
    def _(i):
        part = pl.ds(pl.multiple_of(i * step, step), step)
        rows = dot_nt(sketch[part, :], inverse[...])
        once[part, :] = rows
        second[...] += dot_tn(rows, rows)


def first_pass(gram, sketch):
    order = gram.shape[0]
    square = jax.ShapeDtypeStruct((order, order), jnp.float32)
    return pl.pallas_call(
        first_kernel,
        out_shape=(square, jax.ShapeDtypeStruct(sketch.shape, jnp.float32), square),
        in_specs=[VMEM, VMEM],
        out_specs=(VMEM, VMEM, VMEM),
        scratch_shapes=[pltpu.VMEM((order, 2 * order), jnp.float32), pltpu.VMEM((order, order), jnp.float32)],
        compiler_params=pltpu.CompilerParams(vmem_limit_bytes=16 << 20),
    )(gram, sketch)


def last_kernel(scale, gram, once, upper_one, basis, factor, work, upper, inverse):
    factor_gram(gram, work, upper, inverse)
    factor[...] = dot_nn(upper[...], upper_one[...]) * (1.0 / scale)
    step = 256

    @pl.loop(0, once.shape[0] // step)
    def _(i):
        part = pl.ds(pl.multiple_of(i * step, step), step)
        basis[part, :] = dot_nt(once[part, :], inverse[...]) * scale


def last_pass(gram, once, upper_one, scale):
    order = gram.shape[0]
    square = pltpu.VMEM((order, order), jnp.float32)
    return pl.pallas_call(
        functools.partial(last_kernel, scale),
        out_shape=(
            jax.ShapeDtypeStruct(once.shape, jnp.float32),
            jax.ShapeDtypeStruct((order, order), jnp.float32),
        ),
        in_specs=[VMEM, VMEM, VMEM],
        out_specs=(VMEM, VMEM),
        scratch_shapes=[pltpu.VMEM((order, 2 * order), jnp.float32), square, square],
        compiler_params=pltpu.CompilerParams(vmem_limit_bytes=16 << 20),
    )(gram, once, upper_one)


def body(nr, nc, a_blocks, omega, route_dest, row_target, col_target):
    order = a_blocks.shape[2]
    width = omega.shape[1]
    slots = nr * CAP
    send, rows = partials(route_dest.reshape(-1), row_target, col_target.reshape(-1), a_blocks, omega, slots)
    send = send.reshape(CHUNKS, nr, CAP, order // CHUNKS, width)
    sketch, gram_one = make_sketch(send, rows, nr, nc)
    upper_one, once, gram_part = first_pass(gram_one, sketch)
    gram_two = gram_sum(gram_part, nr, nc)
    scale = float(nr * nc * RB_DEV * order) ** 0.5
    return last_pass(gram_two, once, upper_one, scale)


def solution(mesh):
    nr, nc = mesh.shape["row"], mesh.shape["col"]
    return jax.shard_map(
        functools.partial(body, nr, nc),
        mesh=mesh,
        in_specs=(
            P(("row", "col"), None, None, None),
            P("col", None),
            P(("row", "col"), None),
            P(("row", "col")),
            P(("row", "col"), None),
        ),
        out_specs=(P(("row", "col"), None), P()),
        check_vma=False,
    )
```

```python
import functools

import jax
import jax.numpy as jnp
from jax import lax
from jax.experimental import pallas as pl
from jax.experimental.pallas import tpu as pltpu
from jax.sharding import PartitionSpec as P

RB_DEV = 8
CAP = 4
PANEL = 64
LOADS = 4
NOWHERE = 1 << 20
INFLATION = 2.0
CHUNKS = 8
WINDOW = 2
WIDE = 4
MESH = pl.DeviceIdType.MESH
VMEM = pl.BlockSpec(memory_space=pltpu.VMEM)
SMEM = pl.BlockSpec(memory_space=pltpu.SMEM)
HIGH = lax.Precision.HIGHEST


def dot_nn(a, b):
    return lax.dot_general(a, b, (((1,), (0,)), ((), ())), precision=HIGH, preferred_element_type=jnp.float32)


def dot_nt(a, b):
    return lax.dot_general(a, b, (((1,), (1,)), ((), ())), precision=HIGH, preferred_element_type=jnp.float32)


def dot_tn(a, b):
    return lax.dot_general(a, b, (((0,), (0,)), ((), ())), precision=HIGH, preferred_element_type=jnp.float32)


def place(dest, target, owners):
    count = dest.shape[1]
    i = lax.broadcasted_iota(jnp.int32, (count, count), 0)
    j = lax.broadcasted_iota(jnp.int32, (count, count), 1)
    down = jnp.sum(jnp.where(i == j, dest, 0), axis=1, keepdims=True)
    rank = jnp.sum(jnp.logical_and(down == dest, j < i).astype(jnp.int32), axis=1, keepdims=True)
    rank_across = jnp.sum(jnp.where(i == j, rank, 0), axis=0, keepdims=True)
    lane = lax.broadcasted_iota(jnp.int32, (count, 128), 1)
    which = lax.broadcasted_iota(jnp.int32, (count, 128), 0)
    source = jnp.sum(jnp.where(down * CAP + rank == lane, which, 0), axis=0, keepdims=True)
    place_of = lax.broadcasted_iota(jnp.int32, (owners * 8, count), 0)
    here = place_of == dest * 8 + rank_across
    rows = jnp.sum(jnp.where(here, target + 1, 0), axis=1, keepdims=True)
    rows = jnp.where(rows > 0, rows - 1, NOWHERE)
    return source, jnp.broadcast_to(rows, (owners * 8, 128))


def signal_all(nr, nc, r, c):
    barrier = pltpu.get_barrier_semaphore()
    for k in range(1, nr):
        pl.semaphore_signal(barrier, inc=1, device_id=(lax.rem(r + k, nr), c), device_id_type=MESH)
    for k in range(1, nc):
        pl.semaphore_signal(barrier, inc=1, device_id=(r, lax.rem(c + k, nc)), device_id_type=MESH)


def wait_all(nr, nc):
    pl.semaphore_wait(pltpu.get_barrier_semaphore(), nr - 1 + nc - 1)


def greet(nr, nc, r, c):
    signal_all(nr, nc, r, c)
    wait_all(nr, nc)


def reduce_packed(nr, nc, r, c, gram, landed, cols, full, sems):
    a_s, a_r, b_s, b_r, c_s, c_r = sems
    chunk = gram.shape[0] // nr
    mine = pl.ds(pl.multiple_of(r * chunk, chunk), chunk)
    copies = []
    for k in range(1, nr):
        d = lax.rem(r + k, nr)
        cp = pltpu.make_async_remote_copy(
            gram.at[pl.ds(pl.multiple_of(d * chunk, chunk), chunk), :], landed.at[k], a_s.at[k], a_r.at[k],
            device_id=(d, c), device_id_type=MESH)
        cp.start()
        copies.append(cp)
    total = gram[mine, :]
    for k in range(1, nr):
        copies[k - 1].wait_recv()
        total = total + landed[k]
    cols[c] = total
    across = []
    for k in range(1, nc):
        cp = pltpu.make_async_remote_copy(
            cols.at[c], cols.at[c], b_s.at[k], b_r.at[k], device_id=(r, lax.rem(c + k, nc)), device_id_type=MESH)
        cp.start()
        across.append(cp)
    for cp in across:
        cp.wait_recv()
    total = cols[0]
    for k in range(1, nc):
        total = total + cols[k]
    full[mine, :] = total
    back = []
    for k in range(1, nr):
        cp = pltpu.make_async_remote_copy(
            full.at[mine, :], full.at[mine, :], c_s.at[k], c_r.at[k], device_id=(lax.rem(r + k, nr), c), device_id_type=MESH)
        cp.start()
        back.append(cp)
    for cp in back:
        cp.wait_recv()
    for cp in copies + across + back:
        cp.wait_send()


def packed_scratch(nr, nc, width):
    dma = pltpu.SemaphoreType.DMA
    half = width // 2
    chunk = 3 * half // nr
    return [
        pltpu.VMEM((3 * half, half), jnp.float32),
        pltpu.VMEM((nr, chunk, half), jnp.float32),
        pltpu.VMEM((nc, chunk, half), jnp.float32),
        pltpu.VMEM((3 * half, half), jnp.float32),
        dma((nr,)), dma((nr,)), dma((nc,)), dma((nc,)), dma((nr,)), dma((nr,)),
    ]


def sum_gram(nr, nc, r, c, gram, out_ref, packed, landed, cols, full, sems):
    half = gram.shape[0] // 2
    packed[:half, :] = gram[:half, :half]
    packed[half:2 * half, :] = gram[:half, half:]
    packed[2 * half:, :] = gram[half:, half:]
    reduce_packed(nr, nc, r, c, packed, landed, cols, full, sems)
    out_ref[:half, :half] = full[:half, :]
    side = full[half:2 * half, :]
    out_ref[:half, half:] = side
    out_ref[half:, :half] = side.T
    out_ref[half:, half:] = full[2 * half:, :]


def arrange(rows, slots):
    count = rows.shape[0]
    i = lax.broadcasted_iota(jnp.int32, rows.shape, 0)
    j = lax.broadcasted_iota(jnp.int32, rows.shape, 1)
    across = jnp.sum(jnp.where(i == j, rows, 0), axis=0, keepdims=True)
    ahead = jnp.logical_or(across < rows, jnp.logical_and(across == rows, j < i))
    ahead = jnp.logical_and(ahead, j < count)
    rank = jnp.sum(ahead.astype(jnp.int32), axis=1, keepdims=True)
    slot = (i // 8) * CAP + lax.rem(i, 8)
    order = jnp.sum(jnp.where(rank == j, slot, 0), axis=0, keepdims=True)
    here = jnp.sum(jnp.where(rank == j, rows, 0), axis=0, keepdims=True)
    before = jnp.sum(jnp.where(rank == j - 1, rows, 0), axis=0, keepdims=True)
    keep = jnp.logical_and(here == before, j[:1] > 0).astype(jnp.int32)
    last = jnp.max(jnp.where(rows == j, rank, -1), axis=0, keepdims=True)
    valid = (last >= 0).astype(jnp.int32)
    order = jnp.minimum(order, slots - 1)
    last = jnp.clip(last, 0, slots - 1)
    return jnp.concatenate([order, keep, last, valid], axis=0)


def sketch_kernel(nr, nc, dest_hbm, target_hbm, col_hbm, a_hbm, omega_hbm, sketch_ref, out_ref, *refs):
    chunks = CHUNKS
    gots, refs = refs[:chunks], refs[chunks:]
    (dest_ref, target_ref, col_ref, a_buf, omega_buf, parts, send_ref, row_ref, sources, a_sem, in_sem,
     rows_in, meta, table, prefix, term, to_right, to_left, total, gram, row_s, row_r, own_s,
     send_s, send_r, right_s, right_r, left_s, left_r), refs = refs[:29], refs[29:]
    targets, groups, order, _ = a_buf.shape
    rq, width = order // chunks, omega_buf.shape[2]
    slots = nr * CAP
    blocks = nc * RB_DEV
    loads = targets // LOADS
    r = lax.axis_index("row")
    c = lax.axis_index("col")

    def fetch(i):
        part = pl.ds(i * LOADS, LOADS)
        return pltpu.make_async_copy(a_hbm.at[part], a_buf.at[part], a_sem.at[i])

    def route(k):
        d = lax.rem(r + k, nr)
        return pltpu.make_async_remote_copy(
            row_ref.at[d], rows_in.at[r], row_s.at[k], row_r.at[k], device_id=(d, c), device_id_type=MESH)

    def swap(q, k):
        d = lax.rem(r + k, nr)
        return pltpu.make_async_remote_copy(
            send_ref.at[q, d], gots[q].at[pl.ds(r * CAP, CAP)], send_s.at[q, k], send_r.at[q, k],
            device_id=(d, c), device_id_type=MESH)

    def keep_own(q):
        return pltpu.make_async_copy(send_ref.at[q, r], gots[q].at[pl.ds(r * CAP, CAP)], own_s.at[q])

    def hop_right(q, d):
        return pltpu.make_async_remote_copy(
            to_right.at[q, d], to_right.at[q, d], right_s.at[q, d], right_r.at[q, d],
            device_id=(r, lax.rem(c + 1, nc)), device_id_type=MESH)

    def hop_left(q, d):
        return pltpu.make_async_remote_copy(
            to_left.at[q, d], to_left.at[q, d], left_s.at[q, d], left_r.at[q, d],
            device_id=(r, lax.rem(c + nc - 1, nc)), device_id_type=MESH)

    others = [pltpu.make_async_copy(src, dst, in_sem.at[i]) for i, (src, dst) in enumerate(
        ((dest_hbm, dest_ref), (target_hbm, target_ref), (col_hbm, col_ref), (omega_hbm, omega_buf)))]
    for copy in others:
        copy.start()
    for i in range(loads):
        fetch(i).start()
    signal_all(nr, nc, r, c)
    others[0].wait()
    others[1].wait()
    source, rows = place(dest_ref[...], target_ref[...], nr)
    row_ref[...] = rows.reshape(nr, 8, 128)
    meta[...] = jnp.zeros_like(meta)
    meta[:1, :] = source
    to_sources = pltpu.make_async_copy(meta, sources, own_s.at[chunks + 1])
    to_sources.start()
    own_rows = pltpu.make_async_copy(row_ref.at[r], rows_in.at[r], own_s.at[chunks])
    own_rows.start()
    gram[...] = jnp.zeros_like(gram)
    to_sources.wait()
    wait_all(nr, nc)
    for k in range(1, nr):
        route(k).start()
    own_rows.wait()
    others[2].wait()
    others[3].wait()

    @pl.loop(0, loads)
    def _(i):
        fetch(i).wait()
        for local in range(LOADS):
            t = i * LOADS + local
            sums = None
            for g in range(0, groups, 2):
                left = jnp.concatenate([a_buf[t, g], a_buf[t, g + 1]], axis=1)
                right = jnp.concatenate([omega_buf[col_ref[g, t]], omega_buf[col_ref[g + 1, t]]], axis=0)
                product = jnp.dot(left, right, preferred_element_type=jnp.float32)
                sums = product if sums is None else sums + product
            sums = sums.astype(jnp.bfloat16)
            for q in range(chunks):
                parts[q, t] = sums[q * rq:(q + 1) * rq]

    for q in range(chunks):
        for d in range(nr):
            for k in range(CAP):
                send_ref[q, d, k] = parts[q, sources[0, d * CAP + k]]
        keep_own(q).start()
        if q == 0:
            for k in range(1, nr):
                swap(0, k).start()
    for k in range(1, nr):
        route(k).wait_recv()
    meta[:4, :] = arrange(rows_in[...].reshape(nr * 8, 128), slots)
    to_table = pltpu.make_async_copy(meta, table, own_s.at[chunks + 1])
    to_table.start()
    to_table.wait()

    def collect(q):
        keep_own(q).wait()
        for k in range(1, nr):
            swap(q, k).wait_send()
        if q + 1 < chunks:
            for k in range(1, nr):
                swap(q + 1, k).start()
        for k in range(1, nr):
            swap(q, k).wait_recv()
        got = gots[q]

        def add(k, acc):
            acc = acc * table[1, k].astype(jnp.float32) + got[table[0, k]].astype(jnp.float32)
            prefix[k] = acc
            return acc

        lax.fori_loop(0, slots, add, jnp.zeros((rq, width), jnp.float32), unroll=4)

        @pl.loop(0, blocks, unroll=4)
        def _(b):
            term[q % 2, b] = prefix[table[2, b]] * table[3, b].astype(jnp.float32)

        @pl.when(c == 0)
        def _():
            for d in range(nc - 1, 0, -1):
                n = q * (nc - 1) + nc - 1 - d - WINDOW
                if n >= 0:
                    hop_right(n // (nc - 1), nc - 1 - n % (nc - 1)).wait_send()
                to_right[q, d] = term[q % 2, d * RB_DEV:(d + 1) * RB_DEV].astype(jnp.bfloat16)
                hop_right(q, d).start()

        @pl.when(c == nc - 1)
        def _():
            for d in range(nc - 1):
                n = q * (nc - 1) + d - WINDOW
                if n >= 0:
                    hop_left(n // (nc - 1), n % (nc - 1)).wait_send()
                to_left[q, d] = term[q % 2, d * RB_DEV:(d + 1) * RB_DEV].astype(jnp.bfloat16)
                hop_left(q, d).start()

    def pass_on(q):
        for k in range(nc - 1, 0, -1):
            @pl.when(jnp.logical_and(c > 0, c + k < nc))
            def _():
                d = c + k
                hop_right(q, d).wait_recv()
                mine = term[q % 2, pl.ds(d * RB_DEV, RB_DEV)]
                to_right[q, d] = (to_right[q, d].astype(jnp.float32) + mine).astype(jnp.bfloat16)
                hop_right(q, d).start()

            @pl.when(jnp.logical_and(c < nc - 1, c - k >= 0))
            def _():
                d = c - k
                hop_left(q, d).wait_recv()
                mine = term[q % 2, pl.ds(d * RB_DEV, RB_DEV)]
                to_left[q, d] = (to_left[q, d].astype(jnp.float32) + mine).astype(jnp.bfloat16)
                hop_left(q, d).start()

        total[...] = term[q % 2, pl.ds(c * RB_DEV, RB_DEV)]

        @pl.when(c > 0)
        def _():
            hop_right(q, c).wait_recv()
            total[...] += to_right[q, c].astype(jnp.float32)

        @pl.when(c < nc - 1)
        def _():
            hop_left(q, c).wait_recv()
            total[...] += to_left[q, c].astype(jnp.float32)

        for b in range(RB_DEV):
            start = b * chunks * rq + q * rq
            sketch_ref[start:start + rq, :] = total[b]
        rows = total[...].reshape(RB_DEV * rq, width)
        gram[...] += dot_tn(rows, rows)

    for q in range(chunks):
        collect(q)
        if q > 0:
            pass_on(q - 1)
    pass_on(chunks - 1)
    sum_gram(nr, nc, r, c, gram, out_ref, *refs[:4], refs[4:])
    for k in range(1, nr):
        route(k).wait_send()

    @pl.when(c == 0)
    def _():
        for n in range(chunks * (nc - 1) - WINDOW, chunks * (nc - 1)):
            hop_right(n // (nc - 1), nc - 1 - n % (nc - 1)).wait_send()

    @pl.when(c == nc - 1)
    def _():
        for n in range(chunks * (nc - 1) - WINDOW, chunks * (nc - 1)):
            hop_left(n // (nc - 1), n % (nc - 1)).wait_send()

    for q in range(chunks):
        for k in range(1, nc):
            @pl.when(jnp.logical_and(c > 0, c + k < nc))
            def _():
                hop_right(q, c + k).wait_send()

            @pl.when(jnp.logical_and(c < nc - 1, c - k >= 0))
            def _():
                hop_left(q, c - k).wait_send()


def make_sketch(dest, target, col_target, a_blocks, omega, nr, nc):
    targets, _, order, _ = a_blocks.shape
    width = omega.shape[2]
    chunks, rq = CHUNKS, order // CHUNKS
    dma = pltpu.SemaphoreType.DMA
    slots, blocks = nr * CAP, nc * RB_DEV
    hops = pltpu.VMEM((chunks, nc, RB_DEV, rq, width), jnp.bfloat16)
    hbm = pl.BlockSpec(memory_space=pltpu.HBM)
    return pl.pallas_call(
        functools.partial(sketch_kernel, nr, nc),
        out_shape=(
            jax.ShapeDtypeStruct((RB_DEV * order, width), jnp.float32),
            jax.ShapeDtypeStruct((width, width), jnp.float32),
        ),
        in_specs=[hbm] * 5,
        out_specs=(VMEM, VMEM),
        scratch_shapes=[pltpu.VMEM((slots, rq, width), jnp.bfloat16)] * chunks + [
            pltpu.VMEM(dest.shape, jnp.int32),
            pltpu.VMEM(target.shape, jnp.int32),
            pltpu.SMEM(col_target.shape, jnp.int32),
            pltpu.VMEM(a_blocks.shape, a_blocks.dtype),
            pltpu.VMEM(omega.shape, omega.dtype),
            pltpu.VMEM((chunks, targets, rq, width), jnp.bfloat16),
            pltpu.VMEM((chunks, nr, CAP, rq, width), jnp.bfloat16),
            pltpu.VMEM((nr, 8, 128), jnp.int32),
            pltpu.SMEM((8, 128), jnp.int32),
            dma((targets // LOADS,)), dma((4,)),
            pltpu.VMEM((nr, 8, 128), jnp.int32),
            pltpu.VMEM((8, 128), jnp.int32),
            pltpu.SMEM((8, 128), jnp.int32),
            pltpu.VMEM((slots, rq, width), jnp.float32),
            pltpu.VMEM((2, blocks, rq, width), jnp.float32),
            hops, hops,
            pltpu.VMEM((RB_DEV, rq, width), jnp.float32),
            pltpu.VMEM((width, width), jnp.float32),
            dma((nr,)), dma((nr,)), dma((chunks + 2,)),
            dma((chunks, nr)), dma((chunks, nr)),
            dma((chunks, nc)), dma((chunks, nc)), dma((chunks, nc)), dma((chunks, nc)),
        ] + packed_scratch(nr, nc, width),
        compiler_params=pltpu.CompilerParams(collective_id=1, has_side_effects=True, vmem_limit_bytes=60 << 20),
    )(dest, target, col_target, a_blocks, omega)


def gram_sum_kernel(nr, nc, gram, out_ref, packed, landed, cols, full, *sems):
    r = lax.axis_index("row")
    c = lax.axis_index("col")
    greet(nr, nc, r, c)
    sum_gram(nr, nc, r, c, gram, out_ref, packed, landed, cols, full, sems)


def gram_sum(gram, nr, nc):
    return pl.pallas_call(
        functools.partial(gram_sum_kernel, nr, nc),
        out_shape=jax.ShapeDtypeStruct(gram.shape, jnp.float32),
        in_specs=[VMEM],
        out_specs=VMEM,
        scratch_shapes=packed_scratch(nr, nc, gram.shape[0]),
        compiler_params=pltpu.CompilerParams(collective_id=3, has_side_effects=True, vmem_limit_bytes=8 << 20),
    )(gram)


def eliminate(x):
    rows = x.shape[0]
    shape = (8, x.shape[1])
    groups = [x[i:i + 8, :] for i in range(0, rows, 8)]
    sub = lax.broadcasted_iota(jnp.int32, shape, 0)
    for j in range(0, rows, WIDE):
        g, o = divmod(j, 8)
        cols = [[jnp.broadcast_to(groups[i][:, j + l:j + l + 1], shape) for l in range(WIDE)]
                for i in range(g, rows // 8)]
        piv = [[jnp.broadcast_to(cols[0][l][o + k:o + k + 1, :], shape) for l in range(WIDE)] for k in range(WIDE)]
        tops = [jnp.broadcast_to(groups[g][o + k:o + k + 1, :], shape) for k in range(WIDE)]
        recip = []
        for k in range(WIDE):
            recip.append(1.0 / piv[k][k])
            for m in range(k + 1, WIDE):
                q = piv[m][k] * recip[k]
                for l in range(k + 1, WIDE):
                    piv[m][l] = piv[m][l] - q * piv[k][l]
                tops[m] = tops[m] - q * tops[k]
        for i in range(g, rows // 8):
            here = cols[i - g]
            value = groups[i]
            for k in range(WIDE):
                f = here[k] * recip[k]
                for l in range(k + 1, WIDE):
                    here[l] = here[l] - f * piv[k][l]
                value = value - f * tops[k]
            if i == g:
                value = jnp.where(sub >= o + WIDE, value, groups[i])
                for k in range(1, WIDE):
                    value = jnp.where(sub == o + k, tops[k], value)
            groups[i] = value
    return jnp.concatenate(groups, axis=0)


def factor_gram(gram, work, upper, inverse):
    order = gram.shape[0]
    row = lax.broadcasted_iota(jnp.int32, (order, order), 0)
    col = lax.broadcasted_iota(jnp.int32, (order, order), 1)
    work[:, :order] = gram[...]
    work[:, order:] = (row == col).astype(jnp.float32)
    lane = lax.broadcasted_iota(jnp.int32, (PANEL, 2 * PANEL), 1)
    prow = lax.broadcasted_iota(jnp.int32, (PANEL, 2 * PANEL), 0)

    @pl.loop(0, order // PANEL)
    def _(p):
        base = pl.multiple_of(p * PANEL, PANEL)
        tile = work[pl.ds(base, PANEL), pl.ds(pl.multiple_of((p // 2) * 2 * PANEL, 2 * PANEL), 2 * PANEL)]
        tile = jnp.where(p % 2 == 1, pltpu.roll(tile, PANEL, 1), tile)
        x = jnp.where(lane < PANEL, tile, (lane - PANEL == prow).astype(jnp.float32))
        x = eliminate(x)
        diag = jnp.sum(jnp.where(lane == prow, x, 0.0), axis=1, keepdims=True)
        left = pltpu.roll(x, PANEL, 1)[:, :PANEL]
        panel = dot_nn(left, work[pl.ds(base, PANEL), :])
        root = 1.0 / jnp.sqrt(diag)
        pcol = lax.broadcasted_iota(jnp.int32, (PANEL, order), 1)
        pr = lax.broadcasted_iota(jnp.int32, (PANEL, order), 0) + base
        upper[pl.ds(base, PANEL), :] = jnp.where(pcol >= pr, panel[:, :order] * root, 0.0)
        inverse[pl.ds(base, PANEL), :] = jnp.where(pcol <= pr, panel[:, order:] * root, 0.0)

        @pl.when(p < order // PANEL - 1)
        def _():
            half = panel * root
            update = dot_tn(half[:, :order], half)
            below = lax.broadcasted_iota(jnp.int32, (order, 1), 0) >= base + PANEL
            work[...] = jnp.where(below, work[...] - update, work[...])


def factor_kernel(scale, gram, upper_out, factor, inverse, again, work):
    factor_gram(gram, work, upper_out, inverse)
    factor[...] = upper_out[...] * (1.0 / scale)
    order = gram.shape[0]
    row = lax.broadcasted_iota(jnp.int32, (order, order), 0)
    col = lax.broadcasted_iota(jnp.int32, (order, order), 1)
    diag = jnp.sum(jnp.where(row == col, gram[...], 0.0), axis=0, keepdims=True)
    spread = jnp.sum(inverse[...] * inverse[...], axis=0, keepdims=True) * diag
    mean = jnp.sum(spread) * (1.0 / order)
    again[0] = jnp.where(mean <= INFLATION, 0, 1)


def factor_first(gram, scale):
    order = gram.shape[0]
    square = jax.ShapeDtypeStruct((order, order), jnp.float32)
    return pl.pallas_call(
        functools.partial(factor_kernel, scale),
        out_shape=(square, square, square, jax.ShapeDtypeStruct((1,), jnp.int32)),
        in_specs=[VMEM],
        out_specs=(VMEM, VMEM, VMEM, SMEM),
        scratch_shapes=[pltpu.VMEM((order, 2 * order), jnp.float32)],
        compiler_params=pltpu.CompilerParams(vmem_limit_bytes=16 << 20),
    )(gram)


def apply_kernel(scale, inverse, sketch, basis):
    step = 256

    @pl.loop(0, sketch.shape[0] // step)
    def _(i):
        part = pl.ds(pl.multiple_of(i * step, step), step)
        basis[part, :] = dot_nt(sketch[part, :], inverse[...]) * scale


def apply_inverse(inverse, sketch, scale):
    return pl.pallas_call(
        functools.partial(apply_kernel, scale),
        out_shape=jax.ShapeDtypeStruct(sketch.shape, jnp.float32),
        in_specs=[VMEM, VMEM],
        out_specs=VMEM,
        compiler_params=pltpu.CompilerParams(vmem_limit_bytes=16 << 20),
    )(inverse, sketch)


def once_kernel(inverse, sketch, once, second):
    second[...] = jnp.zeros_like(second)
    step = 256

    @pl.loop(0, sketch.shape[0] // step)
    def _(i):
        part = pl.ds(pl.multiple_of(i * step, step), step)
        rows = dot_nt(sketch[part, :], inverse[...])
        once[part, :] = rows
        second[...] += dot_tn(rows, rows)


def once_pass(inverse, sketch):
    return pl.pallas_call(
        once_kernel,
        out_shape=(
            jax.ShapeDtypeStruct(sketch.shape, jnp.float32),
            jax.ShapeDtypeStruct(inverse.shape, jnp.float32),
        ),
        in_specs=[VMEM, VMEM],
        out_specs=(VMEM, VMEM),
        compiler_params=pltpu.CompilerParams(vmem_limit_bytes=16 << 20),
    )(inverse, sketch)


def last_kernel(scale, gram, once, upper_one, basis, factor, work, upper, inverse):
    factor_gram(gram, work, upper, inverse)
    factor[...] = dot_nn(upper[...], upper_one[...]) * (1.0 / scale)
    step = 256

    @pl.loop(0, once.shape[0] // step)
    def _(i):
        part = pl.ds(pl.multiple_of(i * step, step), step)
        basis[part, :] = dot_nt(once[part, :], inverse[...]) * scale


def last_pass(gram, once, upper_one, scale):
    order = gram.shape[0]
    square = pltpu.VMEM((order, order), jnp.float32)
    return pl.pallas_call(
        functools.partial(last_kernel, scale),
        out_shape=(
            jax.ShapeDtypeStruct(once.shape, jnp.float32),
            jax.ShapeDtypeStruct((order, order), jnp.float32),
        ),
        in_specs=[VMEM, VMEM, VMEM],
        out_specs=(VMEM, VMEM),
        scratch_shapes=[pltpu.VMEM((order, 2 * order), jnp.float32), square, square],
        compiler_params=pltpu.CompilerParams(vmem_limit_bytes=16 << 20),
    )(gram, once, upper_one)


def body(nr, nc, a_blocks, omega, route_dest, row_target, col_target):
    order = a_blocks.shape[2]
    sketch, gram_one = make_sketch(
        route_dest.T, row_target.reshape(1, -1), col_target.T, a_blocks, omega.reshape(-1, order, omega.shape[1]), nr, nc)
    scale = float(nr * nc * RB_DEV * order) ** 0.5
    upper, factor, inverse, again = factor_first(gram_one, scale)

    def orthogonalize_again():
        once, gram_part = once_pass(inverse, sketch)
        return last_pass(gram_sum(gram_part, nr, nc), once, upper, scale)

    def keep_once():
        return apply_inverse(inverse, sketch, scale), factor

    return lax.cond(again[0] != 0, orthogonalize_again, keep_once)


def solution(mesh):
    nr, nc = mesh.shape["row"], mesh.shape["col"]
    return jax.shard_map(
        functools.partial(body, nr, nc),
        mesh=mesh,
        in_specs=(
            P(("row", "col"), None, None, None),
            P("col", None),
            P(("row", "col"), None),
            P(("row", "col")),
            P(("row", "col"), None),
        ),
        out_specs=(P(("row", "col"), None), P()),
        check_vma=False,
    )
```

```python
import functools

import jax
import jax.numpy as jnp
from jax import lax
from jax.experimental import pallas as pl
from jax.experimental.pallas import tpu as pltpu
from jax.sharding import PartitionSpec as P

RB_DEV = 8
CAP = 4
PANEL = 64
LOADS = 8
NOWHERE = 1 << 20
INFLATION = 2.0
CHUNKS = 8
WINDOW = 2
TERMS = 4
WIDE = 4
MESH = pl.DeviceIdType.MESH
VMEM = pl.BlockSpec(memory_space=pltpu.VMEM)
SMEM = pl.BlockSpec(memory_space=pltpu.SMEM)
HIGH = lax.Precision.HIGHEST


def dot_nn(a, b):
    return lax.dot_general(a, b, (((1,), (0,)), ((), ())), precision=HIGH, preferred_element_type=jnp.float32)


def dot_nt(a, b):
    return lax.dot_general(a, b, (((1,), (1,)), ((), ())), precision=HIGH, preferred_element_type=jnp.float32)


def dot_tn(a, b):
    return lax.dot_general(a, b, (((0,), (0,)), ((), ())), precision=HIGH, preferred_element_type=jnp.float32)


def place(dest, target, owners):
    count = dest.shape[1]
    i = lax.broadcasted_iota(jnp.int32, (count, count), 0)
    j = lax.broadcasted_iota(jnp.int32, (count, count), 1)
    down = jnp.sum(jnp.where(i == j, dest, 0), axis=1, keepdims=True)
    rank = jnp.sum(jnp.logical_and(down == dest, j < i).astype(jnp.int32), axis=1, keepdims=True)
    rank_across = jnp.sum(jnp.where(i == j, rank, 0), axis=0, keepdims=True)
    lane = lax.broadcasted_iota(jnp.int32, (count, 128), 1)
    which = lax.broadcasted_iota(jnp.int32, (count, 128), 0)
    source = jnp.sum(jnp.where(down * CAP + rank == lane, which, 0), axis=0, keepdims=True)
    place_of = lax.broadcasted_iota(jnp.int32, (owners * 8, count), 0)
    here = place_of == dest * 8 + rank_across
    rows = jnp.sum(jnp.where(here, target + 1, 0), axis=1, keepdims=True)
    rows = jnp.where(rows > 0, rows - 1, NOWHERE)
    return source, jnp.broadcast_to(rows, (owners * 8, 128))


def signal_all(nr, nc, r, c):
    barrier = pltpu.get_barrier_semaphore()
    for k in range(1, nr):
        pl.semaphore_signal(barrier, inc=1, device_id=(lax.rem(r + k, nr), c), device_id_type=MESH)
    for k in range(1, nc):
        pl.semaphore_signal(barrier, inc=1, device_id=(r, lax.rem(c + k, nc)), device_id_type=MESH)


def wait_all(nr, nc):
    pl.semaphore_wait(pltpu.get_barrier_semaphore(), nr - 1 + nc - 1)


def greet(nr, nc, r, c):
    signal_all(nr, nc, r, c)
    wait_all(nr, nc)


def reduce_packed(nr, nc, r, c, gram, landed, cols, full, sems):
    a_s, a_r, b_s, b_r, c_s, c_r = sems
    chunk = gram.shape[0] // nr
    mine = pl.ds(pl.multiple_of(r * chunk, chunk), chunk)
    copies = []
    for k in range(1, nr):
        d = lax.rem(r + k, nr)
        cp = pltpu.make_async_remote_copy(
            gram.at[pl.ds(pl.multiple_of(d * chunk, chunk), chunk), :], landed.at[k], a_s.at[k], a_r.at[k],
            device_id=(d, c), device_id_type=MESH)
        cp.start()
        copies.append(cp)
    total = gram[mine, :]
    for k in range(1, nr):
        copies[k - 1].wait_recv()
        total = total + landed[k]
    cols[c] = total
    across = []
    for k in range(1, nc):
        cp = pltpu.make_async_remote_copy(
            cols.at[c], cols.at[c], b_s.at[k], b_r.at[k], device_id=(r, lax.rem(c + k, nc)), device_id_type=MESH)
        cp.start()
        across.append(cp)
    for cp in across:
        cp.wait_recv()
    total = cols[0]
    for k in range(1, nc):
        total = total + cols[k]
    full[mine, :] = total
    back = []
    for k in range(1, nr):
        cp = pltpu.make_async_remote_copy(
            full.at[mine, :], full.at[mine, :], c_s.at[k], c_r.at[k], device_id=(lax.rem(r + k, nr), c), device_id_type=MESH)
        cp.start()
        back.append(cp)
    for cp in back:
        cp.wait_recv()
    for cp in copies + across + back:
        cp.wait_send()


def packed_scratch(nr, nc, width):
    dma = pltpu.SemaphoreType.DMA
    half = width // 2
    chunk = 3 * half // nr
    return [
        pltpu.VMEM((3 * half, half), jnp.float32),
        pltpu.VMEM((nr, chunk, half), jnp.float32),
        pltpu.VMEM((nc, chunk, half), jnp.float32),
        pltpu.VMEM((3 * half, half), jnp.float32),
        dma((nr,)), dma((nr,)), dma((nc,)), dma((nc,)), dma((nr,)), dma((nr,)),
    ]


def sum_gram(nr, nc, r, c, gram, out_ref, packed, landed, cols, full, sems):
    half = gram.shape[0] // 2
    packed[:half, :] = gram[:half, :half]
    packed[half:2 * half, :] = gram[:half, half:]
    packed[2 * half:, :] = gram[half:, half:]
    reduce_packed(nr, nc, r, c, packed, landed, cols, full, sems)
    out_ref[:half, :half] = full[:half, :]
    side = full[half:2 * half, :]
    out_ref[:half, half:] = side
    out_ref[half:, :half] = side.T
    out_ref[half:, half:] = full[2 * half:, :]


def arrange(rows, slots):
    count = rows.shape[0]
    i = lax.broadcasted_iota(jnp.int32, rows.shape, 0)
    j = lax.broadcasted_iota(jnp.int32, rows.shape, 1)
    across = jnp.sum(jnp.where(i == j, rows, 0), axis=0, keepdims=True)
    ahead = jnp.logical_or(across < rows, jnp.logical_and(across == rows, j < i))
    ahead = jnp.logical_and(ahead, j < count)
    rank = jnp.sum(ahead.astype(jnp.int32), axis=1, keepdims=True)
    slot = (i // 8) * CAP + lax.rem(i, 8)
    order = jnp.sum(jnp.where(rank == j, slot, 0), axis=0, keepdims=True)
    here = jnp.sum(jnp.where(rank == j, rows, 0), axis=0, keepdims=True)
    before = jnp.sum(jnp.where(rank == j - 1, rows, 0), axis=0, keepdims=True)
    keep = jnp.logical_and(here == before, j[:1] > 0).astype(jnp.int32)
    last = jnp.max(jnp.where(rows == j, rank, -1), axis=0, keepdims=True)
    valid = (last >= 0).astype(jnp.int32)
    order = jnp.minimum(order, slots - 1)
    last = jnp.clip(last, 0, slots - 1)
    return jnp.concatenate([order, keep, last, valid], axis=0)


def sketch_kernel(nr, nc, dest_hbm, target_hbm, col_hbm, a_hbm, omega_hbm, sketch_ref, out_ref, *refs):
    chunks = CHUNKS
    gots, refs = refs[:chunks], refs[chunks:]
    (dest_ref, target_ref, col_ref, a_buf, omega_buf, parts, send_ref, row_ref, sources, a_sem, in_sem,
     rows_in, meta, table, prefix, term, to_right, to_left, total, gram, row_s, row_r, own_s,
     send_s, send_r, right_s, right_r, left_s, left_r), refs = refs[:29], refs[29:]
    targets, groups, order, _ = a_buf.shape
    rq, width = order // chunks, omega_buf.shape[2]
    slots = nr * CAP
    blocks = nc * RB_DEV
    loads = targets // LOADS
    r = lax.axis_index("row")
    c = lax.axis_index("col")

    def fetch(i):
        part = pl.ds(i * LOADS, LOADS)
        return pltpu.make_async_copy(a_hbm.at[part], a_buf.at[part], a_sem.at[i])

    def route(k):
        d = lax.rem(r + k, nr)
        return pltpu.make_async_remote_copy(
            row_ref.at[d], rows_in.at[r], row_s.at[k], row_r.at[k], device_id=(d, c), device_id_type=MESH)

    def swap(q, k):
        d = lax.rem(r + k, nr)
        return pltpu.make_async_remote_copy(
            send_ref.at[q, d], gots[q].at[pl.ds(r * CAP, CAP)], send_s.at[q, k], send_r.at[q, k],
            device_id=(d, c), device_id_type=MESH)

    def keep_own(q):
        return pltpu.make_async_copy(send_ref.at[q, r], gots[q].at[pl.ds(r * CAP, CAP)], own_s.at[q])

    def hop_right(q, d):
        return pltpu.make_async_remote_copy(
            to_right.at[q, d], to_right.at[q, d], right_s.at[q, d], right_r.at[q, d],
            device_id=(r, lax.rem(c + 1, nc)), device_id_type=MESH)

    def hop_left(q, d):
        return pltpu.make_async_remote_copy(
            to_left.at[q, d], to_left.at[q, d], left_s.at[q, d], left_r.at[q, d],
            device_id=(r, lax.rem(c + nc - 1, nc)), device_id_type=MESH)

    others = [pltpu.make_async_copy(src, dst, in_sem.at[i]) for i, (src, dst) in enumerate(
        ((dest_hbm, dest_ref), (target_hbm, target_ref), (col_hbm, col_ref), (omega_hbm, omega_buf)))]
    for copy in others:
        copy.start()
    for i in range(loads):
        fetch(i).start()
    signal_all(nr, nc, r, c)
    others[0].wait()
    others[1].wait()
    source, rows = place(dest_ref[...], target_ref[...], nr)
    row_ref[...] = rows.reshape(nr, 8, 128)
    meta[...] = jnp.zeros_like(meta)
    meta[:1, :] = source
    to_sources = pltpu.make_async_copy(meta, sources, own_s.at[chunks + 1])
    to_sources.start()
    own_rows = pltpu.make_async_copy(row_ref.at[r], rows_in.at[r], own_s.at[chunks])
    own_rows.start()
    gram[...] = jnp.zeros_like(gram)
    others[2].wait()
    others[3].wait()

    def multiply(i, carry):
        fetch(i).wait()
        for local in range(LOADS):
            t = i * LOADS + local
            sums = None
            for g in range(0, groups, 2):
                left = jnp.concatenate([a_buf[t, g], a_buf[t, g + 1]], axis=1)
                right = jnp.concatenate([omega_buf[col_ref[g, t]], omega_buf[col_ref[g + 1, t]]], axis=0)
                product = jnp.dot(left, right, preferred_element_type=jnp.float32)
                sums = product if sums is None else sums + product
            sums = sums.astype(jnp.bfloat16)
            for q in range(chunks):
                parts[q, t] = sums[q * rq:(q + 1) * rq]
        return carry

    lax.fori_loop(0, loads // 2, multiply, 0)
    wait_all(nr, nc)
    for k in range(1, nr):
        route(k).start()
    lax.fori_loop(loads // 2, loads, multiply, 0)
    own_rows.wait()
    to_sources.wait()
    for q in range(chunks):
        for d in range(nr):
            for k in range(CAP):
                send_ref[q, d, k] = parts[q, sources[0, d * CAP + k]]
        keep_own(q).start()
        if q == 0:
            for k in range(1, nr):
                swap(0, k).start()
    for k in range(1, nr):
        route(k).wait_recv()
    meta[:4, :] = arrange(rows_in[...].reshape(nr * 8, 128), slots)
    to_table = pltpu.make_async_copy(meta, table, own_s.at[chunks + 1])
    to_table.start()
    to_table.wait()

    def collect(q):
        keep_own(q).wait()
        for k in range(1, nr):
            swap(q, k).wait_send()
        if q + 1 < chunks:
            for k in range(1, nr):
                swap(q + 1, k).start()
        for k in range(1, nr):
            swap(q, k).wait_recv()
        got = gots[q]

        def add(k, acc):
            acc = acc * table[1, k].astype(jnp.float32) + got[table[0, k]].astype(jnp.float32)
            prefix[k] = acc
            return acc

        lax.fori_loop(0, slots, add, jnp.zeros((rq, width), jnp.float32), unroll=8)

        @pl.loop(0, blocks, unroll=8)
        def _(b):
            term[q % TERMS, b] = prefix[table[2, b]] * table[3, b].astype(jnp.float32)

        @pl.when(c == 0)
        def _():
            for d in range(nc - 1, 0, -1):
                n = q * (nc - 1) + nc - 1 - d - WINDOW
                if n >= 0:
                    hop_right(n // (nc - 1), nc - 1 - n % (nc - 1)).wait_send()
                to_right[q, d] = term[q % TERMS, d * RB_DEV:(d + 1) * RB_DEV].astype(jnp.bfloat16)
                hop_right(q, d).start()

        @pl.when(c == nc - 1)
        def _():
            for d in range(nc - 1):
                n = q * (nc - 1) + d - WINDOW
                if n >= 0:
                    hop_left(n // (nc - 1), n % (nc - 1)).wait_send()
                to_left[q, d] = term[q % TERMS, d * RB_DEV:(d + 1) * RB_DEV].astype(jnp.bfloat16)
                hop_left(q, d).start()

    def pass_on(q):
        for k in range(nc - 1, 0, -1):
            @pl.when(jnp.logical_and(c > 0, c + k < nc))
            def _():
                d = c + k
                hop_right(q, d).wait_recv()
                mine = term[q % TERMS, pl.ds(d * RB_DEV, RB_DEV)]
                to_right[q, d] = (to_right[q, d].astype(jnp.float32) + mine).astype(jnp.bfloat16)
                hop_right(q, d).start()

            @pl.when(jnp.logical_and(c < nc - 1, c - k >= 0))
            def _():
                d = c - k
                hop_left(q, d).wait_recv()
                mine = term[q % TERMS, pl.ds(d * RB_DEV, RB_DEV)]
                to_left[q, d] = (to_left[q, d].astype(jnp.float32) + mine).astype(jnp.bfloat16)
                hop_left(q, d).start()


    def finish(q):
        total[...] = term[q % TERMS, pl.ds(c * RB_DEV, RB_DEV)]

        @pl.when(c > 0)
        def _():
            hop_right(q, c).wait_recv()
            total[...] += to_right[q, c].astype(jnp.float32)

        @pl.when(c < nc - 1)
        def _():
            hop_left(q, c).wait_recv()
            total[...] += to_left[q, c].astype(jnp.float32)

        for b in range(RB_DEV):
            start = b * chunks * rq + q * rq
            sketch_ref[start:start + rq, :] = total[b]
        rows = total[...].reshape(RB_DEV * rq, width)
        gram[...] += dot_tn(rows, rows)

    for q in range(chunks + 2):
        if q < chunks:
            collect(q)
        if 1 <= q <= chunks:
            pass_on(q - 1)
        if q >= 2:
            finish(q - 2)
    sum_gram(nr, nc, r, c, gram, out_ref, *refs[:4], refs[4:])
    for k in range(1, nr):
        route(k).wait_send()

    @pl.when(c == 0)
    def _():
        for n in range(chunks * (nc - 1) - WINDOW, chunks * (nc - 1)):
            hop_right(n // (nc - 1), nc - 1 - n % (nc - 1)).wait_send()

    @pl.when(c == nc - 1)
    def _():
        for n in range(chunks * (nc - 1) - WINDOW, chunks * (nc - 1)):
            hop_left(n // (nc - 1), n % (nc - 1)).wait_send()

    for q in range(chunks):
        for k in range(1, nc):
            @pl.when(jnp.logical_and(c > 0, c + k < nc))
            def _():
                hop_right(q, c + k).wait_send()

            @pl.when(jnp.logical_and(c < nc - 1, c - k >= 0))
            def _():
                hop_left(q, c - k).wait_send()


def make_sketch(dest, target, col_target, a_blocks, omega, nr, nc):
    targets, _, order, _ = a_blocks.shape
    width = omega.shape[2]
    chunks, rq = CHUNKS, order // CHUNKS
    dma = pltpu.SemaphoreType.DMA
    slots, blocks = nr * CAP, nc * RB_DEV
    hops = pltpu.VMEM((chunks, nc, RB_DEV, rq, width), jnp.bfloat16)
    hbm = pl.BlockSpec(memory_space=pltpu.HBM)
    return pl.pallas_call(
        functools.partial(sketch_kernel, nr, nc),
        out_shape=(
            jax.ShapeDtypeStruct((RB_DEV * order, width), jnp.float32),
            jax.ShapeDtypeStruct((width, width), jnp.float32),
        ),
        in_specs=[hbm] * 5,
        out_specs=(VMEM, VMEM),
        scratch_shapes=[pltpu.VMEM((slots, rq, width), jnp.bfloat16)] * chunks + [
            pltpu.VMEM(dest.shape, jnp.int32),
            pltpu.VMEM(target.shape, jnp.int32),
            pltpu.SMEM(col_target.shape, jnp.int32),
            pltpu.VMEM(a_blocks.shape, a_blocks.dtype),
            pltpu.VMEM(omega.shape, omega.dtype),
            pltpu.VMEM((chunks, targets, rq, width), jnp.bfloat16),
            pltpu.VMEM((chunks, nr, CAP, rq, width), jnp.bfloat16),
            pltpu.VMEM((nr, 8, 128), jnp.int32),
            pltpu.SMEM((8, 128), jnp.int32),
            dma((targets // LOADS,)), dma((4,)),
            pltpu.VMEM((nr, 8, 128), jnp.int32),
            pltpu.VMEM((8, 128), jnp.int32),
            pltpu.SMEM((8, 128), jnp.int32),
            pltpu.VMEM((slots, rq, width), jnp.float32),
            pltpu.VMEM((TERMS, blocks, rq, width), jnp.float32),
            hops, hops,
            pltpu.VMEM((RB_DEV, rq, width), jnp.float32),
            pltpu.VMEM((width, width), jnp.float32),
            dma((nr,)), dma((nr,)), dma((chunks + 2,)),
            dma((chunks, nr)), dma((chunks, nr)),
            dma((chunks, nc)), dma((chunks, nc)), dma((chunks, nc)), dma((chunks, nc)),
        ] + packed_scratch(nr, nc, width),
        compiler_params=pltpu.CompilerParams(collective_id=1, has_side_effects=True, vmem_limit_bytes=60 << 20),
    )(dest, target, col_target, a_blocks, omega)


def gram_sum_kernel(nr, nc, gram, out_ref, packed, landed, cols, full, *sems):
    r = lax.axis_index("row")
    c = lax.axis_index("col")
    greet(nr, nc, r, c)
    sum_gram(nr, nc, r, c, gram, out_ref, packed, landed, cols, full, sems)


def gram_sum(gram, nr, nc):
    return pl.pallas_call(
        functools.partial(gram_sum_kernel, nr, nc),
        out_shape=jax.ShapeDtypeStruct(gram.shape, jnp.float32),
        in_specs=[VMEM],
        out_specs=VMEM,
        scratch_shapes=packed_scratch(nr, nc, gram.shape[0]),
        compiler_params=pltpu.CompilerParams(collective_id=3, has_side_effects=True, vmem_limit_bytes=8 << 20),
    )(gram)


def eliminate(x):
    rows = x.shape[0]
    shape = (8, x.shape[1])
    groups = [x[i:i + 8, :] for i in range(0, rows, 8)]
    sub = lax.broadcasted_iota(jnp.int32, shape, 0)
    for j in range(0, rows, WIDE):
        g, o = divmod(j, 8)
        cols = [[jnp.broadcast_to(groups[i][:, j + l:j + l + 1], shape) for l in range(WIDE)]
                for i in range(g, rows // 8)]
        piv = [[jnp.broadcast_to(cols[0][l][o + k:o + k + 1, :], shape) for l in range(WIDE)] for k in range(WIDE)]
        tops = [jnp.broadcast_to(groups[g][o + k:o + k + 1, :], shape) for k in range(WIDE)]
        recip = []
        for k in range(WIDE):
            recip.append(1.0 / piv[k][k])
            for m in range(k + 1, WIDE):
                q = piv[m][k] * recip[k]
                for l in range(k + 1, WIDE):
                    piv[m][l] = piv[m][l] - q * piv[k][l]
                tops[m] = tops[m] - q * tops[k]
        for i in range(g, rows // 8):
            here = cols[i - g]
            value = groups[i]
            for k in range(WIDE):
                f = here[k] * recip[k]
                for l in range(k + 1, WIDE):
                    here[l] = here[l] - f * piv[k][l]
                value = value - f * tops[k]
            if i == g:
                value = jnp.where(sub >= o + WIDE, value, groups[i])
                for k in range(1, WIDE):
                    value = jnp.where(sub == o + k, tops[k], value)
            groups[i] = value
    return jnp.concatenate(groups, axis=0)


def factor_gram(gram, work, upper, inverse):
    order = gram.shape[0]
    row = lax.broadcasted_iota(jnp.int32, (order, order), 0)
    col = lax.broadcasted_iota(jnp.int32, (order, order), 1)
    work[:, :order] = gram[...]
    work[:, order:] = (row == col).astype(jnp.float32)
    lane = lax.broadcasted_iota(jnp.int32, (PANEL, 2 * PANEL), 1)
    prow = lax.broadcasted_iota(jnp.int32, (PANEL, 2 * PANEL), 0)

    @pl.loop(0, order // PANEL)
    def _(p):
        base = pl.multiple_of(p * PANEL, PANEL)
        tile = work[pl.ds(base, PANEL), pl.ds(pl.multiple_of((p // 2) * 2 * PANEL, 2 * PANEL), 2 * PANEL)]
        tile = jnp.where(p % 2 == 1, pltpu.roll(tile, PANEL, 1), tile)
        x = jnp.where(lane < PANEL, tile, (lane - PANEL == prow).astype(jnp.float32))
        x = eliminate(x)
        diag = jnp.sum(jnp.where(lane == prow, x, 0.0), axis=1, keepdims=True)
        left = pltpu.roll(x, PANEL, 1)[:, :PANEL]
        panel = dot_nn(left, work[pl.ds(base, PANEL), :])
        root = 1.0 / jnp.sqrt(diag)
        pcol = lax.broadcasted_iota(jnp.int32, (PANEL, order), 1)
        pr = lax.broadcasted_iota(jnp.int32, (PANEL, order), 0) + base
        upper[pl.ds(base, PANEL), :] = jnp.where(pcol >= pr, panel[:, :order] * root, 0.0)
        inverse[pl.ds(base, PANEL), :] = jnp.where(pcol <= pr, panel[:, order:] * root, 0.0)

        @pl.when(p < order // PANEL - 1)
        def _():
            half = panel * root
            update = dot_tn(half[:, :order], half)
            below = lax.broadcasted_iota(jnp.int32, (order, 1), 0) >= base + PANEL
            work[...] = jnp.where(below, work[...] - update, work[...])


def factor_kernel(scale, gram, upper_out, factor, inverse, again, work):
    factor_gram(gram, work, upper_out, inverse)
    factor[...] = upper_out[...] * (1.0 / scale)
    order = gram.shape[0]
    row = lax.broadcasted_iota(jnp.int32, (order, order), 0)
    col = lax.broadcasted_iota(jnp.int32, (order, order), 1)
    diag = jnp.sum(jnp.where(row == col, gram[...], 0.0), axis=0, keepdims=True)
    spread = jnp.sum(inverse[...] * inverse[...], axis=0, keepdims=True) * diag
    mean = jnp.sum(spread) * (1.0 / order)
    again[0] = jnp.where(mean <= INFLATION, 0, 1)


def factor_first(gram, scale):
    order = gram.shape[0]
    square = jax.ShapeDtypeStruct((order, order), jnp.float32)
    return pl.pallas_call(
        functools.partial(factor_kernel, scale),
        out_shape=(square, square, square, jax.ShapeDtypeStruct((1,), jnp.int32)),
        in_specs=[VMEM],
        out_specs=(VMEM, VMEM, VMEM, SMEM),
        scratch_shapes=[pltpu.VMEM((order, 2 * order), jnp.float32)],
        compiler_params=pltpu.CompilerParams(vmem_limit_bytes=16 << 20),
    )(gram)


def apply_kernel(scale, inverse, sketch, basis):
    step = 256

    @pl.loop(0, sketch.shape[0] // step)
    def _(i):
        part = pl.ds(pl.multiple_of(i * step, step), step)
        basis[part, :] = dot_nt(sketch[part, :], inverse[...]) * scale


def apply_inverse(inverse, sketch, scale):
    return pl.pallas_call(
        functools.partial(apply_kernel, scale),
        out_shape=jax.ShapeDtypeStruct(sketch.shape, jnp.float32),
        in_specs=[VMEM, VMEM],
        out_specs=VMEM,
        compiler_params=pltpu.CompilerParams(vmem_limit_bytes=16 << 20),
    )(inverse, sketch)


def once_kernel(inverse, sketch, once, second):
    second[...] = jnp.zeros_like(second)
    step = 256

    @pl.loop(0, sketch.shape[0] // step)
    def _(i):
        part = pl.ds(pl.multiple_of(i * step, step), step)
        rows = dot_nt(sketch[part, :], inverse[...])
        once[part, :] = rows
        second[...] += dot_tn(rows, rows)


def once_pass(inverse, sketch):
    return pl.pallas_call(
        once_kernel,
        out_shape=(
            jax.ShapeDtypeStruct(sketch.shape, jnp.float32),
            jax.ShapeDtypeStruct(inverse.shape, jnp.float32),
        ),
        in_specs=[VMEM, VMEM],
        out_specs=(VMEM, VMEM),
        compiler_params=pltpu.CompilerParams(vmem_limit_bytes=16 << 20),
    )(inverse, sketch)


def last_kernel(scale, gram, once, upper_one, basis, factor, work, upper, inverse):
    factor_gram(gram, work, upper, inverse)
    factor[...] = dot_nn(upper[...], upper_one[...]) * (1.0 / scale)
    step = 256

    @pl.loop(0, once.shape[0] // step)
    def _(i):
        part = pl.ds(pl.multiple_of(i * step, step), step)
        basis[part, :] = dot_nt(once[part, :], inverse[...]) * scale


def last_pass(gram, once, upper_one, scale):
    order = gram.shape[0]
    square = pltpu.VMEM((order, order), jnp.float32)
    return pl.pallas_call(
        functools.partial(last_kernel, scale),
        out_shape=(
            jax.ShapeDtypeStruct(once.shape, jnp.float32),
            jax.ShapeDtypeStruct((order, order), jnp.float32),
        ),
        in_specs=[VMEM, VMEM, VMEM],
        out_specs=(VMEM, VMEM),
        scratch_shapes=[pltpu.VMEM((order, 2 * order), jnp.float32), square, square],
        compiler_params=pltpu.CompilerParams(vmem_limit_bytes=16 << 20),
    )(gram, once, upper_one)


def body(nr, nc, a_blocks, omega, route_dest, row_target, col_target):
    order = a_blocks.shape[2]
    sketch, gram_one = make_sketch(
        route_dest.T, row_target.reshape(1, -1), col_target.T, a_blocks, omega.reshape(-1, order, omega.shape[1]), nr, nc)
    scale = float(nr * nc * RB_DEV * order) ** 0.5
    upper, factor, inverse, again = factor_first(gram_one, scale)

    def orthogonalize_again():
        once, gram_part = once_pass(inverse, sketch)
        return last_pass(gram_sum(gram_part, nr, nc), once, upper, scale)

    def keep_once():
        return apply_inverse(inverse, sketch, scale), factor

    return lax.cond(again[0] != 0, orthogonalize_again, keep_once)


def solution(mesh):
    nr, nc = mesh.shape["row"], mesh.shape["col"]
    return jax.shard_map(
        functools.partial(body, nr, nc),
        mesh=mesh,
        in_specs=(
            P(("row", "col"), None, None, None),
            P("col", None),
            P(("row", "col"), None),
            P(("row", "col")),
            P(("row", "col"), None),
        ),
        out_specs=(P(("row", "col"), None), P()),
        check_vma=False,
    )
```

```python
import functools

import jax
import jax.numpy as jnp
from jax import lax
from jax.experimental import pallas as pl
from jax.experimental.pallas import tpu as pltpu
from jax.sharding import PartitionSpec as P

RB_DEV = 8
CAP = 4
PANEL = 64
LOADS = 8
NOWHERE = 1 << 20
INFLATION = 2.0
CHUNKS = 8
WINDOW = 2
TERMS = 4
MESH = pl.DeviceIdType.MESH
VMEM = pl.BlockSpec(memory_space=pltpu.VMEM)
SMEM = pl.BlockSpec(memory_space=pltpu.SMEM)
HIGH = lax.Precision.HIGHEST


def dot_nn(a, b):
    return lax.dot_general(a, b, (((1,), (0,)), ((), ())), precision=HIGH, preferred_element_type=jnp.float32)


def dot_nt(a, b):
    return lax.dot_general(a, b, (((1,), (1,)), ((), ())), precision=HIGH, preferred_element_type=jnp.float32)


def dot_tn(a, b):
    return lax.dot_general(a, b, (((0,), (0,)), ((), ())), precision=HIGH, preferred_element_type=jnp.float32)


def place(dest, target, owners):
    count = dest.shape[1]
    i = lax.broadcasted_iota(jnp.int32, (count, count), 0)
    j = lax.broadcasted_iota(jnp.int32, (count, count), 1)
    down = jnp.sum(jnp.where(i == j, dest, 0), axis=1, keepdims=True)
    rank = jnp.sum(jnp.logical_and(down == dest, j < i).astype(jnp.int32), axis=1, keepdims=True)
    rank_across = jnp.sum(jnp.where(i == j, rank, 0), axis=0, keepdims=True)
    lane = lax.broadcasted_iota(jnp.int32, (count, 128), 1)
    which = lax.broadcasted_iota(jnp.int32, (count, 128), 0)
    source = jnp.sum(jnp.where(down * CAP + rank == lane, which, 0), axis=0, keepdims=True)
    place_of = lax.broadcasted_iota(jnp.int32, (owners * 8, count), 0)
    here = place_of == dest * 8 + rank_across
    rows = jnp.sum(jnp.where(here, target + 1, 0), axis=1, keepdims=True)
    rows = jnp.where(rows > 0, rows - 1, NOWHERE)
    return source, jnp.broadcast_to(rows, (owners * 8, 128))


def signal_all(nr, nc, r, c):
    barrier = pltpu.get_barrier_semaphore()
    for k in range(1, nr):
        pl.semaphore_signal(barrier, inc=1, device_id=(lax.rem(r + k, nr), c), device_id_type=MESH)
    for k in range(1, nc):
        pl.semaphore_signal(barrier, inc=1, device_id=(r, lax.rem(c + k, nc)), device_id_type=MESH)


def wait_all(nr, nc):
    pl.semaphore_wait(pltpu.get_barrier_semaphore(), nr - 1 + nc - 1)


def greet(nr, nc, r, c):
    signal_all(nr, nc, r, c)
    wait_all(nr, nc)


def reduce_packed(nr, nc, r, c, gram, landed, cols, full, sems):
    a_s, a_r, b_s, b_r, c_s, c_r = sems
    chunk = gram.shape[0] // nr
    mine = pl.ds(pl.multiple_of(r * chunk, chunk), chunk)
    copies = []
    for k in range(1, nr):
        d = lax.rem(r + k, nr)
        cp = pltpu.make_async_remote_copy(
            gram.at[pl.ds(pl.multiple_of(d * chunk, chunk), chunk), :], landed.at[k], a_s.at[k], a_r.at[k],
            device_id=(d, c), device_id_type=MESH)
        cp.start()
        copies.append(cp)
    total = gram[mine, :]
    for k in range(1, nr):
        copies[k - 1].wait_recv()
        total = total + landed[k]
    cols[c] = total
    across = []
    for k in range(1, nc):
        cp = pltpu.make_async_remote_copy(
            cols.at[c], cols.at[c], b_s.at[k], b_r.at[k], device_id=(r, lax.rem(c + k, nc)), device_id_type=MESH)
        cp.start()
        across.append(cp)
    for cp in across:
        cp.wait_recv()
    total = cols[0]
    for k in range(1, nc):
        total = total + cols[k]
    full[mine, :] = total
    back = []
    for k in range(1, nr):
        cp = pltpu.make_async_remote_copy(
            full.at[mine, :], full.at[mine, :], c_s.at[k], c_r.at[k], device_id=(lax.rem(r + k, nr), c), device_id_type=MESH)
        cp.start()
        back.append(cp)
    for cp in back:
        cp.wait_recv()
    for cp in copies + across + back:
        cp.wait_send()


def packed_scratch(nr, nc, width):
    dma = pltpu.SemaphoreType.DMA
    half = width // 2
    chunk = 3 * half // nr
    return [
        pltpu.VMEM((3 * half, half), jnp.float32),
        pltpu.VMEM((nr, chunk, half), jnp.float32),
        pltpu.VMEM((nc, chunk, half), jnp.float32),
        pltpu.VMEM((3 * half, half), jnp.float32),
        dma((nr,)), dma((nr,)), dma((nc,)), dma((nc,)), dma((nr,)), dma((nr,)),
    ]


def sum_gram(nr, nc, r, c, gram, out_ref, packed, landed, cols, full, *sems):
    half = gram.shape[0] // 2
    packed[:half, :] = gram[:half, :half]
    packed[half:2 * half, :] = gram[:half, half:]
    packed[2 * half:, :] = gram[half:, half:]
    reduce_packed(nr, nc, r, c, packed, landed, cols, full, sems)
    whole = full[...]
    out_ref[:half, :half] = whole[:half]
    side = whole[half:2 * half]
    out_ref[:half, half:] = side
    out_ref[half:, :half] = side.T
    out_ref[half:, half:] = whole[2 * half:]


def arrange(rows, slots):
    count = rows.shape[0]
    i = lax.broadcasted_iota(jnp.int32, rows.shape, 0)
    j = lax.broadcasted_iota(jnp.int32, rows.shape, 1)
    across = jnp.sum(jnp.where(i == j, rows, 0), axis=0, keepdims=True)
    ahead = jnp.logical_or(across < rows, jnp.logical_and(across == rows, j < i))
    ahead = jnp.logical_and(ahead, j < count)
    rank = jnp.sum(ahead.astype(jnp.int32), axis=1, keepdims=True)
    slot = (i // 8) * CAP + lax.rem(i, 8)
    order = jnp.sum(jnp.where(rank == j, slot, 0), axis=0, keepdims=True)
    here = jnp.sum(jnp.where(rank == j, rows, 0), axis=0, keepdims=True)
    before = jnp.sum(jnp.where(rank == j - 1, rows, 0), axis=0, keepdims=True)
    keep = jnp.logical_and(here == before, j[:1] > 0).astype(jnp.int32)
    last = jnp.max(jnp.where(rows == j, rank, -1), axis=0, keepdims=True)
    valid = (last >= 0).astype(jnp.int32)
    order = jnp.minimum(order, slots - 1)
    last = jnp.clip(last, 0, slots - 1)
    return jnp.concatenate([order, keep, last, valid], axis=0)


def sketch_kernel(nr, nc, dest_hbm, target_hbm, col_hbm, a_hbm, omega_hbm, sketch_ref, *refs):
    chunks = CHUNKS
    gots, refs = refs[:chunks], refs[chunks:]
    (dest_ref, target_ref, col_ref, a_buf, omega_buf, parts, send_ref, row_ref, sources, a_sem, in_sem,
     rows_in, meta, table, prefix, term, to_right, to_left, total, gram, row_s, row_r, own_s,
     send_s, send_r, right_s, right_r, left_s, left_r), refs = refs[:29], refs[29:]
    targets, groups, order, _ = a_buf.shape
    rq, width = order // chunks, omega_buf.shape[2]
    slots = nr * CAP
    blocks = nc * RB_DEV
    loads = targets // LOADS
    r = lax.axis_index("row")
    c = lax.axis_index("col")

    def fetch(i):
        part = pl.ds(i * LOADS, LOADS)
        return pltpu.make_async_copy(a_hbm.at[part], a_buf.at[part], a_sem.at[i])

    def route(k):
        d = lax.rem(r + k, nr)
        return pltpu.make_async_remote_copy(
            row_ref.at[d], rows_in.at[r], row_s.at[k], row_r.at[k], device_id=(d, c), device_id_type=MESH)

    def swap(q, k):
        d = lax.rem(r + k, nr)
        return pltpu.make_async_remote_copy(
            send_ref.at[q, d], gots[q].at[pl.ds(r * CAP, CAP)], send_s.at[q, k], send_r.at[q, k],
            device_id=(d, c), device_id_type=MESH)

    def keep_own(q):
        return pltpu.make_async_copy(send_ref.at[q, r], gots[q].at[pl.ds(r * CAP, CAP)], own_s.at[q])

    def hop_right(q, d):
        return pltpu.make_async_remote_copy(
            to_right.at[q, d], to_right.at[q, d], right_s.at[q, d], right_r.at[q, d],
            device_id=(r, lax.rem(c + 1, nc)), device_id_type=MESH)

    def hop_left(q, d):
        return pltpu.make_async_remote_copy(
            to_left.at[q, d], to_left.at[q, d], left_s.at[q, d], left_r.at[q, d],
            device_id=(r, lax.rem(c + nc - 1, nc)), device_id_type=MESH)

    others = [pltpu.make_async_copy(src, dst, in_sem.at[i]) for i, (src, dst) in enumerate(
        ((dest_hbm, dest_ref), (target_hbm, target_ref), (col_hbm, col_ref), (omega_hbm, omega_buf)))]
    for copy in others:
        copy.start()
    for i in range(loads):
        fetch(i).start()
    signal_all(nr, nc, r, c)
    others[0].wait()
    others[1].wait()
    source, rows = place(dest_ref[...], target_ref[...], nr)
    row_ref[...] = rows.reshape(nr, 8, 128)
    meta[...] = jnp.zeros_like(meta)
    meta[:1, :] = source
    to_sources = pltpu.make_async_copy(meta, sources, own_s.at[chunks + 1])
    to_sources.start()
    own_rows = pltpu.make_async_copy(row_ref.at[r], rows_in.at[r], own_s.at[chunks])
    own_rows.start()
    gram[...] = jnp.zeros_like(gram)
    others[2].wait()
    others[3].wait()

    def multiply(i, carry):
        fetch(i).wait()
        for local in range(LOADS):
            t = i * LOADS + local
            sums = None
            for g in range(0, groups, 2):
                left = jnp.concatenate([a_buf[t, g], a_buf[t, g + 1]], axis=1)
                right = jnp.concatenate([omega_buf[col_ref[g, t]], omega_buf[col_ref[g + 1, t]]], axis=0)
                product = jnp.dot(left, right, preferred_element_type=jnp.float32)
                sums = product if sums is None else sums + product
            sums = sums.astype(jnp.bfloat16)
            for q in range(chunks):
                parts[q, t] = sums[q * rq:(q + 1) * rq]
        return carry

    lax.fori_loop(0, loads // 2, multiply, 0)
    wait_all(nr, nc)
    for k in range(1, nr):
        route(k).start()
    lax.fori_loop(loads // 2, loads, multiply, 0)
    own_rows.wait()
    to_sources.wait()
    for q in range(chunks):
        for d in range(nr):
            for k in range(CAP):
                send_ref[q, d, k] = parts[q, sources[0, d * CAP + k]]
        keep_own(q).start()
        if q == 0:
            for k in range(1, nr):
                swap(0, k).start()
    for k in range(1, nr):
        route(k).wait_recv()
    meta[:4, :] = arrange(rows_in[...].reshape(nr * 8, 128), slots)
    to_table = pltpu.make_async_copy(meta, table, own_s.at[chunks + 1])
    to_table.start()
    to_table.wait()

    def collect(q):
        keep_own(q).wait()
        for k in range(1, nr):
            swap(q, k).wait_send()
        if q + 1 < chunks:
            for k in range(1, nr):
                swap(q + 1, k).start()
        for k in range(1, nr):
            swap(q, k).wait_recv()
        got = gots[q]

        def add(k, acc):
            acc = acc * table[1, k].astype(jnp.float32) + got[table[0, k]].astype(jnp.float32)
            prefix[k] = acc
            return acc

        lax.fori_loop(0, slots, add, jnp.zeros((rq, width), jnp.float32), unroll=8)

        @pl.loop(0, blocks, unroll=8)
        def _(b):
            term[q % TERMS, b] = prefix[table[2, b]] * table[3, b].astype(jnp.float32)

        @pl.when(c == 0)
        def _():
            for d in range(nc - 1, 0, -1):
                n = q * (nc - 1) + nc - 1 - d - WINDOW
                if n >= 0:
                    hop_right(n // (nc - 1), nc - 1 - n % (nc - 1)).wait_send()
                to_right[q, d] = term[q % TERMS, d * RB_DEV:(d + 1) * RB_DEV].astype(jnp.bfloat16)
                hop_right(q, d).start()

        @pl.when(c == nc - 1)
        def _():
            for d in range(nc - 1):
                n = q * (nc - 1) + d - WINDOW
                if n >= 0:
                    hop_left(n // (nc - 1), n % (nc - 1)).wait_send()
                to_left[q, d] = term[q % TERMS, d * RB_DEV:(d + 1) * RB_DEV].astype(jnp.bfloat16)
                hop_left(q, d).start()

    def pass_on(q):
        for k in range(nc - 1, 0, -1):
            @pl.when(jnp.logical_and(c > 0, c + k < nc))
            def _():
                d = c + k
                hop_right(q, d).wait_recv()
                mine = term[q % TERMS, pl.ds(d * RB_DEV, RB_DEV)]
                to_right[q, d] = (to_right[q, d].astype(jnp.float32) + mine).astype(jnp.bfloat16)
                hop_right(q, d).start()

            @pl.when(jnp.logical_and(c < nc - 1, c - k >= 0))
            def _():
                d = c - k
                hop_left(q, d).wait_recv()
                mine = term[q % TERMS, pl.ds(d * RB_DEV, RB_DEV)]
                to_left[q, d] = (to_left[q, d].astype(jnp.float32) + mine).astype(jnp.bfloat16)
                hop_left(q, d).start()


    def finish(q):
        total[...] = term[q % TERMS, pl.ds(c * RB_DEV, RB_DEV)]

        @pl.when(c > 0)
        def _():
            hop_right(q, c).wait_recv()
            total[...] += to_right[q, c].astype(jnp.float32)

        @pl.when(c < nc - 1)
        def _():
            hop_left(q, c).wait_recv()
            total[...] += to_left[q, c].astype(jnp.float32)

        for b in range(RB_DEV):
            start = b * chunks * rq + q * rq
            sketch_ref[start:start + rq, :] = total[b]
        rows = total[...].reshape(RB_DEV * rq, width)
        gram[...] += dot_tn(rows, rows)

    for q in range(chunks + 2):
        if q < chunks:
            collect(q)
        if 1 <= q <= chunks:
            pass_on(q - 1)
        if q >= 2:
            finish(q - 2)
    sum_gram(nr, nc, r, c, gram, sketch_ref.at[pl.ds(RB_DEV * order, width)], *refs)
    for k in range(1, nr):
        route(k).wait_send()

    @pl.when(c == 0)
    def _():
        for n in range(chunks * (nc - 1) - WINDOW, chunks * (nc - 1)):
            hop_right(n // (nc - 1), nc - 1 - n % (nc - 1)).wait_send()

    @pl.when(c == nc - 1)
    def _():
        for n in range(chunks * (nc - 1) - WINDOW, chunks * (nc - 1)):
            hop_left(n // (nc - 1), n % (nc - 1)).wait_send()

    for q in range(chunks):
        for k in range(1, nc):
            @pl.when(jnp.logical_and(c > 0, c + k < nc))
            def _():
                hop_right(q, c + k).wait_send()

            @pl.when(jnp.logical_and(c < nc - 1, c - k >= 0))
            def _():
                hop_left(q, c - k).wait_send()


def make_sketch(dest, target, col_target, a_blocks, omega, nr, nc):
    targets, _, order, _ = a_blocks.shape
    width = omega.shape[2]
    chunks, rq = CHUNKS, order // CHUNKS
    dma = pltpu.SemaphoreType.DMA
    slots, blocks = nr * CAP, nc * RB_DEV
    hops = pltpu.VMEM((chunks, nc, RB_DEV, rq, width), jnp.bfloat16)
    hbm = pl.BlockSpec(memory_space=pltpu.HBM)
    return pl.pallas_call(
        functools.partial(sketch_kernel, nr, nc),
        out_shape=jax.ShapeDtypeStruct((RB_DEV * order + width, width), jnp.float32),
        in_specs=[hbm] * 5,
        out_specs=VMEM,
        scratch_shapes=[pltpu.VMEM((slots, rq, width), jnp.bfloat16)] * chunks + [
            pltpu.VMEM(dest.shape, jnp.int32),
            pltpu.VMEM(target.shape, jnp.int32),
            pltpu.SMEM(col_target.shape, jnp.int32),
            pltpu.VMEM(a_blocks.shape, a_blocks.dtype),
            pltpu.VMEM(omega.shape, omega.dtype),
            pltpu.VMEM((chunks, targets, rq, width), jnp.bfloat16),
            pltpu.VMEM((chunks, nr, CAP, rq, width), jnp.bfloat16),
            pltpu.VMEM((nr, 8, 128), jnp.int32),
            pltpu.SMEM((8, 128), jnp.int32),
            dma((targets // LOADS,)), dma((4,)),
            pltpu.VMEM((nr, 8, 128), jnp.int32),
            pltpu.VMEM((8, 128), jnp.int32),
            pltpu.SMEM((8, 128), jnp.int32),
            pltpu.VMEM((slots, rq, width), jnp.float32),
            pltpu.VMEM((TERMS, blocks, rq, width), jnp.float32),
            hops, hops,
            pltpu.VMEM((RB_DEV, rq, width), jnp.float32),
            pltpu.VMEM((width, width), jnp.float32),
            dma((nr,)), dma((nr,)), dma((chunks + 2,)),
            dma((chunks, nr)), dma((chunks, nr)),
            dma((chunks, nc)), dma((chunks, nc)), dma((chunks, nc)), dma((chunks, nc)),
        ] + packed_scratch(nr, nc, width),
        compiler_params=pltpu.CompilerParams(collective_id=1, has_side_effects=True, vmem_limit_bytes=60 << 20),
    )(dest, target, col_target, a_blocks, omega)


def gram_sum_kernel(nr, nc, gram, out_ref, *refs):
    r = lax.axis_index("row")
    c = lax.axis_index("col")
    greet(nr, nc, r, c)
    sum_gram(nr, nc, r, c, gram, out_ref, *refs)


def gram_sum(gram, nr, nc):
    return pl.pallas_call(
        functools.partial(gram_sum_kernel, nr, nc),
        out_shape=jax.ShapeDtypeStruct(gram.shape, jnp.float32),
        in_specs=[VMEM],
        out_specs=VMEM,
        scratch_shapes=packed_scratch(nr, nc, gram.shape[0]),
        compiler_params=pltpu.CompilerParams(collective_id=3, has_side_effects=True, vmem_limit_bytes=8 << 20),
    )(gram)


def eliminate(x):
    rows = x.shape[0]
    shape = (8, x.shape[1])
    groups = [x[i:i + 8, :] for i in range(0, rows, 8)]
    sub = lax.broadcasted_iota(jnp.int32, shape, 0)
    for g in range(rows // 8):
        j = 8 * g
        cols = [[jnp.broadcast_to(groups[i][:, j + l:j + l + 1], shape) for l in range(8)]
                for i in range(g, rows // 8)]
        piv = [[jnp.broadcast_to(cols[0][l][k:k + 1, :], shape) for l in range(8)] for k in range(8)]
        tops = [jnp.broadcast_to(groups[g][k:k + 1, :], shape) for k in range(8)]
        recip = []
        for k in range(8):
            if k % 2 == 0:
                det = piv[k][k] * piv[k + 1][k + 1] - piv[k + 1][k] * piv[k][k + 1]
                recip += [1.0 / piv[k][k], piv[k][k] * (1.0 / det)]
            for m in range(k + 1, 8):
                q = piv[m][k] * recip[k]
                for l in range(k + 1, 8):
                    piv[m][l] = piv[m][l] - q * piv[k][l]
                tops[m] = tops[m] - q * tops[k]
        for i in range(g + 1, rows // 8):
            here = cols[i - g]
            value = groups[i]
            for k in range(8):
                f = here[k] * recip[k]
                for l in range(k + 1, 8):
                    here[l] = here[l] - f * piv[k][l]
                value = value - f * tops[k]
            groups[i] = value
        for k in range(1, 8):
            groups[g] = jnp.where(sub == k, tops[k], groups[g])
    return jnp.concatenate(groups, axis=0)


def factor_gram(gram, left, right, upper, inverse):
    order = gram.shape[0]
    row = lax.broadcasted_iota(jnp.int32, (order, order), 0)
    col = lax.broadcasted_iota(jnp.int32, (order, order), 1)
    only = jnp.where(row == col, gram[...], 0.0)
    diag = jnp.sum(only, axis=0, keepdims=True)
    unit = 1.0 / jnp.sqrt(diag)
    back = diag * unit
    left[...] = gram[...] * (1.0 / jnp.sqrt(jnp.sum(only, axis=1, keepdims=True))) * unit
    right[...] = jnp.where(row == col, unit, 0.0)
    upper[...] = jnp.zeros_like(upper)
    inverse[...] = jnp.zeros_like(inverse)
    lane = lax.broadcasted_iota(jnp.int32, (PANEL, 2 * PANEL), 1)
    prow = lax.broadcasted_iota(jnp.int32, (PANEL, 2 * PANEL), 0)
    for base in range(0, order, PANEL):
        low = base // (2 * PANEL) * 2 * PANEL
        high = low + 2 * PANEL
        here = slice(base, base + PANEL)
        tile = left[here, low:high]
        if base > low:
            tile = pltpu.roll(tile, PANEL, 1)
        x = eliminate(jnp.where(lane < PANEL, tile, (lane - PANEL == prow).astype(jnp.float32)))
        root = 1.0 / jnp.sqrt(jnp.sum(jnp.where(lane == prow, x, 0.0), axis=1, keepdims=True))
        factor = pltpu.roll(x, PANEL, 1)[:, :PANEL]
        u = dot_nn(factor, left[here, low:]) * root
        v = dot_nn(factor, right[here, :high]) * root
        upper[here, low:] = jnp.where(col[here, low:] >= row[here, low:], u * back[:, low:], 0.0)
        inverse[here, :high] = jnp.where(col[here, :high] <= row[here, :high], v, 0.0)
        after = base + PANEL
        if after < order:
            start = after // (2 * PANEL) * 2 * PANEL
            rest = u[:, start - low:]
            left[after:, start:] -= dot_tn(rest, rest)[after - start:]
            right[after:, :high] -= dot_tn(rest, v)[after - start:]


def factor_kernel(scale, sketch, upper_out, factor, inverse, again, left, right):
    order = inverse.shape[0]
    gram = sketch.at[pl.ds(sketch.shape[0] - order, order)]
    factor_gram(gram, left, right, upper_out, inverse)
    factor[...] = upper_out[...] * (1.0 / scale)
    row = lax.broadcasted_iota(jnp.int32, (order, order), 0)
    col = lax.broadcasted_iota(jnp.int32, (order, order), 1)
    diag = jnp.sum(jnp.where(row == col, gram[...], 0.0), axis=0, keepdims=True)
    spread = jnp.sum(inverse[...] * inverse[...], axis=0, keepdims=True) * diag
    mean = jnp.sum(spread) * (1.0 / order)
    again[0] = jnp.where(mean <= INFLATION, 0, 1)


def factor_first(sketch, scale):
    order = sketch.shape[1]
    square = jax.ShapeDtypeStruct((order, order), jnp.float32)
    return pl.pallas_call(
        functools.partial(factor_kernel, scale),
        out_shape=(square, square, square, jax.ShapeDtypeStruct((1,), jnp.int32)),
        in_specs=[VMEM],
        out_specs=(VMEM, VMEM, VMEM, SMEM),
        scratch_shapes=[pltpu.VMEM((order, order), jnp.float32)] * 2,
        compiler_params=pltpu.CompilerParams(vmem_limit_bytes=16 << 20),
    )(sketch)


def apply_kernel(scale, inverse, sketch, basis, ready, sem):
    pieces, step, _ = ready.shape
    matrix = inverse[...] * scale

    def store(i):
        return pltpu.make_async_copy(ready.at[i], basis.at[pl.ds(i * step, step)], sem.at[i])

    for i in range(pieces):
        ready[i] = dot_nt(sketch[i * step:(i + 1) * step, :], matrix)
        store(i).start()
    for i in range(pieces):
        store(i).wait()


def apply_inverse(inverse, sketch, scale):
    rows, width = sketch.shape[0] - sketch.shape[1], sketch.shape[1]
    pieces = 4
    return pl.pallas_call(
        functools.partial(apply_kernel, scale),
        out_shape=jax.ShapeDtypeStruct((rows, width), jnp.float32),
        in_specs=[VMEM, VMEM],
        out_specs=pl.BlockSpec(memory_space=pltpu.HBM),
        scratch_shapes=[pltpu.VMEM((pieces, rows // pieces, width), jnp.float32), pltpu.SemaphoreType.DMA((pieces,))],
        compiler_params=pltpu.CompilerParams(vmem_limit_bytes=16 << 20),
    )(inverse, sketch)


def once_kernel(inverse, sketch, once, second):
    second[...] = jnp.zeros_like(second)
    step = 256

    @pl.loop(0, once.shape[0] // step)
    def _(i):
        part = pl.ds(pl.multiple_of(i * step, step), step)
        rows = dot_nt(sketch[part, :], inverse[...])
        once[part, :] = rows
        second[...] += dot_tn(rows, rows)


def once_pass(inverse, sketch):
    return pl.pallas_call(
        once_kernel,
        out_shape=(
            jax.ShapeDtypeStruct((sketch.shape[0] - sketch.shape[1], sketch.shape[1]), jnp.float32),
            jax.ShapeDtypeStruct(inverse.shape, jnp.float32),
        ),
        in_specs=[VMEM, VMEM],
        out_specs=(VMEM, VMEM),
        compiler_params=pltpu.CompilerParams(vmem_limit_bytes=16 << 20),
    )(inverse, sketch)


def last_kernel(scale, gram, once, upper_one, basis, factor, left, right, upper, inverse):
    factor_gram(gram, left, right, upper, inverse)
    factor[...] = dot_nn(upper[...], upper_one[...]) * (1.0 / scale)
    step = 256

    @pl.loop(0, once.shape[0] // step)
    def _(i):
        part = pl.ds(pl.multiple_of(i * step, step), step)
        basis[part, :] = dot_nt(once[part, :], inverse[...]) * scale


def last_pass(gram, once, upper_one, scale):
    order = gram.shape[0]
    square = pltpu.VMEM((order, order), jnp.float32)
    return pl.pallas_call(
        functools.partial(last_kernel, scale),
        out_shape=(
            jax.ShapeDtypeStruct(once.shape, jnp.float32),
            jax.ShapeDtypeStruct((order, order), jnp.float32),
        ),
        in_specs=[VMEM, VMEM, VMEM],
        out_specs=(VMEM, VMEM),
        scratch_shapes=[square] * 4,
        compiler_params=pltpu.CompilerParams(vmem_limit_bytes=16 << 20),
    )(gram, once, upper_one)


def body(nr, nc, a_blocks, omega, route_dest, row_target, col_target):
    order = a_blocks.shape[2]
    sketch = make_sketch(
        route_dest.T, row_target.reshape(1, -1), col_target.T, a_blocks, omega.reshape(-1, order, omega.shape[1]), nr, nc)
    scale = float(nr * nc * RB_DEV * order) ** 0.5
    upper, factor, inverse, again = factor_first(sketch, scale)

    def orthogonalize_again():
        once, gram_part = once_pass(inverse, sketch)
        return last_pass(gram_sum(gram_part, nr, nc), once, upper, scale)

    def keep_once():
        return apply_inverse(inverse, sketch, scale), factor

    return lax.cond(again[0] != 0, orthogonalize_again, keep_once)


def solution(mesh):
    nr, nc = mesh.shape["row"], mesh.shape["col"]
    return jax.shard_map(
        functools.partial(body, nr, nc),
        mesh=mesh,
        in_specs=(
            P(("row", "col"), None, None, None),
            P("col", None),
            P(("row", "col"), None),
            P(("row", "col")),
            P(("row", "col"), None),
        ),
        out_specs=(P(("row", "col"), None), P()),
        check_vma=False,
    )
```

```python
import functools

import jax
import jax.numpy as jnp
from jax import lax
from jax.experimental import pallas as pl
from jax.experimental.pallas import tpu as pltpu
from jax.sharding import PartitionSpec as P

RB_DEV = 8
CAP = 4
PANEL = 64
LOADS = 8
NOWHERE = 1 << 20
INFLATION = 2.0
CHUNKS = 8
WINDOW = 2
MESH = pl.DeviceIdType.MESH
VMEM = pl.BlockSpec(memory_space=pltpu.VMEM)
SMEM = pl.BlockSpec(memory_space=pltpu.SMEM)
HIGH = lax.Precision.HIGHEST


def dot_nn(a, b):
    return lax.dot_general(a, b, (((1,), (0,)), ((), ())), precision=HIGH, preferred_element_type=jnp.float32)


def dot_nt(a, b):
    return lax.dot_general(a, b, (((1,), (1,)), ((), ())), precision=HIGH, preferred_element_type=jnp.float32)


def dot_tn(a, b):
    return lax.dot_general(a, b, (((0,), (0,)), ((), ())), precision=HIGH, preferred_element_type=jnp.float32)


def place(dest, target, owners):
    count = dest.shape[1]
    i = lax.broadcasted_iota(jnp.int32, (count, count), 0)
    j = lax.broadcasted_iota(jnp.int32, (count, count), 1)
    down = jnp.sum(jnp.where(i == j, dest, 0), axis=1, keepdims=True)
    rank = jnp.sum(jnp.logical_and(down == dest, j < i).astype(jnp.int32), axis=1, keepdims=True)
    rank_across = jnp.sum(jnp.where(i == j, rank, 0), axis=0, keepdims=True)
    lane = lax.broadcasted_iota(jnp.int32, (count, 128), 1)
    which = lax.broadcasted_iota(jnp.int32, (count, 128), 0)
    source = jnp.sum(jnp.where(down * CAP + rank == lane, which, 0), axis=0, keepdims=True)
    place_of = lax.broadcasted_iota(jnp.int32, (owners * 8, count), 0)
    here = place_of == dest * 8 + rank_across
    rows = jnp.sum(jnp.where(here, target + 1, 0), axis=1, keepdims=True)
    rows = jnp.where(rows > 0, rows - 1, NOWHERE)
    return source, jnp.broadcast_to(rows, (owners * 8, 128))


def signal_all(nr, nc, r, c):
    barrier = pltpu.get_barrier_semaphore()
    for k in range(1, nr):
        pl.semaphore_signal(barrier, inc=1, device_id=(lax.rem(r + k, nr), c), device_id_type=MESH)
    for k in range(1, nc):
        pl.semaphore_signal(barrier, inc=1, device_id=(r, lax.rem(c + k, nc)), device_id_type=MESH)


def wait_all(nr, nc):
    pl.semaphore_wait(pltpu.get_barrier_semaphore(), nr - 1 + nc - 1)


def greet(nr, nc, r, c):
    signal_all(nr, nc, r, c)
    wait_all(nr, nc)


def reduce_packed(nr, nc, r, c, gram, landed, cols, full, sems):
    a_s, a_r, b_s, b_r, c_s, c_r = sems
    chunk = gram.shape[0] // nr
    mine = pl.ds(pl.multiple_of(r * chunk, chunk), chunk)
    copies = []
    for k in range(1, nr):
        d = lax.rem(r + k, nr)
        cp = pltpu.make_async_remote_copy(
            gram.at[pl.ds(pl.multiple_of(d * chunk, chunk), chunk), :], landed.at[k], a_s.at[k], a_r.at[k],
            device_id=(d, c), device_id_type=MESH)
        cp.start()
        copies.append(cp)
    total = gram[mine, :]
    for k in range(1, nr):
        copies[k - 1].wait_recv()
        total = total + landed[k]
    cols[c] = total
    across = []
    for k in range(1, nc):
        cp = pltpu.make_async_remote_copy(
            cols.at[c], cols.at[c], b_s.at[k], b_r.at[k], device_id=(r, lax.rem(c + k, nc)), device_id_type=MESH)
        cp.start()
        across.append(cp)
    for cp in across:
        cp.wait_recv()
    total = cols[0]
    for k in range(1, nc):
        total = total + cols[k]
    full[mine, :] = total
    back = []
    for k in range(1, nr):
        cp = pltpu.make_async_remote_copy(
            full.at[mine, :], full.at[mine, :], c_s.at[k], c_r.at[k], device_id=(lax.rem(r + k, nr), c), device_id_type=MESH)
        cp.start()
        back.append(cp)
    for cp in back:
        cp.wait_recv()
    for cp in copies + across + back:
        cp.wait_send()


def packed_scratch(nr, nc, width):
    dma = pltpu.SemaphoreType.DMA
    half = width // 2
    chunk = 3 * half // nr
    return [
        pltpu.VMEM((3 * half, half), jnp.float32),
        pltpu.VMEM((nr, chunk, half), jnp.float32),
        pltpu.VMEM((nc, chunk, half), jnp.float32),
        pltpu.VMEM((3 * half, half), jnp.float32),
        dma((nr,)), dma((nr,)), dma((nc,)), dma((nc,)), dma((nr,)), dma((nr,)),
    ]


def sum_gram(nr, nc, r, c, gram, out_ref, packed, landed, cols, full, *sems):
    half = gram.shape[0] // 2
    packed[:half, :] = gram[:half, :half]
    packed[half:2 * half, :] = gram[:half, half:]
    packed[2 * half:, :] = gram[half:, half:]
    reduce_packed(nr, nc, r, c, packed, landed, cols, full, sems)
    whole = full[...]
    out_ref[:half, :half] = whole[:half]
    side = whole[half:2 * half]
    out_ref[:half, half:] = side
    out_ref[half:, :half] = side.T
    out_ref[half:, half:] = whole[2 * half:]


def arrange(rows, slots):
    count = rows.shape[0]
    i = lax.broadcasted_iota(jnp.int32, rows.shape, 0)
    j = lax.broadcasted_iota(jnp.int32, rows.shape, 1)
    across = jnp.sum(jnp.where(i == j, rows, 0), axis=0, keepdims=True)
    ahead = jnp.logical_or(across < rows, jnp.logical_and(across == rows, j < i))
    ahead = jnp.logical_and(ahead, j < count)
    rank = jnp.sum(ahead.astype(jnp.int32), axis=1, keepdims=True)
    slot = (i // 8) * CAP + lax.rem(i, 8)
    order = jnp.sum(jnp.where(rank == j, slot, 0), axis=0, keepdims=True)
    here = jnp.sum(jnp.where(rank == j, rows, 0), axis=0, keepdims=True)
    before = jnp.sum(jnp.where(rank == j - 1, rows, 0), axis=0, keepdims=True)
    keep = jnp.logical_and(here == before, j[:1] > 0).astype(jnp.int32)
    last = jnp.max(jnp.where(rows == j, rank, -1), axis=0, keepdims=True)
    valid = (last >= 0).astype(jnp.int32)
    order = jnp.minimum(order, slots - 1)
    last = jnp.clip(last, 0, slots - 1)
    return jnp.concatenate([order, keep, last, valid], axis=0)


def sketch_kernel(nr, nc, dest_hbm, target_hbm, col_hbm, a_hbm, omega_hbm, sketch_ref, *refs):
    chunks = CHUNKS
    gots, refs = refs[:chunks], refs[chunks:]
    (dest_ref, target_ref, col_ref, a_buf, omega_buf, parts, send_ref, row_ref, sources, a_sem, in_sem,
     rows_in, meta, table, prefix, term, to_right, to_left, total, gram, row_s, row_r, own_s,
     send_s, send_r, right_s, right_r, left_s, left_r), refs = refs[:29], refs[29:]
    targets, groups, order, _ = a_buf.shape
    rq, width = order // chunks, omega_buf.shape[2]
    slots = nr * CAP
    blocks = nc * RB_DEV
    loads = targets // LOADS
    r = lax.axis_index("row")
    c = lax.axis_index("col")

    def fetch(i):
        part = pl.ds(i * LOADS, LOADS)
        return pltpu.make_async_copy(a_hbm.at[part], a_buf.at[part], a_sem.at[i])

    def route(k):
        d = lax.rem(r + k, nr)
        return pltpu.make_async_remote_copy(
            row_ref.at[d], rows_in.at[r], row_s.at[k], row_r.at[k], device_id=(d, c), device_id_type=MESH)

    def swap(q, k):
        d = lax.rem(r + k, nr)
        return pltpu.make_async_remote_copy(
            send_ref.at[q, d], gots[q].at[pl.ds(r * CAP, CAP)], send_s.at[q, k], send_r.at[q, k],
            device_id=(d, c), device_id_type=MESH)

    def keep_own(q):
        return pltpu.make_async_copy(send_ref.at[q, r], gots[q].at[pl.ds(r * CAP, CAP)], own_s.at[q])

    def hop_right(q, d):
        return pltpu.make_async_remote_copy(
            to_right.at[q, d], to_right.at[q, d], right_s.at[q, d], right_r.at[q, d],
            device_id=(r, lax.rem(c + 1, nc)), device_id_type=MESH)

    def hop_left(q, d):
        return pltpu.make_async_remote_copy(
            to_left.at[q, d], to_left.at[q, d], left_s.at[q, d], left_r.at[q, d],
            device_id=(r, lax.rem(c + nc - 1, nc)), device_id_type=MESH)

    others = [pltpu.make_async_copy(src, dst, in_sem.at[i]) for i, (src, dst) in enumerate(
        ((dest_hbm, dest_ref), (target_hbm, target_ref), (col_hbm, col_ref), (omega_hbm, omega_buf)))]
    for copy in others:
        copy.start()
    for i in range(loads):
        fetch(i).start()
    signal_all(nr, nc, r, c)
    others[0].wait()
    others[1].wait()
    source, rows = place(dest_ref[...], target_ref[...], nr)
    row_ref[...] = rows.reshape(nr, 8, 128)
    meta[...] = jnp.zeros_like(meta)
    meta[:1, :] = source
    to_sources = pltpu.make_async_copy(meta, sources, own_s.at[chunks + 1])
    to_sources.start()
    own_rows = pltpu.make_async_copy(row_ref.at[r], rows_in.at[r], own_s.at[chunks])
    own_rows.start()
    gram[...] = jnp.zeros_like(gram)
    others[2].wait()
    others[3].wait()

    def multiply(i, carry):
        fetch(i).wait()
        for local in range(LOADS):
            t = i * LOADS + local
            sums = None
            for g in range(0, groups, 2):
                left = jnp.concatenate([a_buf[t, g], a_buf[t, g + 1]], axis=1)
                right = jnp.concatenate([omega_buf[col_ref[g, t]], omega_buf[col_ref[g + 1, t]]], axis=0)
                product = jnp.dot(left, right, preferred_element_type=jnp.float32)
                sums = product if sums is None else sums + product
            sums = sums.astype(jnp.bfloat16)
            for q in range(chunks):
                parts[q, t] = sums[q * rq:(q + 1) * rq]
        return carry

    lax.fori_loop(0, loads // 2, multiply, 0)
    wait_all(nr, nc)
    for k in range(1, nr):
        route(k).start()
    lax.fori_loop(loads // 2, loads, multiply, 0)
    own_rows.wait()
    to_sources.wait()
    for q in range(chunks):
        for d in range(nr):
            for k in range(CAP):
                send_ref[q, d, k] = parts[q, sources[0, d * CAP + k]]
        keep_own(q).start()
        if q == 0:
            for k in range(1, nr):
                swap(0, k).start()
    for k in range(1, nr):
        route(k).wait_recv()
    meta[:4, :] = arrange(rows_in[...].reshape(nr * 8, 128), slots)
    to_table = pltpu.make_async_copy(meta, table, own_s.at[chunks + 1])
    to_table.start()
    to_table.wait()

    from_first = [(q, d) for q in range(chunks) for d in range(nc - 1, 0, -1)]
    from_last = [(q, d) for q in range(chunks) for d in range(nc - 1)]

    def start_ends(q, sends, buffer, hop):
        for n, (at, d) in enumerate(sends):
            if at == q:
                if n >= WINDOW:
                    hop(*sends[n - WINDOW]).wait_send()
                buffer[q, d] = term[q % nc, d * RB_DEV:(d + 1) * RB_DEV].astype(jnp.bfloat16)
                hop(q, d).start()

    def collect(q):
        keep_own(q).wait()
        for k in range(1, nr):
            swap(q, k).wait_send()
        if q + 1 < chunks:
            for k in range(1, nr):
                swap(q + 1, k).start()
        for k in range(1, nr):
            swap(q, k).wait_recv()
        got = gots[q]

        def add(k, acc):
            acc = acc * table[1, k].astype(jnp.float32) + got[table[0, k]].astype(jnp.float32)
            prefix[k] = acc
            return acc

        lax.fori_loop(0, slots, add, jnp.zeros((rq, width), jnp.float32), unroll=8)

        @pl.loop(0, blocks, unroll=8)
        def _(b):
            term[q % nc, b] = prefix[table[2, b]] * table[3, b].astype(jnp.float32)

        @pl.when(c == 0)
        def _():
            start_ends(q, from_first, to_right, hop_right)

        @pl.when(c == nc - 1)
        def _():
            start_ends(q, from_last, to_left, hop_left)

    def add_and_send(q, d, buffer, hop):
        hop(q, d).wait_recv()
        mine = term[q % nc, d * RB_DEV:(d + 1) * RB_DEV]
        buffer[q, d] = (buffer[q, d].astype(jnp.float32) + mine).astype(jnp.bfloat16)
        hop(q, d).start()

    def pass_on(q, hops):
        @pl.when(c == hops)
        def _():
            for d in range(nc - 1, hops, -1):
                add_and_send(q, d, to_right, hop_right)

        @pl.when(c == nc - 1 - hops)
        def _():
            for d in range(nc - 1 - hops):
                add_and_send(q, d, to_left, hop_left)

    def finish(q):
        total[...] = term[q % nc, pl.ds(c * RB_DEV, RB_DEV)]

        @pl.when(c > 0)
        def _():
            hop_right(q, c).wait_recv()
            total[...] += to_right[q, c].astype(jnp.float32)

        @pl.when(c < nc - 1)
        def _():
            hop_left(q, c).wait_recv()
            total[...] += to_left[q, c].astype(jnp.float32)

        for b in range(RB_DEV):
            start = b * chunks * rq + q * rq
            sketch_ref[start:start + rq, :] = total[b]
        rows = total[...].reshape(RB_DEV * rq, width)
        gram[...] += dot_tn(rows, rows)

    for q in range(chunks + nc - 1):
        if q < chunks:
            collect(q)
        for hops in range(1, nc - 1):
            if 0 <= q - hops < chunks:
                pass_on(q - hops, hops)
        if q >= nc - 1:
            finish(q - nc + 1)

    sum_gram(nr, nc, r, c, gram, sketch_ref.at[pl.ds(RB_DEV * order, width)], *refs)
    for k in range(1, nr):
        route(k).wait_send()
    for q in range(chunks):
        for d in range(nc):
            @pl.when(jnp.logical_and(c > 0, c < d))
            def _():
                hop_right(q, d).wait_send()

            @pl.when(jnp.logical_and(c < nc - 1, c > d))
            def _():
                hop_left(q, d).wait_send()

    @pl.when(c == 0)
    def _():
        for send in from_first[-WINDOW:]:
            hop_right(*send).wait_send()

    @pl.when(c == nc - 1)
    def _():
        for send in from_last[-WINDOW:]:
            hop_left(*send).wait_send()


def make_sketch(dest, target, col_target, a_blocks, omega, nr, nc):
    targets, _, order, _ = a_blocks.shape
    width = omega.shape[2]
    chunks, rq = CHUNKS, order // CHUNKS
    dma = pltpu.SemaphoreType.DMA
    slots, blocks = nr * CAP, nc * RB_DEV
    hops = pltpu.VMEM((chunks, nc, RB_DEV, rq, width), jnp.bfloat16)
    hbm = pl.BlockSpec(memory_space=pltpu.HBM)
    return pl.pallas_call(
        functools.partial(sketch_kernel, nr, nc),
        out_shape=jax.ShapeDtypeStruct((RB_DEV * order + width, width), jnp.float32),
        in_specs=[hbm] * 5,
        out_specs=VMEM,
        scratch_shapes=[pltpu.VMEM((slots, rq, width), jnp.bfloat16)] * chunks + [
            pltpu.VMEM(dest.shape, jnp.int32),
            pltpu.VMEM(target.shape, jnp.int32),
            pltpu.SMEM(col_target.shape, jnp.int32),
            pltpu.VMEM(a_blocks.shape, a_blocks.dtype),
            pltpu.VMEM(omega.shape, omega.dtype),
            pltpu.VMEM((chunks, targets, rq, width), jnp.bfloat16),
            pltpu.VMEM((chunks, nr, CAP, rq, width), jnp.bfloat16),
            pltpu.VMEM((nr, 8, 128), jnp.int32),
            pltpu.SMEM((8, 128), jnp.int32),
            dma((targets // LOADS,)), dma((4,)),
            pltpu.VMEM((nr, 8, 128), jnp.int32),
            pltpu.VMEM((8, 128), jnp.int32),
            pltpu.SMEM((8, 128), jnp.int32),
            pltpu.VMEM((slots, rq, width), jnp.float32),
            pltpu.VMEM((nc, blocks, rq, width), jnp.float32),
            hops, hops,
            pltpu.VMEM((RB_DEV, rq, width), jnp.float32),
            pltpu.VMEM((width, width), jnp.float32),
            dma((nr,)), dma((nr,)), dma((chunks + 2,)),
            dma((chunks, nr)), dma((chunks, nr)),
            dma((chunks, nc)), dma((chunks, nc)), dma((chunks, nc)), dma((chunks, nc)),
        ] + packed_scratch(nr, nc, width),
        compiler_params=pltpu.CompilerParams(collective_id=1, has_side_effects=True, vmem_limit_bytes=60 << 20),
    )(dest, target, col_target, a_blocks, omega)


def gram_sum_kernel(nr, nc, gram, out_ref, *refs):
    r = lax.axis_index("row")
    c = lax.axis_index("col")
    greet(nr, nc, r, c)
    sum_gram(nr, nc, r, c, gram, out_ref, *refs)


def gram_sum(gram, nr, nc):
    return pl.pallas_call(
        functools.partial(gram_sum_kernel, nr, nc),
        out_shape=jax.ShapeDtypeStruct(gram.shape, jnp.float32),
        in_specs=[VMEM],
        out_specs=VMEM,
        scratch_shapes=packed_scratch(nr, nc, gram.shape[0]),
        compiler_params=pltpu.CompilerParams(collective_id=3, has_side_effects=True, vmem_limit_bytes=8 << 20),
    )(gram)


def eliminate(x):
    rows = x.shape[0]
    shape = (8, x.shape[1])
    groups = [x[i:i + 8, :] for i in range(0, rows, 8)]
    sub = lax.broadcasted_iota(jnp.int32, shape, 0)
    for g in range(rows // 8):
        j = 8 * g
        cols = [[jnp.broadcast_to(groups[i][:, j + l:j + l + 1], shape) for l in range(8)]
                for i in range(g, rows // 8)]
        piv = [[jnp.broadcast_to(cols[0][l][k:k + 1, :], shape) if l >= k else None for l in range(8)] for k in range(8)]
        tops = [jnp.broadcast_to(groups[g][k:k + 1, :], shape) for k in range(8)]
        ratio, scaled = [], []
        for k in range(8):
            if k % 2 == 0:
                side = piv[k][k + 1]
                det = piv[k][k] * piv[k + 1][k + 1] - side * side
                recip, second = 1.0 / piv[k][k], piv[k][k] * (1.0 / det)
            else:
                recip = second
            ratio.append([piv[k][l] * recip if l > k else None for l in range(8)])
            scaled.append(tops[k] * recip)
            for m in range(k + 1, 8):
                for l in range(m, 8):
                    piv[m][l] = piv[m][l] - ratio[k][m] * piv[k][l]
                tops[m] = tops[m] - ratio[k][m] * tops[k]
        for i in range(g + 1, rows // 8):
            here = cols[i - g]
            value = groups[i]
            for k in range(8):
                for l in range(k + 1, 8):
                    here[l] = here[l] - here[k] * ratio[k][l]
                value = value - here[k] * scaled[k]
            groups[i] = value
        for k in range(1, 8):
            groups[g] = jnp.where(sub == k, tops[k], groups[g])
    return jnp.concatenate(groups, axis=0)


def factor_gram(gram, left, right, upper, inverse):
    order = gram.shape[0]
    row = lax.broadcasted_iota(jnp.int32, (order, order), 0)
    col = lax.broadcasted_iota(jnp.int32, (order, order), 1)
    only = jnp.where(row == col, gram[...], 0.0)
    diag = jnp.sum(only, axis=0, keepdims=True)
    unit = 1.0 / jnp.sqrt(diag)
    back = diag * unit
    left[...] = gram[...] * (1.0 / jnp.sqrt(jnp.sum(only, axis=1, keepdims=True))) * unit
    right[...] = jnp.where(row == col, unit, 0.0)
    upper[...] = jnp.zeros_like(upper)
    inverse[...] = jnp.zeros_like(inverse)
    lane = lax.broadcasted_iota(jnp.int32, (PANEL, 2 * PANEL), 1)
    prow = lax.broadcasted_iota(jnp.int32, (PANEL, 2 * PANEL), 0)
    for base in range(0, order, PANEL):
        low = base // (2 * PANEL) * 2 * PANEL
        high = low + 2 * PANEL
        here = slice(base, base + PANEL)
        tile = left[here, low:high]
        if base > low:
            tile = pltpu.roll(tile, PANEL, 1)
        x = eliminate(jnp.where(lane < PANEL, tile, (lane - PANEL == prow).astype(jnp.float32)))
        root = 1.0 / jnp.sqrt(jnp.sum(jnp.where(lane == prow, x, 0.0), axis=1, keepdims=True))
        factor = pltpu.roll(x, PANEL, 1)[:, :PANEL]
        u = dot_nn(factor, left[here, low:]) * root
        v = dot_nn(factor, right[here, :high]) * root
        upper[here, low:] = jnp.where(col[here, low:] >= row[here, low:], u * back[:, low:], 0.0)
        inverse[here, :high] = jnp.where(col[here, :high] <= row[here, :high], v, 0.0)
        after = base + PANEL
        if after < order:
            start = after // (2 * PANEL) * 2 * PANEL
            rest = u[:, start - low:]
            left[after:, start:] -= dot_tn(rest, rest)[after - start:]
            right[after:, :high] -= dot_tn(rest, v)[after - start:]


def factor_kernel(scale, sketch, upper_out, factor, inverse, again, left, right):
    order = inverse.shape[0]
    gram = sketch.at[pl.ds(sketch.shape[0] - order, order)]
    factor_gram(gram, left, right, upper_out, inverse)
    factor[...] = upper_out[...] * (1.0 / scale)
    row = lax.broadcasted_iota(jnp.int32, (order, order), 0)
    col = lax.broadcasted_iota(jnp.int32, (order, order), 1)
    diag = jnp.sum(jnp.where(row == col, gram[...], 0.0), axis=0, keepdims=True)
    spread = jnp.sum(inverse[...] * inverse[...], axis=0, keepdims=True) * diag
    mean = jnp.sum(spread) * (1.0 / order)
    again[0] = jnp.where(mean <= INFLATION, 0, 1)


def factor_first(sketch, scale):
    order = sketch.shape[1]
    square = jax.ShapeDtypeStruct((order, order), jnp.float32)
    return pl.pallas_call(
        functools.partial(factor_kernel, scale),
        out_shape=(square, square, square, jax.ShapeDtypeStruct((1,), jnp.int32)),
        in_specs=[VMEM],
        out_specs=(VMEM, VMEM, VMEM, SMEM),
        scratch_shapes=[pltpu.VMEM((order, order), jnp.float32)] * 2,
        compiler_params=pltpu.CompilerParams(vmem_limit_bytes=16 << 20),
    )(sketch)


def apply_kernel(scale, inverse, sketch, basis, ready, sem):
    pieces, step, _ = ready.shape
    matrix = inverse[...] * scale

    def store(i):
        return pltpu.make_async_copy(ready.at[i], basis.at[pl.ds(i * step, step)], sem.at[i])

    for i in range(pieces):
        ready[i] = dot_nt(sketch[i * step:(i + 1) * step, :], matrix)
        store(i).start()
    for i in range(pieces):
        store(i).wait()


def apply_inverse(inverse, sketch, scale):
    rows, width = sketch.shape[0] - sketch.shape[1], sketch.shape[1]
    pieces = 4
    return pl.pallas_call(
        functools.partial(apply_kernel, scale),
        out_shape=jax.ShapeDtypeStruct((rows, width), jnp.float32),
        in_specs=[VMEM, VMEM],
        out_specs=pl.BlockSpec(memory_space=pltpu.HBM),
        scratch_shapes=[pltpu.VMEM((pieces, rows // pieces, width), jnp.float32), pltpu.SemaphoreType.DMA((pieces,))],
        compiler_params=pltpu.CompilerParams(vmem_limit_bytes=16 << 20),
    )(inverse, sketch)


def once_kernel(inverse, sketch, once, second):
    second[...] = jnp.zeros_like(second)
    step = 256

    @pl.loop(0, once.shape[0] // step)
    def _(i):
        part = pl.ds(pl.multiple_of(i * step, step), step)
        rows = dot_nt(sketch[part, :], inverse[...])
        once[part, :] = rows
        second[...] += dot_tn(rows, rows)


def once_pass(inverse, sketch):
    return pl.pallas_call(
        once_kernel,
        out_shape=(
            jax.ShapeDtypeStruct((sketch.shape[0] - sketch.shape[1], sketch.shape[1]), jnp.float32),
            jax.ShapeDtypeStruct(inverse.shape, jnp.float32),
        ),
        in_specs=[VMEM, VMEM],
        out_specs=(VMEM, VMEM),
        compiler_params=pltpu.CompilerParams(vmem_limit_bytes=16 << 20),
    )(inverse, sketch)


def last_kernel(scale, gram, once, upper_one, basis, factor, left, right, upper, inverse):
    factor_gram(gram, left, right, upper, inverse)
    factor[...] = dot_nn(upper[...], upper_one[...]) * (1.0 / scale)
    step = 256

    @pl.loop(0, once.shape[0] // step)
    def _(i):
        part = pl.ds(pl.multiple_of(i * step, step), step)
        basis[part, :] = dot_nt(once[part, :], inverse[...]) * scale


def last_pass(gram, once, upper_one, scale):
    order = gram.shape[0]
    square = pltpu.VMEM((order, order), jnp.float32)
    return pl.pallas_call(
        functools.partial(last_kernel, scale),
        out_shape=(
            jax.ShapeDtypeStruct(once.shape, jnp.float32),
            jax.ShapeDtypeStruct((order, order), jnp.float32),
        ),
        in_specs=[VMEM, VMEM, VMEM],
        out_specs=(VMEM, VMEM),
        scratch_shapes=[square] * 4,
        compiler_params=pltpu.CompilerParams(vmem_limit_bytes=16 << 20),
    )(gram, once, upper_one)


def body(nr, nc, a_blocks, omega, route_dest, row_target, col_target):
    order = a_blocks.shape[2]
    sketch = make_sketch(
        route_dest.T, row_target.reshape(1, -1), col_target.T, a_blocks, omega.reshape(-1, order, omega.shape[1]), nr, nc)
    scale = float(nr * nc * RB_DEV * order) ** 0.5
    upper, factor, inverse, again = factor_first(sketch, scale)

    def orthogonalize_again():
        once, gram_part = once_pass(inverse, sketch)
        return last_pass(gram_sum(gram_part, nr, nc), once, upper, scale)

    def keep_once():
        return apply_inverse(inverse, sketch, scale), factor

    return lax.cond(again[0] != 0, orthogonalize_again, keep_once)


def solution(mesh):
    nr, nc = mesh.shape["row"], mesh.shape["col"]
    return jax.shard_map(
        functools.partial(body, nr, nc),
        mesh=mesh,
        in_specs=(
            P(("row", "col"), None, None, None),
            P("col", None),
            P(("row", "col"), None),
            P(("row", "col")),
            P(("row", "col"), None),
        ),
        out_specs=(P(("row", "col"), None), P()),
        check_vma=False,
    )
```

```python
import functools

import jax
import jax.numpy as jnp
from jax import lax
from jax.experimental import pallas as pl
from jax.experimental.pallas import tpu as pltpu
from jax.sharding import PartitionSpec as P

RB_DEV = 8
CAP = 4
PANEL = 64
LOADS = 8
FIRST = 4
NOWHERE = 1 << 20
INFLATION = 2.0
CHUNKS = 8
WINDOW = 2
MESH = pl.DeviceIdType.MESH
VMEM = pl.BlockSpec(memory_space=pltpu.VMEM)
SMEM = pl.BlockSpec(memory_space=pltpu.SMEM)
HIGH = lax.Precision.HIGHEST


def dot_nn(a, b):
    return lax.dot_general(a, b, (((1,), (0,)), ((), ())), precision=HIGH, preferred_element_type=jnp.float32)


def dot_nt(a, b):
    return lax.dot_general(a, b, (((1,), (1,)), ((), ())), precision=HIGH, preferred_element_type=jnp.float32)


def dot_tn(a, b):
    return lax.dot_general(a, b, (((0,), (0,)), ((), ())), precision=HIGH, preferred_element_type=jnp.float32)


def place(dest, target, owners):
    count = dest.shape[1]
    i = lax.broadcasted_iota(jnp.int32, (count, count), 0)
    j = lax.broadcasted_iota(jnp.int32, (count, count), 1)
    down = jnp.sum(jnp.where(i == j, dest, 0), axis=1, keepdims=True)
    rank = jnp.sum(jnp.logical_and(down == dest, j < i).astype(jnp.int32), axis=1, keepdims=True)
    rank_across = jnp.sum(jnp.where(i == j, rank, 0), axis=0, keepdims=True)
    lane = lax.broadcasted_iota(jnp.int32, (count, 128), 1)
    which = lax.broadcasted_iota(jnp.int32, (count, 128), 0)
    source = jnp.sum(jnp.where(down * CAP + rank == lane, which, 0), axis=0, keepdims=True)
    place_of = lax.broadcasted_iota(jnp.int32, (owners * 8, count), 0)
    here = place_of == dest * 8 + rank_across
    rows = jnp.sum(jnp.where(here, target + 1, 0), axis=1, keepdims=True)
    rows = jnp.where(rows > 0, rows - 1, NOWHERE)
    return source, jnp.broadcast_to(rows, (owners * 8, 128))


def signal_all(nr, nc, r, c):
    barrier = pltpu.get_barrier_semaphore()
    for k in range(1, nr):
        pl.semaphore_signal(barrier, inc=1, device_id=(lax.rem(r + k, nr), c), device_id_type=MESH)
    for k in range(1, nc):
        pl.semaphore_signal(barrier, inc=1, device_id=(r, lax.rem(c + k, nc)), device_id_type=MESH)


def wait_all(nr, nc):
    pl.semaphore_wait(pltpu.get_barrier_semaphore(), nr - 1 + nc - 1)


def greet(nr, nc, r, c):
    signal_all(nr, nc, r, c)
    wait_all(nr, nc)


def reduce_packed(nr, nc, r, c, packed, landed, cols, full, sems):
    a_s, a_r, b_s, b_r, c_s, c_r = sems
    copies, across, back = [], [], []
    for k in range(1, nr):
        d = lax.rem(r + k, nr)
        copies.append(pltpu.make_async_remote_copy(
            packed.at[d], landed.at[k], a_s.at[k], a_r.at[k], device_id=(d, c), device_id_type=MESH))
        copies[-1].start()
    total = packed[r]
    for k in range(1, nr):
        copies[k - 1].wait_recv()
        total = total + landed[k]
    cols[c] = total
    for k in range(1, nc):
        across.append(pltpu.make_async_remote_copy(
            cols.at[c], cols.at[c], b_s.at[k], b_r.at[k], device_id=(r, lax.rem(c + k, nc)), device_id_type=MESH))
        across[-1].start()
    for cp in across:
        cp.wait_recv()
    total = cols[0]
    for k in range(1, nc):
        total = total + cols[k]
    full[r] = total
    for k in range(1, nr):
        back.append(pltpu.make_async_remote_copy(
            full.at[r], full.at[r], c_s.at[k], c_r.at[k], device_id=(lax.rem(r + k, nr), c), device_id_type=MESH))
        back[-1].start()
    for cp in back:
        cp.wait_recv()
    for cp in copies + across + back:
        cp.wait_send()


def packed_scratch(nr, nc, width):
    dma = pltpu.SemaphoreType.DMA
    piece = (width // nr + 8, width // 2)
    return [
        pltpu.VMEM((nr,) + piece, jnp.float32),
        pltpu.VMEM((nr,) + piece, jnp.float32),
        pltpu.VMEM((nc,) + piece, jnp.float32),
        pltpu.VMEM((nr,) + piece, jnp.float32),
        dma((nr,)), dma((nr,)), dma((nc,)), dma((nc,)), dma((nr,)), dma((nr,)),
    ]


def sum_gram(nr, nc, r, c, gram, out_ref, packed, landed, cols, full, *sems):
    half = gram.shape[0] // 2
    main = 2 * half // nr
    row = lax.broadcasted_iota(jnp.int32, (half, half), 0)
    col = lax.broadcasted_iota(jnp.int32, (half, half), 1)
    low = gram[half:, half:]
    mixed = jnp.where(row <= col, gram[:half, :half], pltpu.roll(low, 1, 0))
    for k in range(nr):
        source, start = (gram[:half, half:], k * main) if k < nr // 2 else (mixed, k * main - half)
        packed[k, :main] = source[start:start + main]
        packed[k, main:] = jnp.broadcast_to(low[half - 1:half, :], (8, half))
    reduce_packed(nr, nc, r, c, packed, landed, cols, full, sems)
    side = full[:nr // 2, :main].reshape(half, half)
    mixed = full[nr // 2:, :main].reshape(half, half)
    low = jnp.where(row == half - 1, jnp.broadcast_to(full[0, main:main + 1], (half, half)), pltpu.roll(mixed, half - 1, 0))
    out_ref[:half, :half] = jnp.where(row <= col, mixed, mixed.T)
    out_ref[:half, half:] = side
    out_ref[half:, :half] = side.T
    out_ref[half:, half:] = jnp.where(row >= col, low, low.T)


def arrange(rows, slots):
    count = rows.shape[0]
    i = lax.broadcasted_iota(jnp.int32, rows.shape, 0)
    j = lax.broadcasted_iota(jnp.int32, rows.shape, 1)
    across = jnp.sum(jnp.where(i == j, rows, 0), axis=0, keepdims=True)
    ahead = jnp.logical_or(across < rows, jnp.logical_and(across == rows, j < i))
    ahead = jnp.logical_and(ahead, j < count)
    rank = jnp.sum(ahead.astype(jnp.int32), axis=1, keepdims=True)
    slot = (i // 8) * CAP + lax.rem(i, 8)
    order = jnp.sum(jnp.where(rank == j, slot, 0), axis=0, keepdims=True)
    here = jnp.sum(jnp.where(rank == j, rows, 0), axis=0, keepdims=True)
    before = jnp.sum(jnp.where(rank == j - 1, rows, 0), axis=0, keepdims=True)
    keep = jnp.logical_and(here == before, j[:1] > 0).astype(jnp.int32)
    last = jnp.max(jnp.where(rows == j, rank, -1), axis=0, keepdims=True)
    valid = (last >= 0).astype(jnp.int32)
    order = jnp.minimum(order, slots - 1)
    last = jnp.clip(last, 0, slots - 1)
    return jnp.concatenate([order, keep, last, valid], axis=0)


def sketch_kernel(nr, nc, dest_hbm, target_hbm, col_hbm, a_hbm, omega_hbm, sketch_ref, *refs):
    chunks = CHUNKS
    gots, refs = refs[:chunks], refs[chunks:]
    (dest_ref, target_ref, col_ref, a_buf, omega_buf, parts, send_ref, row_ref, sources, a_sem, in_sem,
     rows_in, meta, table, prefix, term, to_right, to_left, total, gram, row_s, row_r, own_s,
     send_s, send_r, right_s, right_r, left_s, left_r), refs = refs[:29], refs[29:]
    targets, groups, order, _ = a_buf.shape
    rq, width = order // chunks, omega_buf.shape[2]
    slots = nr * CAP
    blocks = nc * RB_DEV
    early = LOADS // FIRST
    loads = targets // LOADS - 1
    r = lax.axis_index("row")
    c = lax.axis_index("col")

    def fetch(i, size, skip):
        part = pl.ds(skip + i * size, size)
        return pltpu.make_async_copy(a_hbm.at[part], a_buf.at[part], a_sem.at[skip // FIRST + i])

    def route(k):
        d = lax.rem(r + k, nr)
        return pltpu.make_async_remote_copy(
            row_ref.at[d], rows_in.at[r], row_s.at[k], row_r.at[k], device_id=(d, c), device_id_type=MESH)

    def swap(q, k):
        d = lax.rem(r + k, nr)
        return pltpu.make_async_remote_copy(
            send_ref.at[q, d], gots[q].at[pl.ds(r * CAP, CAP)], send_s.at[q, k], send_r.at[q, k],
            device_id=(d, c), device_id_type=MESH)

    def keep_own(q):
        return pltpu.make_async_copy(send_ref.at[q, r], gots[q].at[pl.ds(r * CAP, CAP)], own_s.at[q])

    def hop_right(q, d):
        return pltpu.make_async_remote_copy(
            to_right.at[q, d], to_right.at[q, d], right_s.at[q, d], right_r.at[q, d],
            device_id=(r, lax.rem(c + 1, nc)), device_id_type=MESH)

    def hop_left(q, d):
        return pltpu.make_async_remote_copy(
            to_left.at[q, d], to_left.at[q, d], left_s.at[q, d], left_r.at[q, d],
            device_id=(r, lax.rem(c + nc - 1, nc)), device_id_type=MESH)

    others = [pltpu.make_async_copy(src, dst, in_sem.at[i]) for i, (src, dst) in enumerate(
        ((dest_hbm, dest_ref), (target_hbm, target_ref), (col_hbm, col_ref), (omega_hbm, omega_buf)))]
    for copy in others:
        copy.start()
    for i in range(early):
        fetch(i, FIRST, 0).start()
    for i in range(loads):
        fetch(i, LOADS, LOADS).start()
    signal_all(nr, nc, r, c)
    gram[...] = jnp.zeros_like(gram)
    others[2].wait()
    others[3].wait()

    def multiply(i, carry, size, skip):
        fetch(i, size, skip).wait()
        for local in range(size):
            t = skip + i * size + local
            sums = None
            for g in range(0, groups, 2):
                left = jnp.concatenate([a_buf[t, g], a_buf[t, g + 1]], axis=1)
                right = jnp.concatenate([omega_buf[col_ref[g, t]], omega_buf[col_ref[g + 1, t]]], axis=0)
                product = jnp.dot(left, right, preferred_element_type=jnp.float32)
                sums = product if sums is None else sums + product
            sums = sums.astype(jnp.bfloat16)
            for q in range(chunks):
                parts[q, t] = sums[q * rq:(q + 1) * rq]
        return carry

    lax.fori_loop(0, early, functools.partial(multiply, size=FIRST, skip=0), 0)
    others[0].wait()
    others[1].wait()
    source, rows = place(dest_ref[...], target_ref[...], nr)
    row_ref[...] = rows.reshape(nr, 8, 128)
    meta[...] = jnp.zeros_like(meta)
    meta[:1, :] = source
    to_sources = pltpu.make_async_copy(meta, sources, own_s.at[chunks + 1])
    to_sources.start()
    own_rows = pltpu.make_async_copy(row_ref.at[r], rows_in.at[r], own_s.at[chunks])
    own_rows.start()
    wait_all(nr, nc)
    for k in range(1, nr):
        route(k).start()
    lax.fori_loop(0, loads, functools.partial(multiply, size=LOADS, skip=LOADS), 0)
    own_rows.wait()
    to_sources.wait()
    for q in range(chunks):
        for d in range(nr):
            for k in range(CAP):
                send_ref[q, d, k] = parts[q, sources[0, d * CAP + k]]
        keep_own(q).start()
        if q == 0:
            for k in range(1, nr):
                swap(0, k).start()
    for k in range(1, nr):
        route(k).wait_recv()
    meta[:4, :] = arrange(rows_in[...].reshape(nr * 8, 128), slots)
    to_table = pltpu.make_async_copy(meta, table, own_s.at[chunks + 1])
    to_table.start()
    to_table.wait()

    def in_turn(far, near):
        turns = []
        for q in range(chunks):
            one = [(q, q, d) for d in far]
            if q > 0:
                one.insert(1, (q, q - 1, near))
            turns += one
        return turns + [(chunks - 1, chunks - 1, near)]

    from_first = in_turn(list(range(nc - 1, 1, -1)), 1)
    from_last = in_turn(list(range(nc - 2)), nc - 2)

    def start_ends(now, sends, buffer, hop):
        for n, (at, q, d) in enumerate(sends):
            if at == now:
                if n >= WINDOW:
                    hop(*sends[n - WINDOW][1:]).wait_send()
                buffer[q, d] = term[q % nc, d * RB_DEV:(d + 1) * RB_DEV].astype(jnp.bfloat16)
                hop(q, d).start()

    def collect(q):
        keep_own(q).wait()
        for k in range(1, nr):
            swap(q, k).wait_send()
        if q + 1 < chunks:
            for k in range(1, nr):
                swap(q + 1, k).start()
        for k in range(1, nr):
            swap(q, k).wait_recv()
        got = gots[q]

        def add(k, acc):
            acc = acc * table[1, k].astype(jnp.float32) + got[table[0, k]].astype(jnp.float32)
            prefix[k] = acc
            return acc

        lax.fori_loop(0, slots, add, jnp.zeros((rq, width), jnp.float32), unroll=8)

        @pl.loop(0, blocks, unroll=8)
        def _(b):
            term[q % nc, b] = prefix[table[2, b]] * table[3, b].astype(jnp.float32)

        @pl.when(c == 0)
        def _():
            start_ends(q, from_first, to_right, hop_right)

        @pl.when(c == nc - 1)
        def _():
            start_ends(q, from_last, to_left, hop_left)

    def add_and_send(q, d, buffer, hop):
        hop(q, d).wait_recv()
        mine = term[q % nc, d * RB_DEV:(d + 1) * RB_DEV]
        buffer[q, d] = (buffer[q, d].astype(jnp.float32) + mine).astype(jnp.bfloat16)
        hop(q, d).start()

    def pass_on(q, hops):
        @pl.when(c == hops)
        def _():
            for d in range(nc - 1, hops, -1):
                add_and_send(q, d, to_right, hop_right)

        @pl.when(c == nc - 1 - hops)
        def _():
            for d in range(nc - 1 - hops):
                add_and_send(q, d, to_left, hop_left)

    def finish(q):
        total[...] = term[q % nc, pl.ds(c * RB_DEV, RB_DEV)]

        @pl.when(c > 0)
        def _():
            hop_right(q, c).wait_recv()
            total[...] += to_right[q, c].astype(jnp.float32)

        @pl.when(c < nc - 1)
        def _():
            hop_left(q, c).wait_recv()
            total[...] += to_left[q, c].astype(jnp.float32)

        for b in range(RB_DEV):
            start = b * chunks * rq + q * rq
            sketch_ref[start:start + rq, :] = total[b]
        rows = total[...].reshape(RB_DEV * rq, width)
        gram[...] += dot_tn(rows, rows)

    for q in range(chunks + nc - 1):
        if q < chunks:
            collect(q)
        for hops in range(nc - 2, 0, -1):
            if 0 <= q - hops < chunks:
                pass_on(q - hops, hops)
        if q >= nc - 1:
            finish(q - nc + 1)

    sum_gram(nr, nc, r, c, gram, sketch_ref.at[pl.ds(RB_DEV * order, width)], *refs)
    for k in range(1, nr):
        route(k).wait_send()
    for q in range(chunks):
        for d in range(nc):
            @pl.when(jnp.logical_and(c > 0, c < d))
            def _():
                hop_right(q, d).wait_send()

            @pl.when(jnp.logical_and(c < nc - 1, c > d))
            def _():
                hop_left(q, d).wait_send()

    @pl.when(c == 0)
    def _():
        for send in from_first[-WINDOW:]:
            hop_right(*send[1:]).wait_send()

    @pl.when(c == nc - 1)
    def _():
        for send in from_last[-WINDOW:]:
            hop_left(*send[1:]).wait_send()


def make_sketch(dest, target, col_target, a_blocks, omega, nr, nc):
    targets, _, order, _ = a_blocks.shape
    width = omega.shape[2]
    chunks, rq = CHUNKS, order // CHUNKS
    dma = pltpu.SemaphoreType.DMA
    slots, blocks = nr * CAP, nc * RB_DEV
    hops = pltpu.VMEM((chunks, nc, RB_DEV, rq, width), jnp.bfloat16)
    hbm = pl.BlockSpec(memory_space=pltpu.HBM)
    return pl.pallas_call(
        functools.partial(sketch_kernel, nr, nc),
        out_shape=jax.ShapeDtypeStruct((RB_DEV * order + width, width), jnp.float32),
        in_specs=[hbm] * 5,
        out_specs=VMEM,
        scratch_shapes=[pltpu.VMEM((slots, rq, width), jnp.bfloat16)] * chunks + [
            pltpu.VMEM(dest.shape, jnp.int32),
            pltpu.VMEM(target.shape, jnp.int32),
            pltpu.SMEM(col_target.shape, jnp.int32),
            pltpu.VMEM(a_blocks.shape, a_blocks.dtype),
            pltpu.VMEM(omega.shape, omega.dtype),
            pltpu.VMEM((chunks, targets, rq, width), jnp.bfloat16),
            pltpu.VMEM((chunks, nr, CAP, rq, width), jnp.bfloat16),
            pltpu.VMEM((nr, 8, 128), jnp.int32),
            pltpu.SMEM((8, 128), jnp.int32),
            dma((targets // FIRST,)), dma((4,)),
            pltpu.VMEM((nr, 8, 128), jnp.int32),
            pltpu.VMEM((8, 128), jnp.int32),
            pltpu.SMEM((8, 128), jnp.int32),
            pltpu.VMEM((slots, rq, width), jnp.float32),
            pltpu.VMEM((nc, blocks, rq, width), jnp.float32),
            hops, hops,
            pltpu.VMEM((RB_DEV, rq, width), jnp.float32),
            pltpu.VMEM((width, width), jnp.float32),
            dma((nr,)), dma((nr,)), dma((chunks + 2,)),
            dma((chunks, nr)), dma((chunks, nr)),
            dma((chunks, nc)), dma((chunks, nc)), dma((chunks, nc)), dma((chunks, nc)),
        ] + packed_scratch(nr, nc, width),
        compiler_params=pltpu.CompilerParams(collective_id=1, has_side_effects=True, vmem_limit_bytes=60 << 20),
    )(dest, target, col_target, a_blocks, omega)


def gram_sum_kernel(nr, nc, gram, out_ref, *refs):
    r = lax.axis_index("row")
    c = lax.axis_index("col")
    greet(nr, nc, r, c)
    sum_gram(nr, nc, r, c, gram, out_ref, *refs)


def gram_sum(gram, nr, nc):
    return pl.pallas_call(
        functools.partial(gram_sum_kernel, nr, nc),
        out_shape=jax.ShapeDtypeStruct(gram.shape, jnp.float32),
        in_specs=[VMEM],
        out_specs=VMEM,
        scratch_shapes=packed_scratch(nr, nc, gram.shape[0]),
        compiler_params=pltpu.CompilerParams(collective_id=3, has_side_effects=True, vmem_limit_bytes=8 << 20),
    )(gram)


def eliminate(x):
    rows = x.shape[0]
    shape = (8, x.shape[1])
    groups = [x[i:i + 8, :] for i in range(0, rows, 8)]
    sub = lax.broadcasted_iota(jnp.int32, shape, 0)
    for g in range(rows // 8):
        j = 8 * g
        cols = [[jnp.broadcast_to(groups[i][:, j + l:j + l + 1], shape) for l in range(8)]
                for i in range(g, rows // 8)]
        piv = [[jnp.broadcast_to(cols[0][l][k:k + 1, :], shape) if l >= k else None for l in range(8)] for k in range(8)]
        tops = [jnp.broadcast_to(groups[g][k:k + 1, :], shape) for k in range(8)]
        recip = []
        for k in range(8):
            if k % 2 == 0:
                side = piv[k][k + 1]
                det = piv[k][k] * piv[k + 1][k + 1] - side * side
                recip += [1.0 / piv[k][k], piv[k][k] * (1.0 / det)]
            for m in range(k + 1, 8):
                q = piv[k][m] * recip[k]
                for l in range(m, 8):
                    piv[m][l] = piv[m][l] - q * piv[k][l]
                tops[m] = tops[m] - q * tops[k]
        for i in range(g + 1, rows // 8):
            here = cols[i - g]
            value = groups[i]
            for k in range(8):
                f = here[k] * recip[k]
                for l in range(k + 1, 8):
                    here[l] = here[l] - f * piv[k][l]
                value = value - f * tops[k]
            groups[i] = value
        for k in range(1, 8):
            groups[g] = jnp.where(sub == k, tops[k], groups[g])
    return jnp.concatenate(groups, axis=0)


def factor_gram(gram, left, right, upper, inverse):
    order = gram.shape[0]
    row = lax.broadcasted_iota(jnp.int32, (order, order), 0)
    col = lax.broadcasted_iota(jnp.int32, (order, order), 1)
    only = jnp.where(row == col, gram[...], 0.0)
    diag = jnp.sum(only, axis=0, keepdims=True)
    unit = 1.0 / jnp.sqrt(diag)
    back = diag * unit
    left[...] = gram[...] * (1.0 / jnp.sqrt(jnp.sum(only, axis=1, keepdims=True))) * unit
    right[...] = jnp.where(row == col, unit, 0.0)
    upper[...] = jnp.zeros_like(upper)
    inverse[...] = jnp.zeros_like(inverse)
    lane = lax.broadcasted_iota(jnp.int32, (PANEL, 2 * PANEL), 1)
    prow = lax.broadcasted_iota(jnp.int32, (PANEL, 2 * PANEL), 0)
    for base in range(0, order, PANEL):
        low = base // (2 * PANEL) * 2 * PANEL
        high = low + 2 * PANEL
        here = slice(base, base + PANEL)
        tile = left[here, low:high]
        if base > low:
            tile = pltpu.roll(tile, PANEL, 1)
        x = eliminate(jnp.where(lane < PANEL, tile, (lane - PANEL == prow).astype(jnp.float32)))
        root = 1.0 / jnp.sqrt(jnp.sum(jnp.where(lane == prow, x, 0.0), axis=1, keepdims=True))
        factor = pltpu.roll(x, PANEL, 1)[:, :PANEL]
        u = dot_nn(factor, left[here, low:]) * root
        v = dot_nn(factor, right[here, :high]) * root
        upper[here, low:] = jnp.where(col[here, low:] >= row[here, low:], u * back[:, low:], 0.0)
        inverse[here, :high] = jnp.where(col[here, :high] <= row[here, :high], v, 0.0)
        after = base + PANEL
        if after < order:
            start = after // (2 * PANEL) * 2 * PANEL
            rest = u[:, start - low:]
            left[after:, start:] -= dot_tn(rest, rest)[after - start:]
            right[after:, :high] -= dot_tn(rest, v)[after - start:]


def factor_kernel(scale, sketch, upper_out, factor, inverse, again, left, right):
    order = inverse.shape[0]
    gram = sketch.at[pl.ds(sketch.shape[0] - order, order)]
    factor_gram(gram, left, right, upper_out, inverse)
    factor[...] = upper_out[...] * (1.0 / scale)
    row = lax.broadcasted_iota(jnp.int32, (order, order), 0)
    col = lax.broadcasted_iota(jnp.int32, (order, order), 1)
    diag = jnp.sum(jnp.where(row == col, gram[...], 0.0), axis=0, keepdims=True)
    spread = jnp.sum(inverse[...] * inverse[...], axis=0, keepdims=True) * diag
    mean = jnp.sum(spread) * (1.0 / order)
    again[0] = jnp.where(mean <= INFLATION, 0, 1)


def factor_first(sketch, scale):
    order = sketch.shape[1]
    square = jax.ShapeDtypeStruct((order, order), jnp.float32)
    return pl.pallas_call(
        functools.partial(factor_kernel, scale),
        out_shape=(square, square, square, jax.ShapeDtypeStruct((1,), jnp.int32)),
        in_specs=[VMEM],
        out_specs=(VMEM, VMEM, VMEM, SMEM),
        scratch_shapes=[pltpu.VMEM((order, order), jnp.float32)] * 2,
        compiler_params=pltpu.CompilerParams(vmem_limit_bytes=16 << 20),
    )(sketch)


def apply_kernel(scale, inverse, sketch, basis, ready, sem):
    pieces, step, _ = ready.shape
    matrix = inverse[...] * scale

    def store(i):
        return pltpu.make_async_copy(ready.at[i], basis.at[pl.ds(i * step, step)], sem.at[i])

    for i in range(pieces):
        ready[i] = dot_nt(sketch[i * step:(i + 1) * step, :], matrix)
        store(i).start()
    for i in range(pieces):
        store(i).wait()


def apply_inverse(inverse, sketch, scale):
    rows, width = sketch.shape[0] - sketch.shape[1], sketch.shape[1]
    pieces = 4
    return pl.pallas_call(
        functools.partial(apply_kernel, scale),
        out_shape=jax.ShapeDtypeStruct((rows, width), jnp.float32),
        in_specs=[VMEM, VMEM],
        out_specs=pl.BlockSpec(memory_space=pltpu.HBM),
        scratch_shapes=[pltpu.VMEM((pieces, rows // pieces, width), jnp.float32), pltpu.SemaphoreType.DMA((pieces,))],
        compiler_params=pltpu.CompilerParams(vmem_limit_bytes=16 << 20),
    )(inverse, sketch)


def once_kernel(inverse, sketch, once, second):
    second[...] = jnp.zeros_like(second)
    step = 256

    @pl.loop(0, once.shape[0] // step)
    def _(i):
        part = pl.ds(pl.multiple_of(i * step, step), step)
        rows = dot_nt(sketch[part, :], inverse[...])
        once[part, :] = rows
        second[...] += dot_tn(rows, rows)


def once_pass(inverse, sketch):
    return pl.pallas_call(
        once_kernel,
        out_shape=(
            jax.ShapeDtypeStruct((sketch.shape[0] - sketch.shape[1], sketch.shape[1]), jnp.float32),
            jax.ShapeDtypeStruct(inverse.shape, jnp.float32),
        ),
        in_specs=[VMEM, VMEM],
        out_specs=(VMEM, VMEM),
        compiler_params=pltpu.CompilerParams(vmem_limit_bytes=16 << 20),
    )(inverse, sketch)


def last_kernel(scale, gram, once, upper_one, basis, factor, left, right, upper, inverse):
    factor_gram(gram, left, right, upper, inverse)
    factor[...] = dot_nn(upper[...], upper_one[...]) * (1.0 / scale)
    step = 256

    @pl.loop(0, once.shape[0] // step)
    def _(i):
        part = pl.ds(pl.multiple_of(i * step, step), step)
        basis[part, :] = dot_nt(once[part, :], inverse[...]) * scale


def last_pass(gram, once, upper_one, scale):
    order = gram.shape[0]
    square = pltpu.VMEM((order, order), jnp.float32)
    return pl.pallas_call(
        functools.partial(last_kernel, scale),
        out_shape=(
            jax.ShapeDtypeStruct(once.shape, jnp.float32),
            jax.ShapeDtypeStruct((order, order), jnp.float32),
        ),
        in_specs=[VMEM, VMEM, VMEM],
        out_specs=(VMEM, VMEM),
        scratch_shapes=[square] * 4,
        compiler_params=pltpu.CompilerParams(vmem_limit_bytes=16 << 20),
    )(gram, once, upper_one)


def body(nr, nc, a_blocks, omega, route_dest, row_target, col_target):
    order = a_blocks.shape[2]
    sketch = make_sketch(
        route_dest.T, row_target.reshape(1, -1), col_target.T, a_blocks, omega.reshape(-1, order, omega.shape[1]), nr, nc)
    scale = float(nr * nc * RB_DEV * order) ** 0.5
    upper, factor, inverse, again = factor_first(sketch, scale)

    def orthogonalize_again():
        once, gram_part = once_pass(inverse, sketch)
        return last_pass(gram_sum(gram_part, nr, nc), once, upper, scale)

    def keep_once():
        return apply_inverse(inverse, sketch, scale), factor

    return lax.cond(again[0] != 0, orthogonalize_again, keep_once)


def solution(mesh):
    nr, nc = mesh.shape["row"], mesh.shape["col"]
    return jax.shard_map(
        functools.partial(body, nr, nc),
        mesh=mesh,
        in_specs=(
            P(("row", "col"), None, None, None),
            P("col", None),
            P(("row", "col"), None),
            P(("row", "col")),
            P(("row", "col"), None),
        ),
        out_specs=(P(("row", "col"), None), P()),
        check_vma=False,
    )
```

```python
import functools

import jax
import jax.numpy as jnp
from jax import lax
from jax.experimental import pallas as pl
from jax.experimental.pallas import tpu as pltpu
from jax.sharding import PartitionSpec as P

RB_DEV = 8
CAP = 4
PANEL = 64
LOADS = 8
FIRST = 4
NOWHERE = 1 << 20
INFLATION = 2.0
CHUNKS = 8
WINDOW = 2
MESH = pl.DeviceIdType.MESH
VMEM = pl.BlockSpec(memory_space=pltpu.VMEM)
SMEM = pl.BlockSpec(memory_space=pltpu.SMEM)
HIGH = lax.Precision.HIGHEST


def dot_nn(a, b):
    return lax.dot_general(a, b, (((1,), (0,)), ((), ())), precision=HIGH, preferred_element_type=jnp.float32)


def dot_nt(a, b):
    return lax.dot_general(a, b, (((1,), (1,)), ((), ())), precision=HIGH, preferred_element_type=jnp.float32)


def dot_tn(a, b):
    return lax.dot_general(a, b, (((0,), (0,)), ((), ())), precision=HIGH, preferred_element_type=jnp.float32)


def place(dest, target, owners):
    count = dest.shape[1]
    i = lax.broadcasted_iota(jnp.int32, (count, count), 0)
    j = lax.broadcasted_iota(jnp.int32, (count, count), 1)
    down = jnp.sum(jnp.where(i == j, dest, 0), axis=1, keepdims=True)
    rank = jnp.sum(jnp.logical_and(down == dest, j < i).astype(jnp.int32), axis=1, keepdims=True)
    rank_across = jnp.sum(jnp.where(i == j, rank, 0), axis=0, keepdims=True)
    lane = lax.broadcasted_iota(jnp.int32, (count, 128), 1)
    which = lax.broadcasted_iota(jnp.int32, (count, 128), 0)
    source = jnp.sum(jnp.where(down * CAP + rank == lane, which, 0), axis=0, keepdims=True)
    place_of = lax.broadcasted_iota(jnp.int32, (owners * 8, count), 0)
    here = place_of == dest * 8 + rank_across
    rows = jnp.sum(jnp.where(here, target + 1, 0), axis=1, keepdims=True)
    rows = jnp.where(rows > 0, rows - 1, NOWHERE)
    return source, jnp.broadcast_to(rows, (owners * 8, 128))


def signal_all(nr, nc, r, c):
    barrier = pltpu.get_barrier_semaphore()
    for k in range(1, nr):
        pl.semaphore_signal(barrier, inc=1, device_id=(lax.rem(r + k, nr), c), device_id_type=MESH)
    for k in range(1, nc):
        pl.semaphore_signal(barrier, inc=1, device_id=(r, lax.rem(c + k, nc)), device_id_type=MESH)


def wait_all(nr, nc):
    pl.semaphore_wait(pltpu.get_barrier_semaphore(), nr - 1 + nc - 1)


def greet(nr, nc, r, c):
    signal_all(nr, nc, r, c)
    wait_all(nr, nc)


def reduce_packed(nr, nc, r, c, packed, landed, cols, full, sems):
    a_s, a_r, b_s, b_r, c_s, c_r = sems
    copies, across, back = [], [], []
    for k in range(1, nr):
        d = lax.rem(r + k, nr)
        copies.append(pltpu.make_async_remote_copy(
            packed.at[d], landed.at[k], a_s.at[k], a_r.at[k], device_id=(d, c), device_id_type=MESH))
        copies[-1].start()
    total = packed[r]
    for k in range(1, nr):
        copies[k - 1].wait_recv()
        total = total + landed[k]
    cols[c] = total
    for k in range(1, nc):
        across.append(pltpu.make_async_remote_copy(
            cols.at[c], cols.at[c], b_s.at[k], b_r.at[k], device_id=(r, lax.rem(c + k, nc)), device_id_type=MESH))
        across[-1].start()
    for cp in across:
        cp.wait_recv()
    total = cols[0]
    for k in range(1, nc):
        total = total + cols[k]
    full[r] = total
    for k in range(1, nr):
        back.append(pltpu.make_async_remote_copy(
            full.at[r], full.at[r], c_s.at[k], c_r.at[k], device_id=(lax.rem(r + k, nr), c), device_id_type=MESH))
        back[-1].start()
    for cp in back:
        cp.wait_recv()
    for cp in copies + across + back:
        cp.wait_send()


def packed_scratch(nr, nc, width):
    dma = pltpu.SemaphoreType.DMA
    piece = (width // nr + 8, width // 2)
    return [
        pltpu.VMEM((nr,) + piece, jnp.float32),
        pltpu.VMEM((nr,) + piece, jnp.float32),
        pltpu.VMEM((nc,) + piece, jnp.float32),
        pltpu.VMEM((nr,) + piece, jnp.float32),
        dma((nr,)), dma((nr,)), dma((nc,)), dma((nc,)), dma((nr,)), dma((nr,)),
    ]


def sum_gram(nr, nc, r, c, gram, out_ref, packed, landed, cols, full, *sems):
    half = gram.shape[0] // 2
    main = 2 * half // nr
    row = lax.broadcasted_iota(jnp.int32, (half, half), 0)
    col = lax.broadcasted_iota(jnp.int32, (half, half), 1)
    low = gram[half:, half:]
    mixed = jnp.where(row <= col, gram[:half, :half], pltpu.roll(low, 1, 0))
    for k in range(nr):
        source, start = (gram[:half, half:], k * main) if k < nr // 2 else (mixed, k * main - half)
        packed[k, :main] = source[start:start + main]
        packed[k, main:] = jnp.broadcast_to(low[half - 1:half, :], (8, half))
    reduce_packed(nr, nc, r, c, packed, landed, cols, full, sems)
    side = full[:nr // 2, :main].reshape(half, half)
    mixed = full[nr // 2:, :main].reshape(half, half)
    low = jnp.where(row == half - 1, jnp.broadcast_to(full[0, main:main + 1], (half, half)), pltpu.roll(mixed, half - 1, 0))
    out_ref[:half, :half] = jnp.where(row <= col, mixed, mixed.T)
    out_ref[:half, half:] = side
    out_ref[half:, :half] = side.T
    out_ref[half:, half:] = jnp.where(row >= col, low, low.T)


def arrange(rows, slots):
    count = rows.shape[0]
    i = lax.broadcasted_iota(jnp.int32, rows.shape, 0)
    j = lax.broadcasted_iota(jnp.int32, rows.shape, 1)
    across = jnp.sum(jnp.where(i == j, rows, 0), axis=0, keepdims=True)
    ahead = jnp.logical_or(across < rows, jnp.logical_and(across == rows, j < i))
    ahead = jnp.logical_and(ahead, j < count)
    rank = jnp.sum(ahead.astype(jnp.int32), axis=1, keepdims=True)
    slot = (i // 8) * CAP + lax.rem(i, 8)
    order = jnp.sum(jnp.where(rank == j, slot, 0), axis=0, keepdims=True)
    here = jnp.sum(jnp.where(rank == j, rows, 0), axis=0, keepdims=True)
    before = jnp.sum(jnp.where(rank == j - 1, rows, 0), axis=0, keepdims=True)
    keep = jnp.logical_and(here == before, j[:1] > 0).astype(jnp.int32)
    last = jnp.max(jnp.where(rows == j, rank, -1), axis=0, keepdims=True)
    valid = (last >= 0).astype(jnp.int32)
    order = jnp.minimum(order, slots - 1)
    last = jnp.clip(last, 0, slots - 1)
    return jnp.concatenate([order, keep, last, valid], axis=0)


def sketch_kernel(nr, nc, dest_hbm, target_hbm, col_hbm, a_hbm, omega_hbm, sketch_ref, *refs):
    chunks = CHUNKS
    gots, refs = refs[:chunks], refs[chunks:]
    (dest_ref, target_ref, col_ref, a_buf, omega_buf, parts, send_ref, row_ref, sources, a_sem, in_sem,
     rows_in, meta, table, prefix, term, to_right, to_left, total, gram, row_s, row_r, own_s,
     send_s, send_r, right_s, right_r, left_s, left_r), refs = refs[:29], refs[29:]
    targets, groups, order, _ = a_buf.shape
    rq, width = order // chunks, omega_buf.shape[2]
    slots = nr * CAP
    blocks = nc * RB_DEV
    early = LOADS // FIRST
    loads = targets // LOADS - 1
    r = lax.axis_index("row")
    c = lax.axis_index("col")

    def fetch(i, size, skip):
        part = pl.ds(skip + i * size, size)
        return pltpu.make_async_copy(a_hbm.at[part], a_buf.at[part], a_sem.at[skip // FIRST + i])

    def route(k):
        d = lax.rem(r + k, nr)
        return pltpu.make_async_remote_copy(
            row_ref.at[d], rows_in.at[r], row_s.at[k], row_r.at[k], device_id=(d, c), device_id_type=MESH)

    def swap(q, k):
        d = lax.rem(r + k, nr)
        return pltpu.make_async_remote_copy(
            send_ref.at[q, d], gots[q].at[pl.ds(r * CAP, CAP)], send_s.at[q, k], send_r.at[q, k],
            device_id=(d, c), device_id_type=MESH)

    def keep_own(q):
        return pltpu.make_async_copy(send_ref.at[q, r], gots[q].at[pl.ds(r * CAP, CAP)], own_s.at[q])

    def hop_right(q, d):
        return pltpu.make_async_remote_copy(
            to_right.at[q, d], to_right.at[q, d], right_s.at[q, d], right_r.at[q, d],
            device_id=(r, lax.rem(c + 1, nc)), device_id_type=MESH)

    def hop_left(q, d):
        return pltpu.make_async_remote_copy(
            to_left.at[q, d], to_left.at[q, d], left_s.at[q, d], left_r.at[q, d],
            device_id=(r, lax.rem(c + nc - 1, nc)), device_id_type=MESH)

    others = [pltpu.make_async_copy(src, dst, in_sem.at[i]) for i, (src, dst) in enumerate(
        ((dest_hbm, dest_ref), (target_hbm, target_ref), (col_hbm, col_ref), (omega_hbm, omega_buf)))]
    for copy in others:
        copy.start()
    for i in range(early):
        fetch(i, FIRST, 0).start()
    for i in range(loads):
        fetch(i, LOADS, LOADS).start()
    signal_all(nr, nc, r, c)
    gram[...] = jnp.zeros_like(gram)
    others[2].wait()
    others[3].wait()

    def multiply(i, carry, size, skip):
        fetch(i, size, skip).wait()
        for local in range(size):
            t = skip + i * size + local
            sums = None
            for g in range(0, groups, 2):
                left = jnp.concatenate([a_buf[t, g], a_buf[t, g + 1]], axis=1)
                right = jnp.concatenate([omega_buf[col_ref[g, t]], omega_buf[col_ref[g + 1, t]]], axis=0)
                product = jnp.dot(left, right, preferred_element_type=jnp.float32)
                sums = product if sums is None else sums + product
            sums = sums.astype(jnp.bfloat16)
            for q in range(chunks):
                parts[q, t] = sums[q * rq:(q + 1) * rq]
        return carry

    lax.fori_loop(0, early, functools.partial(multiply, size=FIRST, skip=0), 0)
    others[0].wait()
    others[1].wait()
    source, rows = place(dest_ref[...], target_ref[...], nr)
    row_ref[...] = rows.reshape(nr, 8, 128)
    meta[...] = jnp.zeros_like(meta)
    meta[:1, :] = source
    to_sources = pltpu.make_async_copy(meta, sources, own_s.at[chunks + 1])
    to_sources.start()
    own_rows = pltpu.make_async_copy(row_ref.at[r], rows_in.at[r], own_s.at[chunks])
    own_rows.start()
    wait_all(nr, nc)
    for k in range(1, nr):
        route(k).start()
    lax.fori_loop(0, loads, functools.partial(multiply, size=LOADS, skip=LOADS), 0)
    own_rows.wait()
    to_sources.wait()
    for q in range(chunks):
        for d in range(nr):
            for k in range(CAP):
                send_ref[q, d, k] = parts[q, sources[0, d * CAP + k]]
        keep_own(q).start()
        if q == 0:
            for k in range(1, nr):
                swap(0, k).start()
    for k in range(1, nr):
        route(k).wait_recv()
    meta[:4, :] = arrange(rows_in[...].reshape(nr * 8, 128), slots)
    to_table = pltpu.make_async_copy(meta, table, own_s.at[chunks + 1])
    to_table.start()
    to_table.wait()

    def in_turn(far, near):
        turns = []
        for q in range(chunks):
            one = [(q, q, d) for d in far]
            if q > 0:
                one.insert(1, (q, q - 1, near))
            turns += one
        return turns + [(chunks - 1, chunks - 1, near)]

    from_first = in_turn(list(range(nc - 1, 1, -1)), 1)
    from_last = in_turn(list(range(nc - 2)), nc - 2)

    def start_ends(now, sends, buffer, hop):
        for n, (at, q, d) in enumerate(sends):
            if at == now:
                if n >= WINDOW:
                    hop(*sends[n - WINDOW][1:]).wait_send()
                buffer[q, d] = term[q % nc, d * RB_DEV:(d + 1) * RB_DEV].astype(jnp.bfloat16)
                hop(q, d).start()

    def collect(q):
        keep_own(q).wait()
        for k in range(1, nr):
            swap(q, k).wait_send()
        if q + 1 < chunks:
            for k in range(1, nr):
                swap(q + 1, k).start()
        for k in range(1, nr):
            swap(q, k).wait_recv()
        got = gots[q]

        def add(k, acc):
            acc = acc * table[1, k].astype(jnp.float32) + got[table[0, k]].astype(jnp.float32)
            prefix[k] = acc
            return acc

        lax.fori_loop(0, slots, add, jnp.zeros((rq, width), jnp.float32), unroll=8)

        @pl.loop(0, blocks, unroll=8)
        def _(b):
            term[q % nc, b] = prefix[table[2, b]] * table[3, b].astype(jnp.float32)

        @pl.when(c == 0)
        def _():
            start_ends(q, from_first, to_right, hop_right)

        @pl.when(c == nc - 1)
        def _():
            start_ends(q, from_last, to_left, hop_left)

    def add_and_send(q, d, buffer, hop):
        hop(q, d).wait_recv()
        mine = term[q % nc, d * RB_DEV:(d + 1) * RB_DEV]
        buffer[q, d] = (buffer[q, d].astype(jnp.float32) + mine).astype(jnp.bfloat16)
        hop(q, d).start()

    def pass_on(q, hops):
        @pl.when(c == hops)
        def _():
            for d in range(nc - 1, hops, -1):
                add_and_send(q, d, to_right, hop_right)

        @pl.when(c == nc - 1 - hops)
        def _():
            for d in range(nc - 1 - hops):
                add_and_send(q, d, to_left, hop_left)

    def finish(q):
        total[...] = term[q % nc, pl.ds(c * RB_DEV, RB_DEV)]

        @pl.when(c > 0)
        def _():
            hop_right(q, c).wait_recv()
            total[...] += to_right[q, c].astype(jnp.float32)

        @pl.when(c < nc - 1)
        def _():
            hop_left(q, c).wait_recv()
            total[...] += to_left[q, c].astype(jnp.float32)

        for b in range(RB_DEV):
            start = b * chunks * rq + q * rq
            sketch_ref[start:start + rq, :] = total[b]
        rows = total[...].reshape(RB_DEV * rq, width)
        gram[...] += dot_tn(rows, rows)

    for q in range(chunks + nc - 1):
        if q < chunks:
            collect(q)
        if q == chunks:
            finish(q - nc + 1)
        for hops in range(nc - 2, 0, -1):
            if 0 <= q - hops < chunks:
                pass_on(q - hops, hops)
        if q >= nc - 1 and q != chunks:
            finish(q - nc + 1)

    sum_gram(nr, nc, r, c, gram, sketch_ref.at[pl.ds(RB_DEV * order, width)], *refs)
    for k in range(1, nr):
        route(k).wait_send()
    for q in range(chunks):
        for d in range(nc):
            @pl.when(jnp.logical_and(c > 0, c < d))
            def _():
                hop_right(q, d).wait_send()

            @pl.when(jnp.logical_and(c < nc - 1, c > d))
            def _():
                hop_left(q, d).wait_send()

    @pl.when(c == 0)
    def _():
        for send in from_first[-WINDOW:]:
            hop_right(*send[1:]).wait_send()

    @pl.when(c == nc - 1)
    def _():
        for send in from_last[-WINDOW:]:
            hop_left(*send[1:]).wait_send()


def make_sketch(dest, target, col_target, a_blocks, omega, nr, nc):
    targets, _, order, _ = a_blocks.shape
    width = omega.shape[2]
    chunks, rq = CHUNKS, order // CHUNKS
    dma = pltpu.SemaphoreType.DMA
    slots, blocks = nr * CAP, nc * RB_DEV
    hops = pltpu.VMEM((chunks, nc, RB_DEV, rq, width), jnp.bfloat16)
    hbm = pl.BlockSpec(memory_space=pltpu.HBM)
    return pl.pallas_call(
        functools.partial(sketch_kernel, nr, nc),
        out_shape=jax.ShapeDtypeStruct((RB_DEV * order + width, width), jnp.float32),
        in_specs=[hbm] * 5,
        out_specs=VMEM,
        scratch_shapes=[pltpu.VMEM((slots, rq, width), jnp.bfloat16)] * chunks + [
            pltpu.VMEM(dest.shape, jnp.int32),
            pltpu.VMEM(target.shape, jnp.int32),
            pltpu.SMEM(col_target.shape, jnp.int32),
            pltpu.VMEM(a_blocks.shape, a_blocks.dtype),
            pltpu.VMEM(omega.shape, omega.dtype),
            pltpu.VMEM((chunks, targets, rq, width), jnp.bfloat16),
            pltpu.VMEM((chunks, nr, CAP, rq, width), jnp.bfloat16),
            pltpu.VMEM((nr, 8, 128), jnp.int32),
            pltpu.SMEM((8, 128), jnp.int32),
            dma((targets // FIRST,)), dma((4,)),
            pltpu.VMEM((nr, 8, 128), jnp.int32),
            pltpu.VMEM((8, 128), jnp.int32),
            pltpu.SMEM((8, 128), jnp.int32),
            pltpu.VMEM((slots, rq, width), jnp.float32),
            pltpu.VMEM((nc, blocks, rq, width), jnp.float32),
            hops, hops,
            pltpu.VMEM((RB_DEV, rq, width), jnp.float32),
            pltpu.VMEM((width, width), jnp.float32),
            dma((nr,)), dma((nr,)), dma((chunks + 2,)),
            dma((chunks, nr)), dma((chunks, nr)),
            dma((chunks, nc)), dma((chunks, nc)), dma((chunks, nc)), dma((chunks, nc)),
        ] + packed_scratch(nr, nc, width),
        compiler_params=pltpu.CompilerParams(collective_id=1, has_side_effects=True, vmem_limit_bytes=60 << 20),
    )(dest, target, col_target, a_blocks, omega)


def gram_sum_kernel(nr, nc, gram, out_ref, *refs):
    r = lax.axis_index("row")
    c = lax.axis_index("col")
    greet(nr, nc, r, c)
    sum_gram(nr, nc, r, c, gram, out_ref, *refs)


def gram_sum(gram, nr, nc):
    return pl.pallas_call(
        functools.partial(gram_sum_kernel, nr, nc),
        out_shape=jax.ShapeDtypeStruct(gram.shape, jnp.float32),
        in_specs=[VMEM],
        out_specs=VMEM,
        scratch_shapes=packed_scratch(nr, nc, gram.shape[0]),
        compiler_params=pltpu.CompilerParams(collective_id=3, has_side_effects=True, vmem_limit_bytes=8 << 20),
    )(gram)


def eliminate(x):
    rows = x.shape[0]
    shape = (8, x.shape[1])
    groups = [x[i:i + 8, :] for i in range(0, rows, 8)]
    sub = lax.broadcasted_iota(jnp.int32, shape, 0)
    for g in range(rows // 8):
        j = 8 * g
        cols = [[jnp.broadcast_to(groups[i][:, j + l:j + l + 1], shape) for l in range(8)]
                for i in range(g, rows // 8)]
        piv = [[jnp.broadcast_to(cols[0][l][k:k + 1, :], shape) if l >= k else None for l in range(8)] for k in range(8)]
        tops = [jnp.broadcast_to(groups[g][k:k + 1, :], shape) for k in range(8)]
        recip = []
        for k in range(8):
            if k % 2 == 0:
                side = piv[k][k + 1]
                det = piv[k][k] * piv[k + 1][k + 1] - side * side
                recip += [1.0 / piv[k][k], piv[k][k] * (1.0 / det)]
            for m in range(k + 1, 8):
                q = piv[k][m] * recip[k]
                for l in range(m, 8):
                    piv[m][l] = piv[m][l] - q * piv[k][l]
                tops[m] = tops[m] - q * tops[k]
        for i in range(g + 1, rows // 8):
            here = cols[i - g]
            value = groups[i]
            for k in range(8):
                f = here[k] * recip[k]
                for l in range(k + 1, 8):
                    here[l] = here[l] - f * piv[k][l]
                value = value - f * tops[k]
            groups[i] = value
        for k in range(1, 8):
            groups[g] = jnp.where(sub == k, tops[k], groups[g])
    return jnp.concatenate(groups, axis=0)


def factor_gram(gram, left, right, upper, inverse):
    order = gram.shape[0]
    row = lax.broadcasted_iota(jnp.int32, (order, order), 0)
    col = lax.broadcasted_iota(jnp.int32, (order, order), 1)
    only = jnp.where(row == col, gram[...], 0.0)
    diag = jnp.sum(only, axis=0, keepdims=True)
    unit = 1.0 / jnp.sqrt(diag)
    back = diag * unit
    left[...] = gram[...] * (1.0 / jnp.sqrt(jnp.sum(only, axis=1, keepdims=True))) * unit
    right[...] = jnp.where(row == col, unit, 0.0)
    upper[...] = jnp.zeros_like(upper)
    inverse[...] = jnp.zeros_like(inverse)
    lane = lax.broadcasted_iota(jnp.int32, (PANEL, 2 * PANEL), 1)
    prow = lax.broadcasted_iota(jnp.int32, (PANEL, 2 * PANEL), 0)
    for base in range(0, order, PANEL):
        low = base // (2 * PANEL) * 2 * PANEL
        high = low + 2 * PANEL
        here = slice(base, base + PANEL)
        tile = left[here, low:high]
        if base > low:
            tile = pltpu.roll(tile, PANEL, 1)
        x = eliminate(jnp.where(lane < PANEL, tile, (lane - PANEL == prow).astype(jnp.float32)))
        root = 1.0 / jnp.sqrt(jnp.sum(jnp.where(lane == prow, x, 0.0), axis=1, keepdims=True))
        factor = pltpu.roll(x, PANEL, 1)[:, :PANEL]
        u = dot_nn(factor, left[here, low:]) * root
        v = dot_nn(factor, right[here, :high]) * root
        upper[here, low:] = jnp.where(col[here, low:] >= row[here, low:], u * back[:, low:], 0.0)
        inverse[here, :high] = jnp.where(col[here, :high] <= row[here, :high], v, 0.0)
        after = base + PANEL
        if after < order:
            start = after // (2 * PANEL) * 2 * PANEL
            rest = u[:, start - low:]
            left[after:, start:] -= dot_tn(rest, rest)[after - start:]
            right[after:, :high] -= dot_tn(rest, v)[after - start:]


def factor_kernel(scale, sketch, upper_out, factor, inverse, again, left, right):
    order = inverse.shape[0]
    gram = sketch.at[pl.ds(sketch.shape[0] - order, order)]
    factor_gram(gram, left, right, upper_out, inverse)
    factor[...] = upper_out[...] * (1.0 / scale)
    row = lax.broadcasted_iota(jnp.int32, (order, order), 0)
    col = lax.broadcasted_iota(jnp.int32, (order, order), 1)
    diag = jnp.sum(jnp.where(row == col, gram[...], 0.0), axis=0, keepdims=True)
    spread = jnp.sum(inverse[...] * inverse[...], axis=0, keepdims=True) * diag
    mean = jnp.sum(spread) * (1.0 / order)
    again[0] = jnp.where(mean <= INFLATION, 0, 1)


def factor_first(sketch, scale):
    order = sketch.shape[1]
    square = jax.ShapeDtypeStruct((order, order), jnp.float32)
    return pl.pallas_call(
        functools.partial(factor_kernel, scale),
        out_shape=(square, square, square, jax.ShapeDtypeStruct((1,), jnp.int32)),
        in_specs=[VMEM],
        out_specs=(VMEM, VMEM, VMEM, SMEM),
        scratch_shapes=[pltpu.VMEM((order, order), jnp.float32)] * 2,
        compiler_params=pltpu.CompilerParams(vmem_limit_bytes=16 << 20),
    )(sketch)


def apply_kernel(scale, inverse, sketch, basis, ready, sem):
    pieces, step, _ = ready.shape
    matrix = inverse[...] * scale

    def store(i):
        return pltpu.make_async_copy(ready.at[i], basis.at[pl.ds(i * step, step)], sem.at[i])

    for i in range(pieces):
        ready[i] = dot_nt(sketch[i * step:(i + 1) * step, :], matrix)
        store(i).start()
    for i in range(pieces):
        store(i).wait()


def apply_inverse(inverse, sketch, scale):
    rows, width = sketch.shape[0] - sketch.shape[1], sketch.shape[1]
    pieces = 4
    return pl.pallas_call(
        functools.partial(apply_kernel, scale),
        out_shape=jax.ShapeDtypeStruct((rows, width), jnp.float32),
        in_specs=[VMEM, VMEM],
        out_specs=pl.BlockSpec(memory_space=pltpu.HBM),
        scratch_shapes=[pltpu.VMEM((pieces, rows // pieces, width), jnp.float32), pltpu.SemaphoreType.DMA((pieces,))],
        compiler_params=pltpu.CompilerParams(vmem_limit_bytes=16 << 20),
    )(inverse, sketch)


def once_kernel(inverse, sketch, once, second):
    second[...] = jnp.zeros_like(second)
    step = 256

    @pl.loop(0, once.shape[0] // step)
    def _(i):
        part = pl.ds(pl.multiple_of(i * step, step), step)
        rows = dot_nt(sketch[part, :], inverse[...])
        once[part, :] = rows
        second[...] += dot_tn(rows, rows)


def once_pass(inverse, sketch):
    return pl.pallas_call(
        once_kernel,
        out_shape=(
            jax.ShapeDtypeStruct((sketch.shape[0] - sketch.shape[1], sketch.shape[1]), jnp.float32),
            jax.ShapeDtypeStruct(inverse.shape, jnp.float32),
        ),
        in_specs=[VMEM, VMEM],
        out_specs=(VMEM, VMEM),
        compiler_params=pltpu.CompilerParams(vmem_limit_bytes=16 << 20),
    )(inverse, sketch)


def last_kernel(scale, gram, once, upper_one, basis, factor, left, right, upper, inverse):
    factor_gram(gram, left, right, upper, inverse)
    factor[...] = dot_nn(upper[...], upper_one[...]) * (1.0 / scale)
    step = 256

    @pl.loop(0, once.shape[0] // step)
    def _(i):
        part = pl.ds(pl.multiple_of(i * step, step), step)
        basis[part, :] = dot_nt(once[part, :], inverse[...]) * scale


def last_pass(gram, once, upper_one, scale):
    order = gram.shape[0]
    square = pltpu.VMEM((order, order), jnp.float32)
    return pl.pallas_call(
        functools.partial(last_kernel, scale),
        out_shape=(
            jax.ShapeDtypeStruct(once.shape, jnp.float32),
            jax.ShapeDtypeStruct((order, order), jnp.float32),
        ),
        in_specs=[VMEM, VMEM, VMEM],
        out_specs=(VMEM, VMEM),
        scratch_shapes=[square] * 4,
        compiler_params=pltpu.CompilerParams(vmem_limit_bytes=16 << 20),
    )(gram, once, upper_one)


def body(nr, nc, a_blocks, omega, route_dest, row_target, col_target):
    order = a_blocks.shape[2]
    sketch = make_sketch(
        route_dest.T, row_target.reshape(1, -1), col_target.T, a_blocks, omega.reshape(-1, order, omega.shape[1]), nr, nc)
    scale = float(nr * nc * RB_DEV * order) ** 0.5
    upper, factor, inverse, again = factor_first(sketch, scale)

    def orthogonalize_again():
        once, gram_part = once_pass(inverse, sketch)
        return last_pass(gram_sum(gram_part, nr, nc), once, upper, scale)

    def keep_once():
        return apply_inverse(inverse, sketch, scale), factor

    return lax.cond(again[0] != 0, orthogonalize_again, keep_once)


def solution(mesh):
    nr, nc = mesh.shape["row"], mesh.shape["col"]
    return jax.shard_map(
        functools.partial(body, nr, nc),
        mesh=mesh,
        in_specs=(
            P(("row", "col"), None, None, None),
            P("col", None),
            P(("row", "col"), None),
            P(("row", "col")),
            P(("row", "col"), None),
        ),
        out_specs=(P(("row", "col"), None), P()),
        check_vma=False,
    )
```

```python
import functools

import jax
import jax.numpy as jnp
from jax import lax
from jax.experimental import pallas as pl
from jax.experimental.pallas import tpu as pltpu
from jax.sharding import PartitionSpec as P

RB_DEV = 8
CAP = 4
PANEL = 64
LOADS = 8
FIRST = 4
NOWHERE = 1 << 20
INFLATION = 2.0
CHUNKS = 8
WINDOW = 2
MESH = pl.DeviceIdType.MESH
VMEM = pl.BlockSpec(memory_space=pltpu.VMEM)
SMEM = pl.BlockSpec(memory_space=pltpu.SMEM)
HIGH = lax.Precision.HIGHEST


def dot_nn(a, b):
    return lax.dot_general(a, b, (((1,), (0,)), ((), ())), precision=HIGH, preferred_element_type=jnp.float32)


def dot_nt(a, b):
    return lax.dot_general(a, b, (((1,), (1,)), ((), ())), precision=HIGH, preferred_element_type=jnp.float32)


def dot_tn(a, b):
    return lax.dot_general(a, b, (((0,), (0,)), ((), ())), precision=HIGH, preferred_element_type=jnp.float32)


def place(dest, target, owners):
    count = dest.shape[1]
    i = lax.broadcasted_iota(jnp.int32, (count, count), 0)
    j = lax.broadcasted_iota(jnp.int32, (count, count), 1)
    down = jnp.sum(jnp.where(i == j, dest, 0), axis=1, keepdims=True)
    rank = jnp.sum(jnp.logical_and(down == dest, j < i).astype(jnp.int32), axis=1, keepdims=True)
    rank_across = jnp.sum(jnp.where(i == j, rank, 0), axis=0, keepdims=True)
    lane = lax.broadcasted_iota(jnp.int32, (count, 128), 1)
    which = lax.broadcasted_iota(jnp.int32, (count, 128), 0)
    source = jnp.sum(jnp.where(down * CAP + rank == lane, which, 0), axis=0, keepdims=True)
    place_of = lax.broadcasted_iota(jnp.int32, (owners * 8, count), 0)
    here = place_of == dest * 8 + rank_across
    rows = jnp.sum(jnp.where(here, target + 1, 0), axis=1, keepdims=True)
    rows = jnp.where(rows > 0, rows - 1, NOWHERE)
    return source, jnp.broadcast_to(rows, (owners * 8, 128))


def signal_all(nr, nc, r, c):
    barrier = pltpu.get_barrier_semaphore()
    for k in range(1, nr):
        pl.semaphore_signal(barrier, inc=1, device_id=(lax.rem(r + k, nr), c), device_id_type=MESH)
    for k in range(1, nc):
        pl.semaphore_signal(barrier, inc=1, device_id=(r, lax.rem(c + k, nc)), device_id_type=MESH)


def wait_all(nr, nc):
    pl.semaphore_wait(pltpu.get_barrier_semaphore(), nr - 1 + nc - 1)


def greet(nr, nc, r, c):
    signal_all(nr, nc, r, c)
    wait_all(nr, nc)


def reduce_packed(nr, nc, r, c, packed, landed, cols, full, sems):
    a_s, a_r, b_s, b_r, c_s, c_r = sems
    copies, across, back = [], [], []
    for k in range(1, nr):
        d = lax.rem(r + k, nr)
        copies.append(pltpu.make_async_remote_copy(
            packed.at[d], landed.at[k], a_s.at[k], a_r.at[k], device_id=(d, c), device_id_type=MESH))
        copies[-1].start()
    total = packed[r]
    for k in range(1, nr):
        copies[k - 1].wait_recv()
        total = total + landed[k]
    cols[c] = total
    for k in range(1, nc):
        across.append(pltpu.make_async_remote_copy(
            cols.at[c], cols.at[c], b_s.at[k], b_r.at[k], device_id=(r, lax.rem(c + k, nc)), device_id_type=MESH))
        across[-1].start()
    for cp in across:
        cp.wait_recv()
    total = cols[0]
    for k in range(1, nc):
        total = total + cols[k]
    full[r] = total
    for k in range(1, nr):
        back.append(pltpu.make_async_remote_copy(
            full.at[r], full.at[r], c_s.at[k], c_r.at[k], device_id=(lax.rem(r + k, nr), c), device_id_type=MESH))
        back[-1].start()
    for cp in back:
        cp.wait_recv()
    for cp in copies + across + back:
        cp.wait_send()


def packed_scratch(nr, nc, width):
    dma = pltpu.SemaphoreType.DMA
    piece = (width // nr + 8, width // 2)
    return [
        pltpu.VMEM((nr,) + piece, jnp.float32),
        pltpu.VMEM((nr,) + piece, jnp.float32),
        pltpu.VMEM((nc,) + piece, jnp.float32),
        pltpu.VMEM((nr,) + piece, jnp.float32),
        dma((nr,)), dma((nr,)), dma((nc,)), dma((nc,)), dma((nr,)), dma((nr,)),
    ]


def sum_gram(nr, nc, r, c, gram, out_ref, packed, landed, cols, full, *sems):
    half = gram.shape[0] // 2
    main = 2 * half // nr
    row = lax.broadcasted_iota(jnp.int32, (half, half), 0)
    col = lax.broadcasted_iota(jnp.int32, (half, half), 1)
    low = gram[half:, half:]
    mixed = jnp.where(row <= col, gram[:half, :half], pltpu.roll(low, 1, 0))
    for k in range(nr):
        source, start = (gram[:half, half:], k * main) if k < nr // 2 else (mixed, k * main - half)
        packed[k, :main] = source[start:start + main]
        packed[k, main:] = jnp.broadcast_to(low[half - 1:half, :], (8, half))
    reduce_packed(nr, nc, r, c, packed, landed, cols, full, sems)
    side = full[:nr // 2, :main].reshape(half, half)
    mixed = full[nr // 2:, :main].reshape(half, half)
    low = jnp.where(row == half - 1, jnp.broadcast_to(full[0, main:main + 1], (half, half)), pltpu.roll(mixed, half - 1, 0))
    out_ref[:half, :half] = jnp.where(row <= col, mixed, mixed.T)
    out_ref[:half, half:] = side
    out_ref[half:, :half] = side.T
    out_ref[half:, half:] = jnp.where(row >= col, low, low.T)


def arrange(rows, slots):
    count = rows.shape[0]
    i = lax.broadcasted_iota(jnp.int32, rows.shape, 0)
    j = lax.broadcasted_iota(jnp.int32, rows.shape, 1)
    across = jnp.sum(jnp.where(i == j, rows, 0), axis=0, keepdims=True)
    ahead = jnp.logical_or(across < rows, jnp.logical_and(across == rows, j < i))
    ahead = jnp.logical_and(ahead, j < count)
    rank = jnp.sum(ahead.astype(jnp.int32), axis=1, keepdims=True)
    slot = (i // 8) * CAP + lax.rem(i, 8)
    order = jnp.sum(jnp.where(rank == j, slot, 0), axis=0, keepdims=True)
    here = jnp.sum(jnp.where(rank == j, rows, 0), axis=0, keepdims=True)
    before = jnp.sum(jnp.where(rank == j - 1, rows, 0), axis=0, keepdims=True)
    keep = jnp.logical_and(here == before, j[:1] > 0).astype(jnp.int32)
    last = jnp.max(jnp.where(rows == j, rank, -1), axis=0, keepdims=True)
    valid = (last >= 0).astype(jnp.int32)
    order = jnp.minimum(order, slots - 1)
    last = jnp.clip(last, 0, slots - 1)
    return jnp.concatenate([order, keep, last, valid], axis=0)


def sketch_kernel(nr, nc, dest_hbm, target_hbm, col_hbm, a_hbm, omega_hbm, sketch_ref, *refs):
    chunks = CHUNKS
    gots, refs = refs[:chunks], refs[chunks:]
    (dest_ref, target_ref, col_ref, a_buf, omega_buf, parts, send_ref, row_ref, sources, a_sem, in_sem,
     rows_in, meta, table, prefix, term, to_right, to_left, total, gram, row_s, row_r, own_s,
     send_s, send_r, right_s, right_r, left_s, left_r), refs = refs[:29], refs[29:]
    targets, groups, order, _ = a_buf.shape
    rq, width = order // chunks, omega_buf.shape[2]
    slots = nr * CAP
    blocks = nc * RB_DEV
    early = LOADS // FIRST
    loads = targets // LOADS - 1
    r = lax.axis_index("row")
    c = lax.axis_index("col")

    def fetch(i, size, skip):
        part = pl.ds(skip + i * size, size)
        return pltpu.make_async_copy(a_hbm.at[part], a_buf.at[part], a_sem.at[skip // FIRST + i])

    def route(k):
        d = lax.rem(r + k, nr)
        return pltpu.make_async_remote_copy(
            row_ref.at[d], rows_in.at[r], row_s.at[k], row_r.at[k], device_id=(d, c), device_id_type=MESH)

    def swap(q, k):
        d = lax.rem(r + k, nr)
        return pltpu.make_async_remote_copy(
            send_ref.at[q, d], gots[q].at[pl.ds(r * CAP, CAP)], send_s.at[q, k], send_r.at[q, k],
            device_id=(d, c), device_id_type=MESH)

    def keep_own(q):
        return pltpu.make_async_copy(send_ref.at[q, r], gots[q].at[pl.ds(r * CAP, CAP)], own_s.at[q])

    def hop_right(q, d):
        return pltpu.make_async_remote_copy(
            to_right.at[q, d], to_right.at[q, d], right_s.at[q, d], right_r.at[q, d],
            device_id=(r, lax.rem(c + 1, nc)), device_id_type=MESH)

    def hop_left(q, d):
        return pltpu.make_async_remote_copy(
            to_left.at[q, d], to_left.at[q, d], left_s.at[q, d], left_r.at[q, d],
            device_id=(r, lax.rem(c + nc - 1, nc)), device_id_type=MESH)

    others = [pltpu.make_async_copy(src, dst, in_sem.at[i]) for i, (src, dst) in enumerate(
        ((dest_hbm, dest_ref), (target_hbm, target_ref), (col_hbm, col_ref), (omega_hbm, omega_buf)))]
    for copy in others:
        copy.start()
    for i in range(early):
        fetch(i, FIRST, 0).start()
    for i in range(loads):
        fetch(i, LOADS, LOADS).start()
    signal_all(nr, nc, r, c)
    gram[...] = jnp.zeros_like(gram)
    others[2].wait()
    others[3].wait()

    def multiply(i, carry, size, skip):
        fetch(i, size, skip).wait()
        for local in range(size):
            t = skip + i * size + local
            sums = None
            for g in range(0, groups, 2):
                left = jnp.concatenate([a_buf[t, g], a_buf[t, g + 1]], axis=1)
                right = jnp.concatenate([omega_buf[col_ref[g, t]], omega_buf[col_ref[g + 1, t]]], axis=0)
                product = jnp.dot(left, right, preferred_element_type=jnp.float32)
                sums = product if sums is None else sums + product
            sums = sums.astype(jnp.bfloat16)
            for q in range(chunks):
                parts[q, t] = sums[q * rq:(q + 1) * rq]
        return carry

    lax.fori_loop(0, early, functools.partial(multiply, size=FIRST, skip=0), 0)
    others[0].wait()
    others[1].wait()
    source, rows = place(dest_ref[...], target_ref[...], nr)
    row_ref[...] = rows.reshape(nr, 8, 128)
    meta[...] = jnp.zeros_like(meta)
    meta[:1, :] = source
    to_sources = pltpu.make_async_copy(meta, sources, own_s.at[chunks + 1])
    to_sources.start()
    own_rows = pltpu.make_async_copy(row_ref.at[r], rows_in.at[r], own_s.at[chunks])
    own_rows.start()
    wait_all(nr, nc)
    for k in range(1, nr):
        route(k).start()
    lax.fori_loop(0, loads, functools.partial(multiply, size=LOADS, skip=LOADS), 0)
    own_rows.wait()
    to_sources.wait()
    for q in range(chunks):
        for d in range(nr):
            for k in range(CAP):
                send_ref[q, d, k] = parts[q, sources[0, d * CAP + k]]
        keep_own(q).start()
        if q == 0:
            for k in range(1, nr):
                swap(0, k).start()
    for k in range(1, nr):
        route(k).wait_recv()
    meta[:4, :] = arrange(rows_in[...].reshape(nr * 8, 128), slots)
    to_table = pltpu.make_async_copy(meta, table, own_s.at[chunks + 1])
    to_table.start()
    to_table.wait()

    def in_turn(far, near):
        turns = []
        for q in range(chunks):
            one = [(q, q, d) for d in far]
            if q > 0:
                one.insert(1, (q, q - 1, near))
            turns += one
        return turns + [(chunks - 1, chunks - 1, near)]

    from_first = in_turn(list(range(nc - 1, 1, -1)), 1)
    from_last = in_turn(list(range(nc - 2)), nc - 2)

    def start_ends(now, sends, buffer, hop):
        for n, (at, q, d) in enumerate(sends):
            if at == now:
                if n >= WINDOW:
                    hop(*sends[n - WINDOW][1:]).wait_send()
                buffer[q, d] = term[q % nc, d * RB_DEV:(d + 1) * RB_DEV].astype(jnp.bfloat16)
                hop(q, d).start()

    def collect(q):
        keep_own(q).wait()
        for k in range(1, nr):
            swap(q, k).wait_send()
        if q + 1 < chunks:
            for k in range(1, nr):
                swap(q + 1, k).start()
        for k in range(1, nr):
            swap(q, k).wait_recv()
        got = gots[q]

        def add(k, acc):
            acc = acc * table[1, k].astype(jnp.float32) + got[table[0, k]].astype(jnp.float32)
            prefix[k] = acc
            return acc

        lax.fori_loop(0, slots, add, jnp.zeros((rq, width), jnp.float32), unroll=16)

        @pl.loop(0, blocks, unroll=16)
        def _(b):
            term[q % nc, b] = prefix[table[2, b]] * table[3, b].astype(jnp.float32)

        @pl.when(c == 0)
        def _():
            start_ends(q, from_first, to_right, hop_right)

        @pl.when(c == nc - 1)
        def _():
            start_ends(q, from_last, to_left, hop_left)

    def add_and_send(q, d, buffer, hop):
        hop(q, d).wait_recv()
        mine = term[q % nc, d * RB_DEV:(d + 1) * RB_DEV]
        buffer[q, d] = (buffer[q, d].astype(jnp.float32) + mine).astype(jnp.bfloat16)
        hop(q, d).start()

    def pass_on(q, hops):
        @pl.when(c == hops)
        def _():
            for d in range(nc - 1, hops, -1):
                add_and_send(q, d, to_right, hop_right)

        @pl.when(c == nc - 1 - hops)
        def _():
            for d in range(nc - 1 - hops):
                add_and_send(q, d, to_left, hop_left)

    def finish(q):
        total[...] = term[q % nc, pl.ds(c * RB_DEV, RB_DEV)]

        @pl.when(c > 0)
        def _():
            hop_right(q, c).wait_recv()
            total[...] += to_right[q, c].astype(jnp.float32)

        @pl.when(c < nc - 1)
        def _():
            hop_left(q, c).wait_recv()
            total[...] += to_left[q, c].astype(jnp.float32)

        for b in range(RB_DEV):
            start = b * chunks * rq + q * rq
            sketch_ref[start:start + rq, :] = total[b]
        rows = total[...].reshape(RB_DEV * rq, width)
        gram[...] += dot_tn(rows, rows)

    for q in range(chunks + nc - 1):
        if q < chunks:
            collect(q)
        if q == chunks:
            finish(q - nc + 1)
        for hops in range(nc - 2, 0, -1):
            if 0 <= q - hops < chunks:
                pass_on(q - hops, hops)
        if q >= nc - 1 and q != chunks:
            finish(q - nc + 1)

    sum_gram(nr, nc, r, c, gram, sketch_ref.at[pl.ds(RB_DEV * order, width)], *refs)
    for k in range(1, nr):
        route(k).wait_send()
    for q in range(chunks):
        for d in range(nc):
            @pl.when(jnp.logical_and(c > 0, c < d))
            def _():
                hop_right(q, d).wait_send()

            @pl.when(jnp.logical_and(c < nc - 1, c > d))
            def _():
                hop_left(q, d).wait_send()

    @pl.when(c == 0)
    def _():
        for send in from_first[-WINDOW:]:
            hop_right(*send[1:]).wait_send()

    @pl.when(c == nc - 1)
    def _():
        for send in from_last[-WINDOW:]:
            hop_left(*send[1:]).wait_send()


def make_sketch(dest, target, col_target, a_blocks, omega, nr, nc):
    targets, _, order, _ = a_blocks.shape
    width = omega.shape[2]
    chunks, rq = CHUNKS, order // CHUNKS
    dma = pltpu.SemaphoreType.DMA
    slots, blocks = nr * CAP, nc * RB_DEV
    hops = pltpu.VMEM((chunks, nc, RB_DEV, rq, width), jnp.bfloat16)
    hbm = pl.BlockSpec(memory_space=pltpu.HBM)
    return pl.pallas_call(
        functools.partial(sketch_kernel, nr, nc),
        out_shape=jax.ShapeDtypeStruct((RB_DEV * order + width, width), jnp.float32),
        in_specs=[hbm] * 5,
        out_specs=VMEM,
        scratch_shapes=[pltpu.VMEM((slots, rq, width), jnp.bfloat16)] * chunks + [
            pltpu.VMEM(dest.shape, jnp.int32),
            pltpu.VMEM(target.shape, jnp.int32),
            pltpu.SMEM(col_target.shape, jnp.int32),
            pltpu.VMEM(a_blocks.shape, a_blocks.dtype),
            pltpu.VMEM(omega.shape, omega.dtype),
            pltpu.VMEM((chunks, targets, rq, width), jnp.bfloat16),
            pltpu.VMEM((chunks, nr, CAP, rq, width), jnp.bfloat16),
            pltpu.VMEM((nr, 8, 128), jnp.int32),
            pltpu.SMEM((8, 128), jnp.int32),
            dma((targets // FIRST,)), dma((4,)),
            pltpu.VMEM((nr, 8, 128), jnp.int32),
            pltpu.VMEM((8, 128), jnp.int32),
            pltpu.SMEM((8, 128), jnp.int32),
            pltpu.VMEM((slots, rq, width), jnp.float32),
            pltpu.VMEM((nc, blocks, rq, width), jnp.float32),
            hops, hops,
            pltpu.VMEM((RB_DEV, rq, width), jnp.float32),
            pltpu.VMEM((width, width), jnp.float32),
            dma((nr,)), dma((nr,)), dma((chunks + 2,)),
            dma((chunks, nr)), dma((chunks, nr)),
            dma((chunks, nc)), dma((chunks, nc)), dma((chunks, nc)), dma((chunks, nc)),
        ] + packed_scratch(nr, nc, width),
        compiler_params=pltpu.CompilerParams(collective_id=1, has_side_effects=True, vmem_limit_bytes=60 << 20),
    )(dest, target, col_target, a_blocks, omega)


def gram_sum_kernel(nr, nc, gram, out_ref, *refs):
    r = lax.axis_index("row")
    c = lax.axis_index("col")
    greet(nr, nc, r, c)
    sum_gram(nr, nc, r, c, gram, out_ref, *refs)


def gram_sum(gram, nr, nc):
    return pl.pallas_call(
        functools.partial(gram_sum_kernel, nr, nc),
        out_shape=jax.ShapeDtypeStruct(gram.shape, jnp.float32),
        in_specs=[VMEM],
        out_specs=VMEM,
        scratch_shapes=packed_scratch(nr, nc, gram.shape[0]),
        compiler_params=pltpu.CompilerParams(collective_id=3, has_side_effects=True, vmem_limit_bytes=8 << 20),
    )(gram)


def eliminate(x):
    rows = x.shape[0]
    shape = (8, x.shape[1])
    groups = [x[i:i + 8, :] for i in range(0, rows, 8)]
    sub = lax.broadcasted_iota(jnp.int32, shape, 0)
    for g in range(rows // 8):
        j = 8 * g
        cols = [[jnp.broadcast_to(groups[i][:, j + l:j + l + 1], shape) for l in range(8)]
                for i in range(g, rows // 8)]
        piv = [[jnp.broadcast_to(cols[0][l][k:k + 1, :], shape) if l >= k else None for l in range(8)] for k in range(8)]
        tops = [jnp.broadcast_to(groups[g][k:k + 1, :], shape) for k in range(8)]
        recip = []
        for k in range(8):
            if k % 2 == 0:
                side = piv[k][k + 1]
                det = piv[k][k] * piv[k + 1][k + 1] - side * side
                recip += [1.0 / piv[k][k], piv[k][k] * (1.0 / det)]
            for m in range(k + 1, 8):
                q = piv[k][m] * recip[k]
                for l in range(m, 8):
                    piv[m][l] = piv[m][l] - q * piv[k][l]
                tops[m] = tops[m] - q * tops[k]
        for i in range(g + 1, rows // 8):
            here = cols[i - g]
            value = groups[i]
            for k in range(8):
                f = here[k] * recip[k]
                for l in range(k + 1, 8):
                    here[l] = here[l] - f * piv[k][l]
                value = value - f * tops[k]
            groups[i] = value
        for k in range(1, 8):
            groups[g] = jnp.where(sub == k, tops[k], groups[g])
    return jnp.concatenate(groups, axis=0)


def factor_gram(gram, left, right, upper, inverse):
    order = gram.shape[0]
    row = lax.broadcasted_iota(jnp.int32, (order, order), 0)
    col = lax.broadcasted_iota(jnp.int32, (order, order), 1)
    only = jnp.where(row == col, gram[...], 0.0)
    diag = jnp.sum(only, axis=0, keepdims=True)
    unit = 1.0 / jnp.sqrt(diag)
    back = diag * unit
    left[...] = gram[...] * (1.0 / jnp.sqrt(jnp.sum(only, axis=1, keepdims=True))) * unit
    right[...] = jnp.where(row == col, unit, 0.0)
    upper[...] = jnp.zeros_like(upper)
    inverse[...] = jnp.zeros_like(inverse)
    lane = lax.broadcasted_iota(jnp.int32, (PANEL, 2 * PANEL), 1)
    prow = lax.broadcasted_iota(jnp.int32, (PANEL, 2 * PANEL), 0)
    for base in range(0, order, PANEL):
        low = base // (2 * PANEL) * 2 * PANEL
        high = low + 2 * PANEL
        here = slice(base, base + PANEL)
        tile = left[here, low:high]
        if base > low:
            tile = pltpu.roll(tile, PANEL, 1)
        x = eliminate(jnp.where(lane < PANEL, tile, (lane - PANEL == prow).astype(jnp.float32)))
        root = 1.0 / jnp.sqrt(jnp.sum(jnp.where(lane == prow, x, 0.0), axis=1, keepdims=True))
        factor = pltpu.roll(x, PANEL, 1)[:, :PANEL]
        u = dot_nn(factor, left[here, low:]) * root
        v = dot_nn(factor, right[here, :high]) * root
        upper[here, low:] = jnp.where(col[here, low:] >= row[here, low:], u * back[:, low:], 0.0)
        inverse[here, :high] = jnp.where(col[here, :high] <= row[here, :high], v, 0.0)
        after = base + PANEL
        if after < order:
            start = after // (2 * PANEL) * 2 * PANEL
            rest = u[:, start - low:]
            left[after:, start:] -= dot_tn(rest, rest)[after - start:]
            right[after:, :high] -= dot_tn(rest, v)[after - start:]


def factor_kernel(scale, sketch, upper_out, factor, inverse, again, left, right):
    order = inverse.shape[0]
    gram = sketch.at[pl.ds(sketch.shape[0] - order, order)]
    factor_gram(gram, left, right, upper_out, inverse)
    factor[...] = upper_out[...] * (1.0 / scale)
    row = lax.broadcasted_iota(jnp.int32, (order, order), 0)
    col = lax.broadcasted_iota(jnp.int32, (order, order), 1)
    diag = jnp.sum(jnp.where(row == col, gram[...], 0.0), axis=0, keepdims=True)
    spread = jnp.sum(inverse[...] * inverse[...], axis=0, keepdims=True) * diag
    mean = jnp.sum(spread) * (1.0 / order)
    again[0] = jnp.where(mean <= INFLATION, 0, 1)


def factor_first(sketch, scale):
    order = sketch.shape[1]
    square = jax.ShapeDtypeStruct((order, order), jnp.float32)
    return pl.pallas_call(
        functools.partial(factor_kernel, scale),
        out_shape=(square, square, square, jax.ShapeDtypeStruct((1,), jnp.int32)),
        in_specs=[VMEM],
        out_specs=(VMEM, VMEM, VMEM, SMEM),
        scratch_shapes=[pltpu.VMEM((order, order), jnp.float32)] * 2,
        compiler_params=pltpu.CompilerParams(vmem_limit_bytes=16 << 20),
    )(sketch)


def apply_kernel(scale, inverse, sketch, basis, ready, sem):
    pieces, step, _ = ready.shape
    matrix = inverse[...] * scale

    def store(i):
        return pltpu.make_async_copy(ready.at[i], basis.at[pl.ds(i * step, step)], sem.at[i])

    for i in range(pieces):
        ready[i] = dot_nt(sketch[i * step:(i + 1) * step, :], matrix)
        store(i).start()
    for i in range(pieces):
        store(i).wait()


def apply_inverse(inverse, sketch, scale):
    rows, width = sketch.shape[0] - sketch.shape[1], sketch.shape[1]
    pieces = 4
    return pl.pallas_call(
        functools.partial(apply_kernel, scale),
        out_shape=jax.ShapeDtypeStruct((rows, width), jnp.float32),
        in_specs=[VMEM, VMEM],
        out_specs=pl.BlockSpec(memory_space=pltpu.HBM),
        scratch_shapes=[pltpu.VMEM((pieces, rows // pieces, width), jnp.float32), pltpu.SemaphoreType.DMA((pieces,))],
        compiler_params=pltpu.CompilerParams(vmem_limit_bytes=16 << 20),
    )(inverse, sketch)


def once_kernel(inverse, sketch, once, second):
    second[...] = jnp.zeros_like(second)
    step = 256

    @pl.loop(0, once.shape[0] // step)
    def _(i):
        part = pl.ds(pl.multiple_of(i * step, step), step)
        rows = dot_nt(sketch[part, :], inverse[...])
        once[part, :] = rows
        second[...] += dot_tn(rows, rows)


def once_pass(inverse, sketch):
    return pl.pallas_call(
        once_kernel,
        out_shape=(
            jax.ShapeDtypeStruct((sketch.shape[0] - sketch.shape[1], sketch.shape[1]), jnp.float32),
            jax.ShapeDtypeStruct(inverse.shape, jnp.float32),
        ),
        in_specs=[VMEM, VMEM],
        out_specs=(VMEM, VMEM),
        compiler_params=pltpu.CompilerParams(vmem_limit_bytes=16 << 20),
    )(inverse, sketch)


def last_kernel(scale, gram, once, upper_one, basis, factor, left, right, upper, inverse):
    factor_gram(gram, left, right, upper, inverse)
    factor[...] = dot_nn(upper[...], upper_one[...]) * (1.0 / scale)
    step = 256

    @pl.loop(0, once.shape[0] // step)
    def _(i):
        part = pl.ds(pl.multiple_of(i * step, step), step)
        basis[part, :] = dot_nt(once[part, :], inverse[...]) * scale


def last_pass(gram, once, upper_one, scale):
    order = gram.shape[0]
    square = pltpu.VMEM((order, order), jnp.float32)
    return pl.pallas_call(
        functools.partial(last_kernel, scale),
        out_shape=(
            jax.ShapeDtypeStruct(once.shape, jnp.float32),
            jax.ShapeDtypeStruct((order, order), jnp.float32),
        ),
        in_specs=[VMEM, VMEM, VMEM],
        out_specs=(VMEM, VMEM),
        scratch_shapes=[square] * 4,
        compiler_params=pltpu.CompilerParams(vmem_limit_bytes=16 << 20),
    )(gram, once, upper_one)


def body(nr, nc, a_blocks, omega, route_dest, row_target, col_target):
    order = a_blocks.shape[2]
    sketch = make_sketch(
        route_dest.T, row_target.reshape(1, -1), col_target.T, a_blocks, omega.reshape(-1, order, omega.shape[1]), nr, nc)
    scale = float(nr * nc * RB_DEV * order) ** 0.5
    upper, factor, inverse, again = factor_first(sketch, scale)

    def orthogonalize_again():
        once, gram_part = once_pass(inverse, sketch)
        return last_pass(gram_sum(gram_part, nr, nc), once, upper, scale)

    def keep_once():
        return apply_inverse(inverse, sketch, scale), factor

    return lax.cond(again[0] != 0, orthogonalize_again, keep_once)


def solution(mesh):
    nr, nc = mesh.shape["row"], mesh.shape["col"]
    return jax.shard_map(
        functools.partial(body, nr, nc),
        mesh=mesh,
        in_specs=(
            P(("row", "col"), None, None, None),
            P("col", None),
            P(("row", "col"), None),
            P(("row", "col")),
            P(("row", "col"), None),
        ),
        out_specs=(P(("row", "col"), None), P()),
        check_vma=False,
    )
```
